32 devices in a mesh: dp: 8 (over y, x, core), fsdp: 4 (over z).
Axes of the slice: x: 2, y: 2, z: 4, core: 2. Of those that a mesh axis runs over, the one named last changes fastest.
Arguments:
- gene_ids: int32 [32, 2048], P(('dp', 'fsdp')), may hold values from 0 to 12799
- expr_bins: int32 [32, 2048], P(('dp', 'fsdp')), may hold values from 0 to 63
- study_ids: int32 [32], P(('dp', 'fsdp')), may hold values from 0 to 63
- lengths: int32 [32], P(('dp', 'fsdp')), may hold values from 256 to 2048, as said below
- prior_embed: bfloat16 [32, 2048, 256], P(('dp', 'fsdp')), may hold values from -3 to 3
- cotangent: bfloat16 [32, 2048, 256], P(('dp', 'fsdp')), may hold values from -6 to 6
- gene_table: bfloat16 [12800, 256], P('fsdp'), may hold values from -3 to 3
- expr_table: bfloat16 [64, 256], P('fsdp'), may hold values from -3 to 3
- study_table: bfloat16 [64, 256], P('fsdp'), may hold values from -3 to 3
- position_table: bfloat16 [2048, 256], P('fsdp'), may hold values from -3 to 3
- norm1_gain: bfloat16 [256], P('fsdp'), may hold values from 0.099609375 to 1.8984375
- norm1_shift: bfloat16 [256], P('fsdp'), may hold values from -1.5 to 1.5
- w_qkv: bfloat16 [256, 768], P('fsdp'), may hold values from -0.375 to 0.375
- bias_query: bfloat16 [256], P('fsdp'), may hold values from -1.5 to 1.5
- bias_value: bfloat16 [256], P('fsdp'), may hold values from -1.5 to 1.5
- w_output: bfloat16 [256, 256], P('fsdp'), may hold values from -6 to 6
- bias_output: bfloat16 [256], P('fsdp'), may hold values from -1.5 to 1.5
- norm2_gain: bfloat16 [256], P('fsdp'), may hold values from 0.099609375 to 1.8984375
- norm2_shift: bfloat16 [256], P('fsdp'), may hold values from -1.5 to 1.5
- w_up_proj: bfloat16 [256, 512], P('fsdp'), may hold values from -0.375 to 0.375
- bias_up: bfloat16 [512], P('fsdp'), may hold values from -1.5 to 1.5
- w_down_proj: bfloat16 [512, 256], P('fsdp'), may hold values from -0.25 to 0.25
- bias_down: bfloat16 [256], P('fsdp'), may hold values from -1.5 to 1.5
Outputs:
- hidden_out: bfloat16 [32, 2048, 256], P(('dp', 'fsdp'))
- grad_gene_table: float32 [12800, 256], P('fsdp')
- update_count: int32 [12800], P('fsdp')
- grad_expr_table: float32 [64, 256], P('fsdp')
- grad_study_table: float32 [64, 256], P('fsdp')
- grad_position_table: float32 [2048, 256], P('fsdp')
- grad_norm1_gain: float32 [256], P('fsdp')
- grad_norm1_shift: float32 [256], P('fsdp')
- grad_w_qkv: float32 [256, 768], P('fsdp')
- grad_bias_query: float32 [256], P('fsdp')
- grad_bias_value: float32 [256], P('fsdp')
- grad_w_output: float32 [256, 256], P('fsdp')
- grad_bias_output: float32 [256], P('fsdp')
- grad_norm2_gain: float32 [256], P('fsdp')
- grad_norm2_shift: float32 [256], P('fsdp')
- grad_w_up_proj: float32 [256, 512], P('fsdp')
- grad_bias_up: float32 [512], P('fsdp')
- grad_w_down_proj: float32 [512, 256], P('fsdp')
- grad_bias_down: float32 [256], P('fsdp')
The draws below stay inside these ranges and needn't reach their ends.
Inputs may be any that keep to these rules, and one draw needn't show every extreme that they name: Slots from lengths[c] on are padding; some cell has 2048 genes and some 2048 // 8.
All inputs are finite; a program needn't handle non-finite values.
Results may differ from the reference program's by a relative error of at most 0.0082.
Values may be sent and summed in bfloat16 or wider, within the bound.
No kernel may reach another device: no remote copies, remote signals or barrier semaphores. Data moves between devices by JAX's collectives and lax.ppermute only.
A program may use at most 128 MiB of HBM per device.

```python
import math
import jax
import jax.numpy as jnp
import numpy as np
from jax import lax

D = 256
HEADS = 4
HEAD = 64
FF = 512
LENGTH = 2048
V = 12800
BINS = 64
GROUPS = 64
CELLS = 32


def draw_lengths(key, part):
    sizes = jax.random.randint(key, (CELLS,), LENGTH // 8, LENGTH + 1).astype(jnp.int32)
    sizes = sizes.at[0].set(LENGTH)
    return sizes.at[CELLS - 1].set(LENGTH // 8)


def place_ends(values, stream_key, least, high):
    shape = values.shape
    place = [jax.random.randint(jax.random.fold_in(stream_key, axis), (), 0, shape[axis]) for axis in range(len(shape))]
    values = values.at[tuple(place)].set(least)
    longest = shape.index(max(shape))
    place[longest] = (place[longest] + 1) % shape[longest]
    return values.at[tuple(place)].set(high)


def shard_levels(own_key, shape, pieces, low, largest):
    level = 1.0
    for dim, parts in pieces:
        heights = jax.random.uniform(jax.random.fold_in(jax.random.fold_in(own_key, 6), dim), (parts,), jnp.float32, low / len(pieces), largest / len(pieces))
        level = level * jnp.repeat(jnp.exp(heights), shape[dim] // parts).reshape((-1,) + (1,) * (len(shape) - 1 - dim))
    return level


def rank_table(count, lean):
    portions = [(1 << 20) // math.isqrt(rank ** lean) + 1 for rank in range(1, count + 1)]
    deviation = 1 + sum(portions) // (1 << 30)
    return np.cumsum(np.array([max(1, weight // deviation) for weight in portions]))


def ranked(own_key, extent, amount, skew):
    table = rank_table(amount, skew)
    pick = jax.random.randint(jax.random.fold_in(own_key, 1), extent, 0, int(table[amount - 1]))
    grade = jnp.searchsorted(jnp.asarray(table, jnp.int32), pick, side="right")
    return jax.random.permutation(jax.random.fold_in(own_key, 2), amount)[grade].astype(jnp.int32)


def bell_draw(stream_key, extent, spread, bound, shards=(), kind=jnp.bfloat16):
    values = jax.random.normal(stream_key, extent, jnp.float32) * spread
    if len(shards) > 0:
        values = shard_levels(stream_key, extent, shards, -0.22, 0.18) * values
    return jnp.clip(values, min=-bound, max=bound).astype(kind)


def setup_inputs(seed: int = 0) -> dict:
    arg_keys = jax.random.split(jax.random.key(seed), 24)
    gene_ids = place_ends(ranked(arg_keys[0], (CELLS, LENGTH), V, 2), jax.random.fold_in(arg_keys[0], 3), 0, V - 1).astype(jnp.int32)
    expr_bins = place_ends(jax.random.randint(arg_keys[1], (CELLS, LENGTH), 0, BINS), jax.random.fold_in(arg_keys[1], 1), 0, BINS - 1).astype(jnp.int32)
    study_ids = place_ends(jax.random.randint(arg_keys[2], (CELLS,), 0, GROUPS), jax.random.fold_in(arg_keys[2], 1), 0, GROUPS - 1).astype(jnp.int32)
    lengths = draw_lengths(jax.random.fold_in(arg_keys[23], 71), 0)
    prior_embed = bell_draw(arg_keys[4], (CELLS, LENGTH, D), 0.5, 3.0, ((0, 32),))
    cotangent = bell_draw(arg_keys[5], (CELLS, LENGTH, D), 1.0, 6.0, ((0, 32),))
    gene_table = bell_draw(arg_keys[6], (V, D), 0.5, 3.0, ((0, 4),))
    expr_table = bell_draw(arg_keys[7], (BINS, D), 0.5, 3.0, ((0, 4),))
    study_table = bell_draw(arg_keys[8], (GROUPS, D), 0.5, 3.0, ((0, 4),))
    position_table = bell_draw(arg_keys[9], (LENGTH, D), 0.5, 3.0, ((0, 4),))
    norm1_gain = jnp.clip(1.0 + 0.18 * jax.random.normal(arg_keys[10], (D,), jnp.float32), 0.099609375, 1.8984375).astype(jnp.bfloat16)
    norm1_shift = bell_draw(arg_keys[11], (D,), 0.3, 1.5, ((0, 4),))
    w_qkv = bell_draw(arg_keys[12], (D, 3 * D), D ** -0.5, 0.375, ((0, 4),))
    bias_query = bell_draw(arg_keys[13], (D,), 0.3, 1.5, ((0, 4),))
    bias_value = bell_draw(arg_keys[14], (D,), 0.3, 1.5, ((0, 4),))
    w_output = bell_draw(arg_keys[15], (D, D), (max(1, 3 * D // LENGTH)) ** -0.5, 6.0, ((0, 4),))
    bias_output = bell_draw(arg_keys[16], (D,), 0.3, 1.5, ((0, 4),))
    norm2_gain = jnp.clip(1.0 + 0.18 * jax.random.normal(arg_keys[17], (D,), jnp.float32), 0.099609375, 1.8984375).astype(jnp.bfloat16)
    norm2_shift = bell_draw(arg_keys[18], (D,), 0.3, 1.5, ((0, 4),))
    w_up_proj = bell_draw(arg_keys[19], (D, FF), D ** -0.5, 0.375, ((0, 4),))
    bias_up = bell_draw(arg_keys[20], (FF,), 0.3, 1.5, ((0, 4),))
    w_down_proj = bell_draw(arg_keys[21], (FF, D), FF ** -0.5, 0.25, ((0, 4),))
    bias_down = bell_draw(arg_keys[22], (D,), 0.3, 1.5, ((0, 4),))
    return {"gene_ids": gene_ids, "expr_bins": expr_bins, "study_ids": study_ids, "lengths": lengths, "prior_embed": prior_embed, "cotangent": cotangent, "gene_table": gene_table, "expr_table": expr_table, "study_table": study_table, "position_table": position_table, "norm1_gain": norm1_gain, "norm1_shift": norm1_shift, "w_qkv": w_qkv, "bias_query": bias_query, "bias_value": bias_value, "w_output": w_output, "bias_output": bias_output, "norm2_gain": norm2_gain, "norm2_shift": norm2_shift, "w_up_proj": w_up_proj, "bias_up": bias_up, "w_down_proj": w_down_proj, "bias_down": bias_down}


@jax.custom_vjp
def low(v):
    return lax.optimization_barrier(v.astype(jnp.bfloat16)).astype(jnp.float32)

@jax.custom_vjp
def low_back(v):
    return v

def low_keep(v):
    return (low(v), None)

def low_pass(kept, grad):
    return (grad,)

def back_keep(v):
    return (v, None)

def back_low(kept, grad):
    return (low(grad),)
low.defvjp(low_keep, low_pass)
low_back.defvjp(back_keep, back_low)
epsilon = 1e-05
highest = lax.Precision.HIGHEST

def layer_norm(values, gain, shift):
    average = lax.optimization_barrier(jnp.mean(values, axis=-1, keepdims=True))
    centered = values - average
    variance = lax.optimization_barrier(jnp.mean(centered * centered, axis=-1, keepdims=True))
    return centered * lax.rsqrt(variance + epsilon) * gain + shift

def forward_layer(layer_parameters, gene_ids, expr_bins, study_ids, mask, prior_knowledge):
    gene_table, expr_table, study_table, position_table, norm1_gain, norm1_shift, w_qkv, bias_query, bias_value, w_output, bias_output, norm2_gain, norm2_shift, w_up_proj, bias_up, w_down_proj, bias_down = layer_parameters
    cells, length = gene_ids.shape
    embedded = gene_table[gene_ids] + expr_table[expr_bins] + study_table[study_ids][:, None, :] + position_table[None] + prior_knowledge
    inputs = embedded * mask[..., None]
    normed_one = low(layer_norm(inputs, norm1_gain, norm1_shift))
    mixed = jnp.einsum('cld,de->cle', normed_one, w_qkv, precision=highest)
    query = low(low_back(mixed[..., :D] + bias_query)).reshape(cells, length, HEADS, HEAD)
    keys = low(low_back(mixed[..., D:2 * D])).reshape(cells, length, HEADS, HEAD)
    values = low(low_back(mixed[..., 2 * D:] + bias_value)).reshape(cells, length, HEADS, HEAD)
    scores = low_back(jnp.einsum('cqhk,cshk->chqs', query, keys, precision=highest) * HEAD ** (-0.5))
    scores = jnp.where(mask[:, None, None, :] > 0, scores, -1000000000.0)
    probs = low(jax.nn.softmax(scores, axis=-1))
    attended = jnp.einsum('chqs,cshk->cqhk', probs, values, precision=highest).reshape(cells, length, D)
    attended = low(low_back(attended))
    branch = low_back(jnp.einsum('cld,de->cle', attended, w_output, precision=highest) + bias_output)
    middle = inputs + branch
    normed_two = low(layer_norm(middle, norm2_gain, norm2_shift))
    upward = low_back(jnp.einsum('cld,df->clf', normed_two, w_up_proj, precision=highest) + bias_up)
    activated = low(jax.nn.gelu(upward, approximate=False))
    result = middle + (jnp.einsum('clf,fd->cld', activated, w_down_proj, precision=highest) + bias_down)
    return result * mask[..., None]

def reference(gene_ids, expr_bins, study_ids, lengths, prior_embed, cotangent, gene_table, expr_table, study_table, position_table, norm1_gain, norm1_shift, w_qkv, bias_query, bias_value, w_output, bias_output, norm2_gain, norm2_shift, w_up_proj, bias_up, w_down_proj, bias_down):
    weights = tuple((item.astype(jnp.float32) for item in (gene_table, expr_table, study_table, position_table, norm1_gain, norm1_shift, w_qkv, bias_query, bias_value, w_output, bias_output, norm2_gain, norm2_shift, w_up_proj, bias_up, w_down_proj, bias_down)))
    positions = jnp.arange(LENGTH, dtype=jnp.int32)
    mask = (positions[None, :] < lengths[:, None]).astype(jnp.float32)
    group = math.gcd(CELLS, max(1, 4096 // LENGTH))
    step_count = CELLS // group

    def shaped(array):
        return array.reshape((step_count, group) + array.shape[1:])

    def one_step(totals, embedding_parts):
        token_ids, expression_levels, study_labels, cell_token_mask, prior_knowledge, upstream_gradient = embedding_parts

        def local(layer_parameters):
            return forward_layer(layer_parameters, token_ids, expression_levels, study_labels, cell_token_mask, prior_knowledge.astype(jnp.float32))
        result, pullback = jax.vjp(local, weights)
        grads = pullback(upstream_gradient.astype(jnp.float32))[0]
        return (tuple((a + b for a, b in zip(totals, grads))), result.astype(jnp.bfloat16))
    starting = tuple((jnp.zeros_like(item) for item in weights))
    totals, results = lax.scan(one_step, starting, (shaped(gene_ids), shaped(expr_bins), shaped(study_ids), shaped(mask), shaped(prior_embed), shaped(cotangent)))
    count = jax.ops.segment_sum(mask.reshape(-1), gene_ids.reshape(-1), num_segments=V).astype(jnp.int32)
    return (results.reshape(CELLS, LENGTH, D), totals[0], count, totals[1], totals[2], totals[3], totals[4], totals[5], totals[6], totals[7], totals[8], totals[9], totals[10], totals[11], totals[12], totals[13], totals[14], totals[15], totals[16])
```

```python
import functools

import jax
import jax.numpy as jnp
from jax import lax
from jax.experimental import pallas as pl
from jax.experimental.pallas import tpu as pltpu
from jax.sharding import Mesh
from jax.sharding import PartitionSpec as P

HEADS = 4
INNER = 8
MISC = 16
epsilon = 1e-05
LOG2E = 1.4426950408889634
bf16 = jnp.bfloat16
f32 = jnp.float32
i32 = jnp.int32


def params():
    return pltpu.CompilerParams(vmem_limit_bytes=56 << 20)


def cost(flops, size, calls=0):
    return pl.CostEstimate(flops=int(flops), bytes_accessed=int(size), transcendentals=int(calls))


def dg(left, right, a, b):
    return lax.dot_general(left, right, (((a,), (b,)), ((), ())), preferred_element_type=f32)


def smem():
    return pl.BlockSpec(memory_space=pltpu.SMEM)


def whole(*shape):
    return pl.BlockSpec(shape, lambda *_: (0,) * len(shape))


def rows(size, width):
    return pl.BlockSpec((size, width), lambda i, *_: (i, 0))


def lanes(size):
    return pl.BlockSpec((1, size), lambda i, *_: (0, i))


def aligned(index, step):
    return pl.multiple_of(index, step)


def onehot(ids, base, count):
    number = lax.broadcasted_iota(i32, (count, ids.shape[1]), 0)
    return jnp.where(number == ids - base, 1.0, 0.0).astype(bf16)


def lookup_kernel(plan, base_ref, ids_ref, *refs):
    tables, out_ref = refs[:-1], refs[-1]
    ids = ids_ref[...]
    total = None
    for table, parts in zip(tables, plan):
        hits = [onehot(ids, base_ref[slot] + off, count) for slot, off, count in parts]
        hits = hits[0] if len(hits) == 1 else jnp.concatenate(hits, axis=0)
        term = dg(hits, table[0 : hits.shape[0], :], 0, 0)
        total = term if total is None else total + term
    out_ref[...] = total.astype(bf16)


def lookup(bases, ids, tables, plan, block=512):
    n, width = ids.shape[1], tables[0].shape[1]
    used = sum(c for parts in plan for _, _, c in parts)
    return pl.pallas_call(
        functools.partial(lookup_kernel, plan),
        grid=(n // block,),
        in_specs=[smem(), lanes(block)] + [whole(*t.shape) for t in tables],
        out_specs=rows(block, width),
        out_shape=jax.ShapeDtypeStruct((n, width), bf16),
        compiler_params=params(),
        cost_estimate=cost(2 * n * width * used, 2 * width * (n + used)),
        name="lookup",
    )(bases, ids, *tables)


def count_kernel(len_ref, ids_ref, out_ref):
    ids = ids_ref[...]
    place = lax.broadcasted_iota(i32, ids.shape, 1)
    high = jnp.where(place < len_ref[0], lax.shift_right_logical(ids, 7), -1)
    left = onehot(high, 0, out_ref.shape[0])
    right = onehot(lax.bitwise_and(ids, 127), 0, 128)
    out_ref[...] = dg(left, right, 1, 1).astype(i32)


def count_rows(length, ids, vocab):
    return pl.pallas_call(
        count_kernel,
        in_specs=[smem(), pl.BlockSpec(memory_space=pltpu.VMEM)],
        out_shape=jax.ShapeDtypeStruct((vocab // 128, 128), i32),
        compiler_params=params(),
        name="count_rows",
    )(length, ids)


def assemble_kernel(gene_total, sizes, coord_ref, pos_loc, m_loc, down_loc, misc_loc, *refs):
    F, pos_n, cat_n, down_n = sizes
    pieces = refs[:INNER]
    pos, cat, down, expr, study, vec, up_vec, misc = refs[INNER:]
    z, p = coord_ref[0], coord_ref[1]
    width = pos.shape[1]
    half = m_loc.shape[1] // 2
    parts = half // width
    rows_z = cat_n * (INNER // 2)
    rest_n = pos_n + cat_n * parts + down_n + MISC
    pos[pl.ds(aligned(z * pos_n * INNER, 16), pos_n * INNER), :] = pos_loc[...]
    down[pl.ds(aligned(z * down_n * INNER, 16), down_n * INNER), :] = down_loc[...]
    cat[0, pl.ds(aligned(z * rows_z, 16), rows_z), :] = m_loc[:, 0:half]
    cat[1, pl.ds(aligned(z * rows_z, 16), rows_z), :] = m_loc[:, half:]
    for t in range(3):
        misc[z * INNER + t] = misc_loc[t]
    for k in range(1, F):
        zk = lax.rem(z + F - k, F)
        for j in range(INNER):
            pj = lax.bitwise_xor(p, j)
            ref = pieces[j]
            at = ref.shape[0] - rest_n * (F - k)
            pos[pl.ds(aligned((zk * INNER + pj) * pos_n, 16), pos_n), :] = ref[at : at + pos_n, :]
            at += pos_n
            row = aligned(zk * rows_z + lax.shift_right_logical(pj, 1) * cat_n, 16)
            side = lax.bitwise_and(pj, 1)
            for s in range(parts):
                cat[side, pl.ds(row, cat_n), s * width : (s + 1) * width] = ref[at : at + cat_n, :]
                at += cat_n
            down[pl.ds(aligned((zk * INNER + pj) * down_n, 16), down_n), :] = ref[at : at + down_n, :]
            at += down_n
            misc[zk * INNER + pj] = ref[at : at + MISC, :]
    sub = width // F
    for zz in range(F):
        expr[MISC * zz : MISC * zz + MISC, :] = misc[zz * INNER]
        study[MISC * zz : MISC * zz + MISC, :] = misc[zz * INNER + 1]
    small = [misc[zz * INNER + 2].astype(f32) for zz in range(F)]
    for i in range(8):
        r, c = i // F, sub * (i % F)
        vec[i : i + 1, :] = jnp.concatenate([s[r : r + 1, c : c + sub] for s in small], axis=1)
    r = 8 // F
    up_vec[...] = jnp.concatenate(
        [s[r : r + 1, 0 : up_vec.shape[1] // F] for s in small], axis=1
    )


def assemble(coord, pos_loc, m_loc, down_loc, misc_loc, pieces, gene_total, F):
    width = pos_loc.shape[1]
    half = m_loc.shape[1] // 2
    up_width = half - width
    sizes = (F, pos_loc.shape[0] // INNER, m_loc.shape[0] // (INNER // 2), down_loc.shape[0] // INNER)
    vmem = pl.BlockSpec(memory_space=pltpu.VMEM)
    return pl.pallas_call(
        functools.partial(assemble_kernel, gene_total, sizes),
        in_specs=[smem()] + [vmem] * (4 + INNER),
        out_shape=[
            jax.ShapeDtypeStruct((F * pos_loc.shape[0], width), bf16),
            jax.ShapeDtypeStruct((2, F * m_loc.shape[0], half), bf16),
            jax.ShapeDtypeStruct((F * down_loc.shape[0], width), bf16),
            jax.ShapeDtypeStruct((F * MISC, width), bf16),
            jax.ShapeDtypeStruct((F * MISC, width), bf16),
            jax.ShapeDtypeStruct((8, width), f32),
            jax.ShapeDtypeStruct((1, up_width), f32),
        ],
        scratch_shapes=[pltpu.VMEM((F * INNER, MISC, width), bf16)],
        compiler_params=params(),
        name="assemble",
    )(coord, pos_loc, m_loc, down_loc, misc_loc, *pieces)


def standard(values):
    average = jnp.mean(values, axis=1, keepdims=True)
    centered = values - average
    scale = lax.rsqrt(jnp.mean(centered * centered, axis=1, keepdims=True) + epsilon)
    return centered * scale, scale


def slot_mask(len_ref, size):
    slot = pl.program_id(0) * size + lax.broadcasted_iota(i32, (size, 1), 0)
    return (slot < len_ref[0]).astype(f32)


def embed_kernel(count, size, scalar_ref, bins_ref, *refs):
    found = refs[:count]
    prior, pos, expr, study, vec, cat, inputs_ref, q_ref, k_ref, v_ref = refs[count:]
    width = prior.shape[1]
    total = dg(onehot(bins_ref[...], 0, expr.shape[0]), expr[...], 0, 0)
    for ref in found:
        total = total + ref[...].astype(f32)
    here = (lax.broadcasted_iota(i32, (8, study.shape[0]), 1) == scalar_ref[1]).astype(bf16)
    total = total + dg(here, study[...], 1, 0)[0:1, :]
    total = total + pos[...].astype(f32) + prior[...].astype(f32)
    total = total * slot_mask(scalar_ref, size)
    inputs_ref[...] = total
    normed, _ = standard(total)
    normed = (normed * vec[0:1, :] + vec[1:2, :]).astype(bf16)
    mixed = dg(normed, cat[0], 1, 0)
    q_ref[...] = (mixed[:, 0:width] + vec[2:3, :]).astype(bf16)
    k_ref[...] = mixed[:, width : 2 * width].astype(bf16)
    v_ref[...] = (mixed[:, 2 * width :] + vec[3:4, :]).astype(bf16)


def embed(scalars, bins, found, prior, pos, expr, study, vec, cat, size=512):
    n, width = prior.shape
    block = rows(size, width)
    return pl.pallas_call(
        functools.partial(embed_kernel, len(found), size),
        grid=(n // size,),
        in_specs=[smem(), lanes(size)]
        + [block] * (len(found) + 2)
        + [whole(*a.shape) for a in (expr, study, vec, cat)],
        out_specs=[block] * 4,
        out_shape=[jax.ShapeDtypeStruct((n, width), f32)]
        + [jax.ShapeDtypeStruct((n, width), bf16)] * 3,
        compiler_params=params(),
        cost_estimate=cost(2 * n * width * 3 * width, n * width * 24),
        name="embed",
    )(scalars, bins, *found, prior, pos, expr, study, vec, cat)


def extend(pair, half, spare):
    size = pair.shape[1] // 2
    lane = lax.broadcasted_iota(i32, pair.shape, 1)
    base = size * (1 - half)
    out = jnp.where((lane >= size * half) & (lane < size * half + size), pair, jnp.zeros_like(pair))
    for t, value in enumerate(spare):
        out = jnp.where(lane == base + t, jnp.broadcast_to(value, pair.shape), out)
    return out


def one():
    return jnp.ones((1, 1), bf16)


def split3(value):
    high = value.astype(bf16)
    rest = value - high.astype(f32)
    middle = rest.astype(bf16)
    return high, middle, (rest - middle.astype(f32)).astype(bf16)


def key_bias(len_ref, n):
    slot = lax.broadcasted_iota(i32, (n, 1), 0)
    return jnp.where(slot < len_ref[0], 0.0, -1e9).astype(bf16)


def pair_lanes(h, pair):
    return slice(pair * (h // 2), pair * (h // 2) + pair)


def attend_kernel(len_ref, q_ref, k_ref, v_ref, o_ref, wide_ref, lse_ref, kx, vt):
    n, width = k_ref.shape
    size = width // HEADS
    factor = size ** (-0.5) * LOG2E

    @pl.when(pl.program_id(0) == 0)
    def _():
        bias = key_bias(len_ref, n)
        for h in range(HEADS):
            kx[h] = extend(k_ref[:, pair_lanes(h, 2 * size)], h % 2, [bias])
        vt[...] = v_ref[...].T

    outs = []
    for h in range(HEADS):
        qx = extend(q_ref[:, pair_lanes(h, 2 * size)], h % 2, [one()])
        scores = dg(kx[h], qx, 1, 1)
        peak = jnp.max(scores, axis=0, keepdims=True)
        raised = jnp.exp2((scores - peak) * factor)
        total = jnp.sum(raised, axis=0, keepdims=True)
        out = dg(vt[size * h : size * h + size, :], raised.astype(bf16), 1, 0)
        outs.append(out * (1.0 / total))
        lse_ref[h : h + 1, :] = peak + jnp.log2(total) * (1.0 / factor)
    out = jnp.concatenate(outs, axis=0).T
    wide_ref[...] = out
    o_ref[...] = out.astype(bf16)


def attend(length, q, k, v, size=512):
    n, width = q.shape
    return pl.pallas_call(
        attend_kernel,
        grid=(n // size,),
        in_specs=[smem(), rows(size, width), whole(n, width), whole(n, width)],
        out_specs=[rows(size, width)] * 2 + [pl.BlockSpec((8, size), lambda i: (0, i))],
        out_shape=[
            jax.ShapeDtypeStruct((n, width), bf16),
            jax.ShapeDtypeStruct((n, width), f32),
            jax.ShapeDtypeStruct((8, n), f32),
        ],
        scratch_shapes=[
            pltpu.VMEM((HEADS, n, 2 * width // HEADS), bf16),
            pltpu.VMEM((width, n), bf16),
        ],
        compiler_params=params(),
        cost_estimate=cost(4 * n * n * width, 8 * n * width, n * n * HEADS),
        name="attend",
    )(length, q, k, v)


def attend_back_kernel(
    len_ref, q_ref, k_ref, v_ref, o_ref, do_ref, lse_ref, dq_ref, dk_ref, dv_ref, kx, vx, dkt, dvt
):
    n, width = k_ref.shape
    size = width // HEADS
    scale = size ** (-0.5)
    factor = scale * LOG2E

    @pl.when(pl.program_id(0) == 0)
    def _():
        bias = key_bias(len_ref, n)
        for h in range(HEADS):
            kx[h] = extend(k_ref[:, pair_lanes(h, 2 * size)], h % 2, [bias, one(), one(), one()])
            vx[h] = extend(v_ref[:, pair_lanes(h, 2 * size)], h % 2, [one(), one(), one()])
        dkt[...] = jnp.zeros_like(dkt)
        dvt[...] = jnp.zeros_like(dvt)

    lse = lse_ref[...].T
    qt = q_ref[...].T
    dot = do_ref[...].T
    grads = []
    for h in range(HEADS):
        lane = pair_lanes(h, 2 * size)
        half = h % 2
        product = do_ref[:, lane].astype(f32) * o_ref[:, lane]
        inner = jnp.sum(product[:, size * half : size * half + size], axis=1, keepdims=True)
        qx = extend(q_ref[:, lane], half, [one(), *split3(-lse[:, h : h + 1])])
        dox = extend(do_ref[:, lane], half, [*split3(-inner)])
        probs = jnp.exp2(dg(qx, kx[h], 1, 1) * factor)
        grad_scores = (probs * dg(dox, vx[h], 1, 1)).astype(bf16)
        span = slice(size * h, size * h + size)
        dvt[span, :] += dg(dot[span, :], probs.astype(bf16), 1, 0)
        dkt[span, :] += dg(qt[span, :], grad_scores, 1, 0)
        grads.append(dg(grad_scores, kx[h], 1, 0))
    low = lax.broadcasted_iota(i32, grads[0].shape, 1) < size
    for t in range(HEADS // 2):
        both = jnp.where(low, grads[2 * t], grads[2 * t + 1])
        dq_ref[:, 2 * size * t : 2 * size * (t + 1)] = (both * scale).astype(bf16)

    @pl.when(pl.program_id(0) == pl.num_programs(0) - 1)
    def _():
        dk_ref[...] = (dkt[...] * scale).T.astype(bf16)
        dv_ref[...] = dvt[...].T.astype(bf16)


def attend_back(length, q, k, v, o, do, lse, size=512):
    n, width = q.shape
    block, full = rows(size, width), whole(n, width)
    return pl.pallas_call(
        attend_back_kernel,
        grid=(n // size,),
        in_specs=[smem(), block, full, full, block, block, pl.BlockSpec((8, size), lambda i: (0, i))],
        out_specs=[block, full, full],
        out_shape=[jax.ShapeDtypeStruct((n, width), bf16)] * 3,
        scratch_shapes=[pltpu.VMEM((HEADS, n, 2 * width // HEADS), bf16)] * 2
        + [pltpu.VMEM((width, n), f32)] * 2,
        compiler_params=params(),
        cost_estimate=cost(10 * n * n * width, 16 * n * width, n * n * HEADS),
        name="attend_back",
    )(length, q, k, v, o, do, lse)


def add_to(ref, value):
    @pl.when(pl.program_id(0) == 0)
    def _():
        ref[...] = value

    @pl.when(pl.program_id(0) != 0)
    def _():
        ref[...] += value


def feed_kernel(
    size, len_ref, att_ref, in_ref, cot_ref, cat, down, vec, up_vec,
    hidden_ref, mid_ref, datt_ref, g_down, g_up, g_out, g_vec, g_up_vec,
):
    width = att_ref.shape[1]
    up_width = down.shape[0]
    w_up, w_out = cat[1, :, 0:up_width], cat[1, :, up_width:]
    mask = slot_mask(len_ref, size)
    att = att_ref[...]
    middle = in_ref[...] + dg(att, w_out, 1, 0) + vec[4:5, :]
    normed, scale = standard(middle)
    low = (normed * vec[5:6, :] + vec[6:7, :]).astype(bf16)
    upward = dg(low, w_up, 1, 0) + up_vec[...]
    share = 0.5 * (1.0 + lax.erf(upward * (0.5**0.5)))
    active = (upward * share).astype(bf16)
    result = middle + dg(active, down[...], 1, 0) + vec[7:8, :]
    hidden_ref[...] = (result * mask).astype(bf16)
    grad_low = (cot_ref[...].astype(f32) * mask).astype(bf16)
    grad = grad_low.astype(f32)
    bell = jnp.exp(upward * upward * -0.5) * 0.3989422804014327
    grad_up = ((share + upward * bell) * dg(grad_low, down[...], 1, 1)).astype(bf16)
    grad_norm = dg(grad_up, w_up, 1, 1)
    scaled = grad_norm * vec[5:6, :]
    back = scaled - jnp.mean(scaled, axis=1, keepdims=True)
    back = back - normed * jnp.mean(scaled * normed, axis=1, keepdims=True)
    grad_mid = grad + scale * back
    branch = grad_mid.astype(bf16)
    mid_ref[...] = grad_mid
    datt_ref[...] = dg(branch, w_out, 1, 1).astype(bf16)
    add_to(g_down, dg(active, grad_low, 0, 0))
    add_to(g_up, dg(low, grad_up, 0, 0))
    add_to(g_out, dg(att, branch, 0, 0))
    sums = [
        jnp.sum(t, axis=0, keepdims=True)
        for t in (branch.astype(f32), grad_norm * normed, grad_norm, grad)
    ]
    add_to(g_vec, jnp.concatenate(sums + sums, axis=0))
    add_to(g_up_vec, jnp.sum(grad_up.astype(f32), axis=0, keepdims=True))


def feed(length, att, inputs, cot, cat, down, vec, up_vec, size=256):
    n, width = att.shape
    up_width = down.shape[0]
    block = rows(size, width)
    shapes = [(up_width, width), (width, up_width), (width, width), (8, width), (1, up_width)]
    return pl.pallas_call(
        functools.partial(feed_kernel, size),
        grid=(n // size,),
        in_specs=[smem(), block, block, block]
        + [whole(*a.shape) for a in (cat, down, vec, up_vec)],
        out_specs=[block] * 3 + [whole(*s) for s in shapes],
        out_shape=[
            jax.ShapeDtypeStruct((n, width), bf16),
            jax.ShapeDtypeStruct((n, width), f32),
            jax.ShapeDtypeStruct((n, width), bf16),
        ]
        + [jax.ShapeDtypeStruct(s, f32) for s in shapes],
        compiler_params=params(),
        cost_estimate=cost(30 * n * width * width, 20 * n * width),
        name="feed",
    )(length, att, inputs, cot, cat, down, vec, up_vec)


def inputs_back_kernel(
    size, F, scalar_ref, bins_ref, dq_ref, dk_ref, dv_ref, in_ref, mid_ref, cat, vec,
    g_down, g_up, g_out, g_vec2, g_up_vec, out_ref, wg_ref, g_qkv, g_vec, g_expr,
):
    width = dq_ref.shape[1]
    mask = slot_mask(scalar_ref, size)
    normed, scale = standard(in_ref[...])
    low = (normed * vec[0:1, :] + vec[1:2, :]).astype(bf16)
    parts = [dq_ref[...], dk_ref[...], dv_ref[...]]
    grad_norm = None
    for t, part in enumerate(parts):
        lane = slice(t * width, (t + 1) * width)
        term = dg(part, cat[0, :, lane], 1, 1)
        grad_norm = term if grad_norm is None else grad_norm + term
        add_to(g_qkv.at[:, lane], dg(low, part, 0, 0))
    scaled = grad_norm * vec[0:1, :]
    back = scaled - jnp.mean(scaled, axis=1, keepdims=True)
    back = back - normed * jnp.mean(scaled * normed, axis=1, keepdims=True)
    grad = (mid_ref[...] + scale * back) * mask
    grad_low = grad.astype(bf16)
    out_ref[...] = grad_low
    sums = [
        jnp.sum(t, axis=0, keepdims=True)
        for t in (grad_norm * normed, grad_norm, parts[0].astype(f32), parts[2].astype(f32), grad)
    ]
    add_to(g_vec, jnp.concatenate(sums + sums[0:3], axis=0))
    add_to(g_expr, dg(onehot(bins_ref[...], 0, g_expr.shape[0]), grad_low, 1, 0))

    @pl.when(pl.program_id(0) == pl.num_programs(0) - 1)
    def _():
        cat_n = width // F // (INNER // 2)
        down_n = g_down.shape[0] // F // INNER
        sub = width // F
        up_sub = g_up_vec.shape[1] // F
        half = g_qkv.shape[1]
        groups = g_expr.shape[0]
        here = lax.broadcasted_iota(i32, (groups, width), 0) == scalar_ref[1]
        g_study = jnp.where(here, jnp.broadcast_to(g_vec[4:5, :], (groups, width)), 0.0)
        vectors = [g_vec[i : i + 1, :] for i in range(4)] + [g_vec2[i : i + 1, :] for i in range(4)]
        for z in range(F):
            small = []
            for r in range(8 // F):
                small.append(
                    jnp.concatenate(
                        [vectors[r * F + i][:, z * sub : (z + 1) * sub] for i in range(F)], axis=1
                    )
                )
            up_row = g_up_vec[:, z * up_sub : (z + 1) * up_sub]
            small.append(jnp.concatenate([up_row, jnp.zeros((1, width - up_sub), f32)], axis=1))
            small.append(jnp.zeros((MISC - len(small), width), f32))
            misc = [
                g_expr[MISC * z : MISC * z + MISC, :],
                g_study[MISC * z : MISC * z + MISC, :],
                jnp.concatenate(small, axis=0),
            ]
            for p in range(INNER):
                c, q = p % 2, p // 2
                span = slice(sub * z + cat_n * q, sub * z + cat_n * (q + 1))
                if c == 0:
                    blocks = [g_qkv[span, t * width : (t + 1) * width] for t in range(3)]
                else:
                    blocks = [
                        g_up[span, t * width : (t + 1) * width]
                        for t in range(half // width - 1)
                    ] + [g_out[span, :]]
                at = down_n * (INNER * z + p)
                blocks.append(g_down[at : at + down_n, :])
                blocks.append(misc[p] if p < 3 else jnp.zeros((MISC, width), f32))
                at = 0
                for b in blocks:
                    wg_ref[c, z, q, at : at + b.shape[0], :] = b.astype(bf16)
                    at += b.shape[0]


def inputs_back(scalars, bins, dq, dk, dv, inputs, mid, cat, vec, grads, bins_total, F, size=256):
    n, width = dq.shape
    block = rows(size, width)
    half = cat.shape[2]
    w_rows = half * (width // F // (INNER // 2)) // width + grads[0].shape[0] // F // INNER + MISC
    shape = (2, F, INNER // 2, w_rows, width)
    return pl.pallas_call(
        functools.partial(inputs_back_kernel, size, F),
        grid=(n // size,),
        in_specs=[smem(), lanes(size)] + [block] * 5 + [whole(*a.shape) for a in (cat, vec, *grads)],
        out_specs=[block, whole(*shape)],
        out_shape=[jax.ShapeDtypeStruct((n, width), bf16), jax.ShapeDtypeStruct(shape, bf16)],
        scratch_shapes=[
            pltpu.VMEM((width, half), f32),
            pltpu.VMEM((8, width), f32),
            pltpu.VMEM((bins_total, width), f32),
        ],
        compiler_params=params(),
        cost_estimate=cost(12 * n * width * width, 24 * n * width),
        name="inputs_back",
    )(scalars, bins, dq, dk, dv, inputs, mid, cat, vec, *grads)


def scatter_kernel(gene_n, pos_n, steps, block_ref, ids0, ids1, g0, g1, w0, w1, out_ref):
    i = pl.program_id(0)
    place = block_ref[i]
    base = place * gene_n
    total = dg(onehot(ids0[...], base, gene_n), g0[...], 1, 0)
    total = total + dg(onehot(ids1[...], base, gene_n), g1[...], 1, 0)
    out_ref[0, 0:gene_n, :] = total.astype(bf16)
    span = pl.ds(aligned(place * pos_n, 16), pos_n)
    out_ref[0, gene_n : gene_n + pos_n, :] = (g0[span, :].astype(f32) + g1[span, :].astype(f32)).astype(bf16)
    out_ref[0, gene_n + pos_n :, :] = (w0[0].astype(f32) + w1[0].astype(f32)).astype(bf16)


def scatter(blocks, ids, g, w, gene_n, pos_n):
    n, width = g[0].shape
    steps = blocks.shape[0]
    w_rows = w[0].shape[1]
    piece = gene_n + pos_n + w_rows
    mine = pl.BlockSpec((1, w_rows, width), lambda i, b: (lax.shift_right_logical(b[i], 1), 0, 0))
    return pl.pallas_call(
        functools.partial(scatter_kernel, gene_n, pos_n, steps),
        grid_spec=pltpu.PrefetchScalarGridSpec(
            num_scalar_prefetch=1,
            grid=(steps,),
            in_specs=[whole(1, n)] * 2 + [whole(n, width)] * 2 + [mine] * 2,
            out_specs=pl.BlockSpec((1, piece, width), lambda i, b: (i, 0, 0)),
        ),
        out_shape=jax.ShapeDtypeStruct((steps, piece, width), bf16),
        compiler_params=params(),
        cost_estimate=cost(4 * steps * gene_n * n * width, 4 * n * width + 2 * steps * piece * width),
        name="scatter",
    )(blocks, *ids, *g, *w)


def unpack_kernel(F, gene_n, pos_n, cat_n, down_n, coord_ref, *refs):
    pieces = refs[: INNER + 2]
    gene, pos, cat, down, misc = refs[INNER + 2 :]
    p = coord_ref[1]
    width = gene.shape[1]
    parts = cat.shape[2] // width
    for j in range(INNER):
        pj = lax.bitwise_xor(p, j)
        if j < 6:
            here = [(pieces[j], 0)]
        else:
            top, bottom = pieces[6 + 2 * (j - 6)], pieces[7 + 2 * (j - 6)]
            here = [(top, 0), (bottom, top.shape[0])]
        for ref, first in here:
            count = min(ref.shape[0], gene_n - first)
            gene[pl.ds(aligned(gene_n * pj + first, 16), count), :] = ref[0:count, :].astype(f32)
        ref, first = here[-1]
        at = gene_n - first
        pos[pl.ds(aligned(pos_n * pj, 16), pos_n), :] = ref[at : at + pos_n, :].astype(f32)
        at += pos_n
        row = pl.ds(aligned(lax.shift_right_logical(pj, 1) * cat_n, 16), cat_n)
        for s in range(parts):
            cat[lax.bitwise_and(pj, 1), row, s * width : (s + 1) * width] = ref[
                at : at + cat_n, :
            ].astype(f32)
            at += cat_n
        down[pl.ds(aligned(pj * down_n, 16), down_n), :] = ref[at : at + down_n, :].astype(f32)
        at += down_n
        misc[pj] = ref[at : at + MISC, :].astype(f32)


def unpack(coord, pieces, F, gene_n, pos_n, cat_n, down_n, half):
    width = pieces[0].shape[1]
    vmem = pl.BlockSpec(memory_space=pltpu.VMEM)
    return pl.pallas_call(
        functools.partial(unpack_kernel, F, gene_n, pos_n, cat_n, down_n),
        in_specs=[smem()] + [vmem] * len(pieces),
        out_shape=[
            jax.ShapeDtypeStruct((gene_n * INNER, width), f32),
            jax.ShapeDtypeStruct((pos_n * INNER, width), f32),
            jax.ShapeDtypeStruct((2, cat_n * INNER // 2, half), f32),
            jax.ShapeDtypeStruct((down_n * INNER, width), f32),
            jax.ShapeDtypeStruct((INNER, MISC, width), f32),
        ],
        compiler_params=params(),
        name="unpack",
    )(coord, *pieces)


def swap(array, bit):
    return lax.ppermute(array, "inner", [(i, i ^ bit) for i in range(INNER)])


def along(array, step, F):
    return lax.ppermute(array, "fsdp", [(i, (i + step) % F) for i in range(F)])


def spread(piece):
    cut = piece.shape[0] // 32 * 16
    near = swap(piece, 2)
    other = swap(piece, 4)
    core = swap(piece, 1)
    upper = swap(near[:cut], 4)
    lower = swap(other[cut:], 2)
    return [
        piece, core, near, swap(near, 1), other, swap(other, 1),
        upper, lower, swap(upper, 1), swap(lower, 1),
    ]


def plus(left, right):
    return (left.astype(f32) + right.astype(f32)).astype(bf16)


def body(
    outer, F,
    gene_ids, expr_bins, study_ids, lengths, prior_embed, cotangent,
    gene_table, expr_table, study_table, position_table,
    norm1_gain, norm1_shift, w_qkv, bias_query, bias_value, w_output, bias_output,
    norm2_gain, norm2_shift, w_up_proj, bias_up, w_down_proj, bias_down,
):
    n = gene_ids.shape[1]
    width = gene_table.shape[1]
    z, p = lax.axis_index("fsdp"), lax.axis_index("inner")
    gene_n = gene_table.shape[0] // INNER
    pos_n = position_table.shape[0] // INNER
    down_n = w_down_proj.shape[0] // INNER
    cat_n = w_qkv.shape[0] // (INNER // 2)
    coord = jnp.stack([z, p]).astype(i32)
    prior, cot = prior_embed[0], cotangent[0]
    scalars = jnp.concatenate([lengths, study_ids])

    merged = jnp.concatenate([w_qkv, w_up_proj, w_output], axis=1)
    half = merged.shape[1] // 2
    small = jnp.concatenate(
        [norm1_gain, norm1_shift, bias_query, bias_value,
         bias_output, norm2_gain, norm2_shift, bias_down, bias_up]
    )
    small = jnp.pad(small, (0, MISC * width - small.shape[0])).reshape(MISC, width)
    misc3 = jnp.stack([expr_table, study_table, small])
    mine = lax.dynamic_slice(
        merged, (lax.shift_right_logical(p, 1) * cat_n, lax.bitwise_and(p, 1) * half), (cat_n, half)
    )
    misc8 = jnp.concatenate([misc3, jnp.zeros((INNER - 3, MISC, width), bf16)])
    piece = jnp.concatenate(
        [
            lax.dynamic_slice_in_dim(gene_table, p * gene_n, gene_n),
            lax.dynamic_slice_in_dim(position_table, p * pos_n, pos_n),
            *[mine[:, t * width : (t + 1) * width] for t in range(half // width)],
            lax.dynamic_slice_in_dim(w_down_proj, p * down_n, down_n),
            lax.dynamic_index_in_dim(misc8, p, keepdims=False),
        ]
    )
    got = [along(piece, k, F) for k in range(1, F)]
    stack = jnp.concatenate([g[:gene_n] for g in got] + [g[gene_n:] for g in got])
    pieces = spread(stack)
    gene_total = (F - 1) * gene_n

    places = [
        lax.rem(z + F - k, F) * INNER + lax.bitwise_xor(p, j) for j in range(INNER) for k in range(1, F)
    ]
    bases = jnp.stack(places + [z * INNER]).astype(i32) * gene_n

    def plan(j, first, count):
        parts = []
        for k in range(F - 1):
            low, high = max(first, k * gene_n), min(first + count, (k + 1) * gene_n)
            if low < high:
                parts.append((j * (F - 1) + k, low - k * gene_n, high - low))
        return tuple(parts)

    def full(j):
        return plan(j, 0, gene_total)

    cut = pieces[6].shape[0]
    top, bottom = (0, cut), (cut, gene_total - cut)
    found = [
        lookup(bases, gene_ids, [gene_table], (((INNER * (F - 1), 0, gene_table.shape[0]),),)),
        lookup(bases, gene_ids, pieces[0:2], (full(0), full(1))),
        lookup(bases, gene_ids, [pieces[2], pieces[4]], (full(2), full(4))),
        lookup(
            bases,
            gene_ids,
            [pieces[3], pieces[5], *pieces[6:]],
            (full(3), full(5), plan(6, *top), plan(6, *bottom), plan(7, *top), plan(7, *bottom)),
        ),
    ]
    pos, cat, down, expr, study, vec, up_vec = assemble(
        coord, position_table, merged, w_down_proj, misc3,
        [*pieces[0:6], pieces[7], pieces[9]], gene_total, F,
    )

    counts = count_rows(lengths, gene_ids, gene_table.shape[0] * F)
    for bit in (1, 2, 4):
        counts = counts + swap(counts, bit)
    counts = counts.reshape(F, -1)
    own = lax.dynamic_index_in_dim(counts, z, keepdims=False)
    for k in range(1, F):
        own = own + along(lax.dynamic_index_in_dim(counts, lax.rem(z + k, F), keepdims=False), k, F)

    inputs, query, keys, values = embed(
        scalars, expr_bins, found, prior, pos, expr, study, vec, cat
    )
    attended, wide, lse = attend(lengths, query, keys, values)
    hidden, mid, grad_attended, *grads = feed(
        lengths, attended, inputs, cot, cat, down, vec, up_vec
    )
    dq, dk, dv = attend_back(lengths, query, keys, values, wide, grad_attended, lse)
    grad, wg = inputs_back(
        scalars, expr_bins, dq, dk, dv, inputs, mid, cat, vec, grads, expr.shape[0], F
    )

    core = lax.bitwise_and(p, 1)
    wg = wg.reshape(2, F * INNER // 2, -1, width)
    wg_mine = lax.dynamic_index_in_dim(wg, core, keepdims=False)
    wg_other = swap(lax.dynamic_index_in_dim(wg, 1 - core, keepdims=False), 1)
    ids = [gene_ids, swap(gene_ids, 1)]
    g = [grad, swap(grad, 1)]
    zk = [lax.rem(z + k, F) * INNER for k in range(F)]
    first, second = range(F // 2), range(F // 2, F)

    def at(ks, bits):
        return [zk[k] + lax.bitwise_xor(p, b) for b in bits for k in ks]

    send = jnp.stack(at(first, (6, 2)) + at(second, (6, 4))).astype(i32)
    keep = jnp.stack(at(first, (4, 0)) + at(second, (2, 0))).astype(i32)
    sent = scatter(send, ids, g, [wg_mine, wg_other], gene_n, pos_n)
    kept = scatter(keep, ids, g, [wg_mine, wg_other], gene_n, pos_n)
    a, b = F, F // 2
    left = plus(kept[:a], swap(sent[:a], 2))
    right = plus(kept[a:], swap(sent[a:], 4))
    left = plus(left[b:], swap(left[:b], 4))
    right = plus(right[b:], swap(right[:b], 2))
    blocks = jnp.concatenate([left, right])
    total = blocks[0].astype(f32)
    for k in range(1, F):
        total = total + along(blocks[k], k, F).astype(f32)
    if outer > 1:
        total = lax.psum(total, "outer")
        own = lax.psum(own, "outer")
    done = spread(total.astype(bf16))
    gene, pos, cat, down, misc = unpack(
        coord, done, F, gene_n, pos_n, cat_n, down_n, half
    )
    sub = width // F
    vectors = misc[2]

    def vector(i):
        return vectors[i // F, sub * (i % F) : sub * (i % F + 1)]

    up_width = half - width
    return (
        hidden[None],
        gene,
        own.reshape(-1),
        misc[0],
        misc[1],
        pos,
        vector(0),
        vector(1),
        cat[0],
        vector(2),
        vector(3),
        cat[1][:, up_width:],
        vector(4),
        vector(5),
        vector(6),
        cat[1][:, :up_width],
        vectors[8 // F, : up_width // F],
        down,
        vector(7),
    )


def solution(mesh):
    dp, F = mesh.devices.shape
    outer = dp // INNER
    mesh = Mesh(mesh.devices.reshape(outer, INNER, F), ("outer", "inner", "fsdp"))
    cells = ("outer", "inner", "fsdp")
    row, line = P("fsdp", None), P("fsdp")
    tables = (row,) * 4 + (line,) * 2 + (row, line, line, row, line, line, line, row, line, row, line)
    return jax.shard_map(
        functools.partial(body, outer, F),
        mesh=mesh,
        in_specs=(P(cells, None), P(cells, None), P(cells), P(cells), P(cells, None, None), P(cells, None, None))
        + tables,
        out_specs=(P(cells, None, None), row, line) + tables[1:],
        check_vma=False,
    )
```

```python
import functools

import jax
import jax.numpy as jnp
from jax import lax
from jax.experimental import pallas as pl
from jax.experimental.pallas import tpu as pltpu
from jax.sharding import Mesh
from jax.sharding import PartitionSpec as P

HEADS = 4
INNER = 8
MISC = 16
epsilon = 1e-05
LOG2E = 1.4426950408889634
bf16 = jnp.bfloat16
f32 = jnp.float32
i32 = jnp.int32


def params():
    return pltpu.CompilerParams(vmem_limit_bytes=56 << 20)


def cost(us):
    return pl.CostEstimate(flops=int(us * 5e7), bytes_accessed=0, transcendentals=0)


def dg(left, right, a, b):
    return lax.dot_general(left, right, (((a,), (b,)), ((), ())), preferred_element_type=f32)


def smem():
    return pl.BlockSpec(memory_space=pltpu.SMEM)


def whole(*shape):
    return pl.BlockSpec(shape, lambda *_: (0,) * len(shape))


def rows(size, width):
    return pl.BlockSpec((size, width), lambda i, *_: (i, 0))


def lanes(size):
    return pl.BlockSpec((1, size), lambda i, *_: (0, i))


def aligned(index, step):
    return pl.multiple_of(index, step)


def onehot(ids, base, count):
    number = lax.broadcasted_iota(i32, (count, ids.shape[1]), 0)
    return jnp.where(number == ids - base, 1.0, 0.0).astype(bf16)


def source(coord_ref, k, j, F):
    z = lax.rem(coord_ref[0] + F - k, F)
    return z * INNER + lax.bitwise_xor(coord_ref[1], j)


def lookup_kernel(plan, F, gene_n, coord_ref, ids_ref, *refs):
    total = find_rows(plan, F, gene_n, coord_ref, ids_ref[...], refs[:-1])
    refs[-1][...] = total.astype(bf16)


def lookup(coord, ids, tables, plan, F, gene_n, block=512):
    n, width = ids.shape[1], tables[0].shape[1]
    used = sum(part[3] for parts in plan for part in parts)
    return pl.pallas_call(
        functools.partial(lookup_kernel, plan, F, gene_n),
        grid=(n // block,),
        in_specs=[smem(), lanes(block)] + [whole(*t.shape) for t in tables],
        out_specs=rows(block, width),
        out_shape=jax.ShapeDtypeStruct((n, width), bf16),
        compiler_params=params(),
        cost_estimate=cost(2.1 + n * used * 6.5e-7),
        name="lookup",
    )(coord, ids, *tables)


def count_kernel(size, coord_ref, ids_ref, out_ref):
    high_n = out_ref.shape[0]
    lines = -(-high_n // 16) * 16
    total = None
    for i in range(size):
        ids = ids_ref[i : i + 1, :]
        left = onehot(lax.shift_right_logical(ids, 7), coord_ref[0] * high_n, lines)
        right = onehot(lax.bitwise_and(ids, 127), 0, 128)
        term = dg(left, right, 1, 1)
        total = term if total is None else total + term
    add_to(out_ref, total[0:high_n, :].astype(i32))


def count_rows(coord, ids, own, size=8):
    cells, n = ids.shape
    return pl.pallas_call(
        functools.partial(count_kernel, size),
        grid=(cells // size,),
        in_specs=[smem(), rows(size, n)],
        out_specs=whole(own // 128, 128),
        out_shape=jax.ShapeDtypeStruct((own // 128, 128), i32),
        compiler_params=params(),
        cost_estimate=cost(1.15e-4 * cells * n),
        name="count_rows",
    )(coord, ids)


def add_to(ref, value):
    @pl.when(pl.program_id(0) == 0)
    def _():
        ref[...] = value

    @pl.when(pl.program_id(0) != 0)
    def _():
        ref[...] += value


def prepare_kernel(
    coord_ref, ids_ref, gene, pos, qkv, up, out, down, expr, study, *refs
):
    vectors, piece_ref, small_ref = refs[:9], refs[9], refs[10]
    p = coord_ref[1]
    width = gene.shape[1]
    sub = vectors[0].shape[1]
    per = width // sub
    lines = [
        jnp.concatenate([vectors[per * r + i][...] for i in range(per)], axis=1)
        for r in range(8 // per)
    ]
    last = vectors[8][...]
    lines.append(jnp.concatenate([last, jnp.zeros((1, width - last.shape[1]), bf16)], axis=1))
    small_ref[...] = jnp.concatenate(
        lines + [jnp.zeros((MISC - len(lines), width), bf16)], axis=0
    )
    at = 0
    for ref in (gene, pos):
        piece_ref[at : at + ref.shape[0], :] = ref[...]
        at += ref.shape[0]
    even = lax.bitwise_and(p, 1) == 0
    odd = [up[:, t * width : (t + 1) * width] for t in range(up.shape[1] // width)] + [out[...]]
    for t in range(qkv.shape[1] // width):
        piece_ref[at : at + qkv.shape[0], :] = jnp.where(
            even, qkv[:, t * width : (t + 1) * width], odd[t]
        )
        at += qkv.shape[0]
    piece_ref[at : at + down.shape[0], :] = down[...]
    at += down.shape[0]
    misc = jnp.where(p == 0, expr[...], jnp.where(p == 1, study[...], small_ref[...]))
    piece_ref[at : at + MISC, :] = jnp.where(p < 3, misc, jnp.zeros_like(misc))
    at += MISC
    n = ids_ref.shape[1]
    slot = lax.broadcasted_iota(i32, (1, n), 1)
    ids = jnp.where(slot < coord_ref[2], ids_ref[...], 255 * 128)
    for part in (lax.shift_right_logical(ids, 7), lax.bitwise_and(ids, 127)):
        part = part.astype(f32)
        lines = [part[:, t * width : (t + 1) * width] for t in range(n // width)]
        piece_ref[at : at + n // width, :] = jnp.concatenate(lines, axis=0).astype(bf16)
        at += n // width


def prepare(coord, ids, gene, pos, qkv, up, out, down, expr, study, vectors):
    width = gene.shape[1]
    eighth = [(a.shape[0] // INNER, a.shape[1]) for a in (gene, pos, down)]
    fourth = [(a.shape[0] // (INNER // 2), a.shape[1]) for a in (qkv, up, out)]
    mine = [pl.BlockSpec(s, lambda i, c: (c[1], 0)) for s in eighth]
    pair = [pl.BlockSpec(s, lambda i, c: (lax.shift_right_logical(c[1], 1), 0)) for s in fourth]
    total = sum(s[0] for s in eighth) + fourth[0][0] * fourth[0][1] // width + MISC
    total += 2 * ids.shape[1] // width
    return pl.pallas_call(
        prepare_kernel,
        grid_spec=pltpu.PrefetchScalarGridSpec(
            num_scalar_prefetch=1,
            grid=(1,),
            in_specs=[whole(*ids.shape)] + mine[0:2] + pair + mine[2:]
            + [whole(*a.shape) for a in (expr, study, *vectors)],
            out_specs=[whole(total, width), whole(MISC, width)],
        ),
        out_shape=[
            jax.ShapeDtypeStruct((total, width), bf16),
            jax.ShapeDtypeStruct((MISC, width), bf16),
        ],
        compiler_params=params(),
        cost_estimate=cost(2.5),
        name="prepare",
    )(coord, ids, gene, pos, qkv, up, out, down, expr, study, *vectors)


def assemble(F, n, coord_ref, local, pieces, outs, misc):
    pos_loc, qkv_loc, up_loc, out_loc, down_loc, *misc_loc = local
    pos, cat, down, expr, study, vec, up_vec, ids = outs
    z, p = coord_ref[0], coord_ref[1]
    width = pos.shape[1]
    pos_n, cat_n = pos_loc.shape[0] // INNER, qkv_loc.shape[0] // (INNER // 2)
    down_n = down_loc.shape[0] // INNER
    half = cat.shape[2]
    parts = half // width
    rows_z = cat_n * (INNER // 2)
    lines = n // width
    rest_n = pos_n + cat_n * parts + down_n + MISC + 2 * lines

    def genes(row, ref, at):
        high, low = ref[at : at + lines, :], ref[at + lines : at + 2 * lines, :]
        number = (high.astype(f32) * 128.0 + low.astype(f32)).astype(i32)
        for t in range(lines):
            ids[row : row + 1, t * width : (t + 1) * width] = number[t : t + 1, :]

    pos[pl.ds(aligned(z * pos_n * INNER, 16), pos_n * INNER), :] = pos_loc[...]
    down[pl.ds(aligned(z * down_n * INNER, 16), down_n * INNER), :] = down_loc[...]
    span = pl.ds(aligned(z * rows_z, 16), rows_z)
    cat[0, span, :] = qkv_loc[...]
    cat[1, span, 0 : half - width] = up_loc[...]
    cat[1, span, half - width :] = out_loc[...]
    for t in range(3):
        misc[z * INNER + t] = misc_loc[t][...]
    for j in range(INNER):
        pj = lax.bitwise_xor(p, j)
        ref = pieces[j]
        for k in range(1, F):
            zk = lax.rem(z + F - k, F)
            at = rest_n * (k - 1)
            pos[pl.ds(aligned((zk * INNER + pj) * pos_n, 16), pos_n), :] = ref[at : at + pos_n, :]
            at += pos_n
            row = aligned(zk * rows_z + lax.shift_right_logical(pj, 1) * cat_n, 16)
            side = lax.bitwise_and(pj, 1)
            for s in range(parts):
                cat[side, pl.ds(row, cat_n), s * width : (s + 1) * width] = ref[at : at + cat_n, :]
                at += cat_n
            down[pl.ds(aligned((zk * INNER + pj) * down_n, 16), down_n), :] = ref[at : at + down_n, :]
            at += down_n
            misc[zk * INNER + pj] = ref[at : at + MISC, :]
            genes(k * INNER + j, ref, at + MISC)
        genes(j, ref, rest_n * (F - 1))
    sub = width // F
    for zz in range(F):
        expr[MISC * zz : MISC * zz + MISC, :] = misc[zz * INNER]
        study[MISC * zz : MISC * zz + MISC, :] = misc[zz * INNER + 1]
    small = [misc[zz * INNER + 2].astype(f32) for zz in range(F)]
    for i in range(8):
        r, c = i // F, sub * (i % F)
        vec[i : i + 1, :] = jnp.concatenate([s[r : r + 1, c : c + sub] for s in small], axis=1)
    r = 8 // F
    up_vec[...] = jnp.concatenate(
        [s[r : r + 1, 0 : up_vec.shape[1] // F] for s in small], axis=1
    )


def standard(values):
    average = jnp.mean(values, axis=1, keepdims=True)
    centered = values - average
    scale = lax.rsqrt(jnp.mean(centered * centered, axis=1, keepdims=True) + epsilon)
    return centered * scale, scale


def slot_mask(len_ref, size):
    slot = pl.program_id(0) * size + lax.broadcasted_iota(i32, (size, 1), 0)
    return (slot < len_ref[2]).astype(f32)


def find_rows(plan, F, gene_n, coord_ref, ids, tables):
    total = None
    for table, parts in zip(tables, plan):
        hits = [
            onehot(ids, source(coord_ref, k, j, F) * gene_n + off, count)
            if j is not None
            else onehot(ids, coord_ref[0] * gene_n * INNER, count)
            for k, j, off, count in parts
        ]
        hits = hits[0] if len(hits) == 1 else jnp.concatenate(hits, axis=0)
        term = dg(hits, table[table.shape[0] - hits.shape[0] :, :], 0, 0)
        total = term if total is None else total + term
    return total


def embed_kernel(F, n, gene_n, plan, use, sizes, coord_ref, ids_ref, bins_ref, prior, *refs):
    size, found_n, local_n, piece_n = sizes
    found, refs = refs[:found_n], refs[found_n:]
    local, refs = refs[:local_n], refs[local_n:]
    pieces, refs = refs[:piece_n], refs[piece_n:]
    inputs_ref, q_ref, k_ref, v_ref = refs[0:4]
    pos, cat, down, expr, study, vec, up_vec, ids_all, misc = refs[4:]
    width = prior.shape[1]

    @pl.when(pl.program_id(0) == 0)
    def _():
        assemble(F, n, coord_ref, local, [pieces[t] for t in use], refs[4:-1], misc)

    total = find_rows(plan, F, gene_n, coord_ref, ids_ref[...], pieces[piece_n - len(plan) :])
    total = total + dg(onehot(bins_ref[...], 0, expr.shape[0]), expr[...], 0, 0)
    for ref in found:
        total = total + ref[...].astype(f32)
    here = (lax.broadcasted_iota(i32, (8, study.shape[0]), 1) == coord_ref[3]).astype(bf16)
    total = total + dg(here, study[...], 1, 0)[0:1, :]
    slots = pl.ds(aligned(pl.program_id(0) * size, size), size)
    total = total + pos[slots, :].astype(f32) + prior[...].astype(f32)
    total = total * slot_mask(coord_ref, size)
    inputs_ref[...] = total
    normed, _ = standard(total)
    normed = (normed * vec[0:1, :] + vec[1:2, :]).astype(bf16)
    mixed = dg(normed, cat[0], 1, 0)
    q_ref[...] = (mixed[:, 0:width] + vec[2:3, :]).astype(bf16)
    k_ref[...] = mixed[:, width : 2 * width].astype(bf16)
    v_ref[...] = (mixed[:, 2 * width :] + vec[3:4, :]).astype(bf16)


def embed(coord, ids, bins, prior, found, local, pieces, use, plan, F, gene_n, rest, size=512):
    n, width = prior.shape
    pos, qkv, up, out, down, *_ = local
    block = rows(size, width)
    outs = [
        ((F * pos.shape[0], width), bf16),
        ((2, F * qkv.shape[0], qkv.shape[1]), bf16),
        ((F * down.shape[0], width), bf16),
        ((F * MISC, width), bf16),
        ((F * MISC, width), bf16),
        ((8, width), f32),
        ((1, up.shape[1]), f32),
        ((F * INNER, n), i32),
    ]
    short = len(pieces) - len(plan)
    kernel = functools.partial(
        embed_kernel, F, n, gene_n, plan, use, (size, len(found), len(local), len(pieces))
    )
    return pl.pallas_call(
        kernel,
        grid=(n // size,),
        in_specs=[smem(), lanes(size), lanes(size)]
        + [block] * (1 + len(found))
        + [whole(*a.shape) for a in local]
        + [whole(rest, width)] * short
        + [whole(*a.shape) for a in pieces[short:]],
        out_specs=[block] * 4 + [whole(*s) for s, _ in outs],
        out_shape=[jax.ShapeDtypeStruct((n, width), f32)]
        + [jax.ShapeDtypeStruct((n, width), bf16)] * 3
        + [jax.ShapeDtypeStruct(*s) for s in outs],
        scratch_shapes=[pltpu.VMEM((F * INNER, MISC, width), bf16)],
        compiler_params=params(),
        cost_estimate=cost(15.5),
        name="embed",
    )(coord, ids, bins, prior, *found, *local, *pieces)


def extend(pair, half, spare):
    size = pair.shape[1] // 2
    lane = lax.broadcasted_iota(i32, pair.shape, 1)
    base = size * (1 - half)
    out = jnp.where((lane >= size * half) & (lane < size * half + size), pair, jnp.zeros_like(pair))
    for t, value in enumerate(spare):
        out = jnp.where(lane == base + t, jnp.broadcast_to(value, pair.shape), out)
    return out


def one():
    return jnp.ones((1, 1), bf16)


def split3(value):
    high = value.astype(bf16)
    rest = value - high.astype(f32)
    middle = rest.astype(bf16)
    return high, middle, (rest - middle.astype(f32)).astype(bf16)


def key_bias(len_ref, n):
    slot = lax.broadcasted_iota(i32, (n, 1), 0)
    return jnp.where(slot < len_ref[0], 0.0, -1e9).astype(bf16)


def pair_lanes(h, pair):
    return slice(pair * (h // 2), pair * (h // 2) + pair)


def attend_kernel(len_ref, q_ref, k_ref, v_ref, o_ref, wide_ref, lse_ref, kx, vt):
    n, width = k_ref.shape
    size = width // HEADS
    factor = size ** (-0.5) * LOG2E

    @pl.when(pl.program_id(0) == 0)
    def _():
        bias = key_bias(len_ref, n)
        for h in range(HEADS):
            kx[h] = extend(k_ref[:, pair_lanes(h, 2 * size)], h % 2, [bias])
        vt[...] = v_ref[...].T

    outs = []
    for h in range(HEADS):
        qx = extend(q_ref[:, pair_lanes(h, 2 * size)], h % 2, [one()])
        scores = dg(kx[h], qx, 1, 1)
        peak = jnp.max(scores, axis=0, keepdims=True)
        raised = jnp.exp2((scores - peak) * factor)
        total = jnp.sum(raised, axis=0, keepdims=True)
        out = dg(vt[size * h : size * h + size, :], raised.astype(bf16), 1, 0)
        outs.append(out * (1.0 / total))
        lse_ref[h : h + 1, :] = peak + jnp.log2(total) * (1.0 / factor)
    out = jnp.concatenate(outs, axis=0).T
    wide_ref[...] = out
    o_ref[...] = out.astype(bf16)


def attend(length, q, k, v, size=512):
    n, width = q.shape
    return pl.pallas_call(
        attend_kernel,
        grid=(n // size,),
        in_specs=[smem(), rows(size, width), whole(n, width), whole(n, width)],
        out_specs=[rows(size, width)] * 2 + [pl.BlockSpec((8, size), lambda i: (0, i))],
        out_shape=[
            jax.ShapeDtypeStruct((n, width), bf16),
            jax.ShapeDtypeStruct((n, width), f32),
            jax.ShapeDtypeStruct((8, n), f32),
        ],
        scratch_shapes=[
            pltpu.VMEM((HEADS, n, 2 * width // HEADS), bf16),
            pltpu.VMEM((width, n), bf16),
        ],
        compiler_params=params(),
        cost_estimate=cost(30),
        name="attend",
    )(length, q, k, v)


def attend_back_kernel(
    first, len_ref, q_ref, k_ref, v_ref, o_ref, do_ref, lse_ref, *refs
):
    dq_ref, dk_ref, dv_ref, kx, vx, dkt, dvt = refs[-7:]
    n, pair = k_ref.shape
    size = pair // 2
    scale = size ** (-0.5)
    factor = scale * LOG2E

    @pl.when(pl.program_id(0) == 0)
    def _():
        bias = key_bias(len_ref, n)
        for h in range(2):
            kx[h] = extend(k_ref[...], h, [bias, one(), one(), one()])
            vx[h] = extend(v_ref[...], h, [one(), one(), one()])
        dkt[...] = jnp.zeros_like(dkt)
        dvt[...] = jnp.zeros_like(dvt)

    lse = lse_ref[...].T
    qt = q_ref[...].T
    dot = do_ref[...].T
    product = do_ref[...].astype(f32) * o_ref[...]
    grads = []
    for h in range(2):
        span = slice(size * h, size * h + size)
        inner = jnp.sum(product[:, span], axis=1, keepdims=True)
        qx = extend(q_ref[...], h, [one(), *split3(-lse[:, first + h : first + h + 1])])
        dox = extend(do_ref[...], h, [*split3(-inner)])
        probs = jnp.exp2(dg(qx, kx[h], 1, 1) * factor)
        grad_scores = (probs * dg(dox, vx[h], 1, 1)).astype(bf16)
        dvt[span, :] += dg(dot[span, :], probs.astype(bf16), 1, 0)
        dkt[span, :] += dg(qt[span, :], grad_scores, 1, 0)
        grads.append(dg(grad_scores, kx[h], 1, 0))
    low = lax.broadcasted_iota(i32, grads[0].shape, 1) < size
    dq_ref[...] = (jnp.where(low, grads[0], grads[1]) * scale).astype(bf16)

    @pl.when(pl.program_id(0) == pl.num_programs(0) - 1)
    def _():
        dk_ref[...] = (dkt[...] * scale).T.astype(bf16)
        dv_ref[...] = dvt[...].T.astype(bf16)


def attend_back(length, q, k, v, o, do, lse, pair, old, size=256):
    n, width = q.shape
    two = 2 * width // HEADS
    block = pl.BlockSpec((size, two), lambda i: (i, pair))
    full = pl.BlockSpec((n, two), lambda i: (0, pair))
    return pl.pallas_call(
        functools.partial(attend_back_kernel, 2 * pair),
        grid=(n // size,),
        in_specs=[smem(), block, full, full, block, block, pl.BlockSpec((8, size), lambda i: (0, i))]
        + [pl.BlockSpec(memory_space=pl.ANY)] * len(old),
        out_specs=[block, full, full],
        out_shape=[jax.ShapeDtypeStruct((n, width), bf16)] * 3,
        input_output_aliases={7 + i: i for i in range(len(old))},
        scratch_shapes=[pltpu.VMEM((2, n, two), bf16)] * 2 + [pltpu.VMEM((two, n), f32)] * 2,
        compiler_params=params(),
        cost_estimate=cost(26),
        name="attend_back",
    )(length, q, k, v, o, do, lse, *old)


def feed_kernel(
    size, len_ref, att_ref, in_ref, cot_ref, cat, down, vec, up_vec,
    hidden_ref, mid_ref, datt_ref, wg_ref, g_vec, g_up_vec, g_down, g_up, g_out,
):
    width = att_ref.shape[1]
    up_width = down.shape[0]
    w_up, w_out = cat[1, :, 0:up_width], cat[1, :, up_width:]
    mask = slot_mask(len_ref, size)
    att = att_ref[...]
    middle = in_ref[...] + dg(att, w_out, 1, 0) + vec[4:5, :]
    normed, scale = standard(middle)
    low = (normed * vec[5:6, :] + vec[6:7, :]).astype(bf16)
    upward = dg(low, w_up, 1, 0) + up_vec[...]
    share = 0.5 * (1.0 + lax.erf(upward * (0.5**0.5)))
    active = (upward * share).astype(bf16)
    result = middle + dg(active, down[...], 1, 0) + vec[7:8, :]
    hidden_ref[...] = (result * mask).astype(bf16)
    grad_low = (cot_ref[...].astype(f32) * mask).astype(bf16)
    grad = grad_low.astype(f32)
    bell = jnp.exp(upward * upward * -0.5) * 0.3989422804014327
    grad_up = ((share + upward * bell) * dg(grad_low, down[...], 1, 1)).astype(bf16)
    grad_norm = dg(grad_up, w_up, 1, 1)
    scaled = grad_norm * vec[5:6, :]
    back = scaled - jnp.mean(scaled, axis=1, keepdims=True)
    back = back - normed * jnp.mean(scaled * normed, axis=1, keepdims=True)
    grad_mid = grad + scale * back
    branch = grad_mid.astype(bf16)
    mid_ref[...] = grad_mid
    datt_ref[...] = dg(branch, w_out, 1, 1).astype(bf16)
    add_to(g_down, dg(active, grad_low, 0, 0))
    add_to(g_up, dg(low, grad_up, 0, 0))
    add_to(g_out, dg(att, branch, 0, 0))
    sums = [
        jnp.sum(t, axis=0, keepdims=True)
        for t in (branch.astype(f32), grad_norm * normed, grad_norm, grad)
    ]
    add_to(g_vec, jnp.concatenate(sums + sums, axis=0))
    add_to(g_up_vec, jnp.sum(grad_up.astype(f32), axis=0, keepdims=True))

    @pl.when(pl.program_id(0) == pl.num_programs(0) - 1)
    def _():
        F = wg_ref.shape[3]
        line_n, down_n = width // F // INNER, up_width // F // INNER
        for z in range(F):
            for p in range(INNER):
                at = line_n * (INNER * z + p)
                blocks = [
                    g_up[at : at + line_n, t * width : (t + 1) * width]
                    for t in range(up_width // width)
                ]
                blocks.append(g_out[at : at + line_n, :])
                at = down_n * (INNER * z + p)
                blocks.append(g_down[at : at + down_n, :])
                at = 0
                for b in blocks:
                    wg_ref[p % 2, p // 2 % 2, p // 4, z, at : at + b.shape[0], :] = b.astype(bf16)
                    at += b.shape[0]


def feed(coord, att, inputs, cot, cat, down, vec, up_vec, F, size=256):
    n, width = att.shape
    up_width = down.shape[0]
    block = rows(size, width)
    w_rows = (width * (up_width + width) // width + up_width) // F // INNER
    shapes = [(2, 2, 2, F, w_rows, width), (8, width), (1, up_width)]
    return pl.pallas_call(
        functools.partial(feed_kernel, size),
        grid=(n // size,),
        in_specs=[smem(), block, block, block]
        + [whole(*a.shape) for a in (cat, down, vec, up_vec)],
        out_specs=[block] * 3 + [whole(*s) for s in shapes],
        out_shape=[
            jax.ShapeDtypeStruct((n, width), bf16),
            jax.ShapeDtypeStruct((n, width), f32),
            jax.ShapeDtypeStruct((n, width), bf16),
        ]
        + [jax.ShapeDtypeStruct(shapes[0], bf16)]
        + [jax.ShapeDtypeStruct(s, f32) for s in shapes[1:]],
        scratch_shapes=[
            pltpu.VMEM((up_width, width), f32),
            pltpu.VMEM((width, up_width), f32),
            pltpu.VMEM((width, width), f32),
        ],
        compiler_params=params(),
        cost_estimate=cost(20),
        name="feed",
    )(coord, att, inputs, cot, cat, down, vec, up_vec)


def inputs_back_kernel(size, coord_ref, dq_ref, dk_ref, dv_ref, in_ref, mid_ref, cat, vec, out_ref, norm_ref):
    width = dq_ref.shape[1]
    normed, scale = standard(in_ref[...])
    grad_norm = None
    for t, part in enumerate((dq_ref, dk_ref, dv_ref)):
        term = dg(part[...], cat[0, :, t * width : (t + 1) * width], 1, 1)
        grad_norm = term if grad_norm is None else grad_norm + term
    scaled = grad_norm * vec[0:1, :]
    back = scaled - jnp.mean(scaled, axis=1, keepdims=True)
    back = back - normed * jnp.mean(scaled * normed, axis=1, keepdims=True)
    out_ref[...] = ((mid_ref[...] + scale * back) * slot_mask(coord_ref, size)).astype(bf16)
    norm_ref[...] = grad_norm


def inputs_back(coord, dq, dk, dv, inputs, mid, cat, vec, size=512):
    n, width = dq.shape
    block = rows(size, width)
    return pl.pallas_call(
        functools.partial(inputs_back_kernel, size),
        grid=(n // size,),
        in_specs=[smem()] + [block] * 5
        + [pl.BlockSpec((1, *cat.shape[1:]), lambda i: (0, 0, 0)), whole(*vec.shape)],
        out_specs=[block] * 2,
        out_shape=[jax.ShapeDtypeStruct((n, width), t) for t in (bf16, f32)],
        compiler_params=params(),
        cost_estimate=cost(6.4),
        name="inputs_back",
    )(coord, dq, dk, dv, inputs, mid, cat, vec)


def weights_back_kernel(
    size, F, scalar_ref, bins_ref, dq_ref, dk_ref, dv_ref, in_ref, grad_ref, norm_ref, vec,
    g_vec2, g_up_vec, wg_ref, g_qkv, g_vec, g_expr,
):
    width = dq_ref.shape[1]
    normed, _ = standard(in_ref[...])
    low = (normed * vec[0:1, :] + vec[1:2, :]).astype(bf16)
    for t, part in enumerate((dq_ref, dk_ref, dv_ref)):
        add_to(g_qkv.at[:, t * width : (t + 1) * width], dg(low, part[...], 0, 0))
    grad_norm, grad = norm_ref[...], grad_ref[...]
    sums = [
        jnp.sum(t, axis=0, keepdims=True)
        for t in (
            grad_norm * normed,
            grad_norm,
            dq_ref[...].astype(f32),
            dv_ref[...].astype(f32),
            grad.astype(f32),
        )
    ]
    add_to(g_vec, jnp.concatenate(sums + sums[0:3], axis=0))
    add_to(g_expr, dg(onehot(bins_ref[...], 0, g_expr.shape[0]), grad, 1, 0))

    @pl.when(pl.program_id(0) == pl.num_programs(0) - 1)
    def _():
        line_n = width // F // INNER
        sub = width // F
        up_sub = g_up_vec.shape[1] // F
        groups = g_expr.shape[0]
        here = lax.broadcasted_iota(i32, (groups, width), 0) == scalar_ref[3]
        g_study = jnp.where(here, jnp.broadcast_to(g_vec[4:5, :], (groups, width)), 0.0)
        vectors = [g_vec[i : i + 1, :] for i in range(4)] + [g_vec2[i : i + 1, :] for i in range(4)]
        for z in range(F):
            small = []
            for r in range(8 // F):
                small.append(
                    jnp.concatenate(
                        [vectors[r * F + i][:, z * sub : (z + 1) * sub] for i in range(F)], axis=1
                    )
                )
            up_row = g_up_vec[:, z * up_sub : (z + 1) * up_sub]
            small.append(jnp.concatenate([up_row, jnp.zeros((1, width - up_sub), f32)], axis=1))
            small.append(jnp.zeros((8 - len(small), width), f32))
            at = MISC * z
            misc = [
                g_expr[at : at + 8, :],
                g_expr[at + 8 : at + 16, :],
                g_study[at : at + 8, :],
                g_study[at + 8 : at + 16, :],
                jnp.concatenate(small, axis=0),
            ]
            for p in range(INNER):
                at = line_n * (INNER * z + p)
                blocks = [
                    g_qkv[at : at + line_n, t * width : (t + 1) * width] for t in range(3)
                ] + [misc[p] if p < 5 else jnp.zeros((8, width), f32)]
                wg_ref[p % 2, p // 2 % 2, p // 4, z] = jnp.concatenate(blocks, axis=0).astype(bf16)


def weights_back(coord, bins, dq, dk, dv, inputs, grad, norm, vec, grads, half, bins_total, F, size=512):
    n, width = dq.shape
    block = rows(size, width)
    shape = (2, 2, 2, F, half // F // INNER + 8, width)
    return pl.pallas_call(
        functools.partial(weights_back_kernel, size, F),
        grid=(n // size,),
        in_specs=[smem(), lanes(size)] + [block] * 6 + [whole(*a.shape) for a in (vec, *grads)],
        out_specs=whole(*shape),
        out_shape=jax.ShapeDtypeStruct(shape, bf16),
        scratch_shapes=[
            pltpu.VMEM((width, half), f32),
            pltpu.VMEM((8, width), f32),
            pltpu.VMEM((bins_total, width), f32),
        ],
        compiler_params=params(),
        cost_estimate=cost(9),
        name="weights_back",
    )(coord, bins, dq, dk, dv, inputs, grad, norm, vec, *grads)


def scatter_kernel(cells, F, gene_n, pos_n, start_at, extra, coord_ref, *refs):
    ids, refs = refs[0], refs[1:]
    grads, refs = refs[: len(cells)], refs[len(cells) :]
    lines, old, out_ref = refs[:extra], refs[extra:-1], refs[-1]
    number = pl.program_id(0) + start_at
    z = lax.rem(coord_ref[0] + number, F)
    other = (number < F).astype(i32)
    place = z * INNER + lax.bitwise_xor(coord_ref[1], other)
    total = None
    for (cell, start, size), ref in zip(cells, grads):
        hits = onehot(ids[cell : cell + 1, start : start + size], place * gene_n, gene_n)
        term = dg(hits, ref[0:size, :], 1, 0)
        total = term if total is None else total + term
    line = None
    for (cell, start, size), ref in zip(cells, grads):
        inside = (place * pos_n >= start) & (place * pos_n < start + size)
        at = aligned(jnp.where(inside, place * pos_n - start, 0), 16)
        term = jnp.where(inside, ref[pl.ds(at, pos_n), :].astype(f32), 0.0)
        line = term if line is None else line + term
    for ref in old:
        total = total + ref[0, 0:gene_n, :]
        line = line + ref[0, gene_n : gene_n + pos_n, :]

    out_ref[0, 0:gene_n, :] = total.astype(out_ref.dtype)
    out_ref[0, gene_n : gene_n + pos_n, :] = line.astype(out_ref.dtype)
    for ref in lines:
        out_ref[0, gene_n + pos_n :, :] = ref[z]


def scatter(coord, cells, ids, grads, old, extra, F, gene_n, pos_n, start):
    width = grads[0].shape[1]
    size = gene_n + pos_n
    count = F if old else 2 * F
    more = [] if extra is None else [extra]
    full = size + sum(e.shape[1] for e in more)
    return pl.pallas_call(
        functools.partial(scatter_kernel, cells, F, gene_n, pos_n, start, len(more)),
        grid=(count,),
        in_specs=[smem(), whole(INNER, ids.shape[1])]
        + [whole(*g.shape) for g in grads]
        + [whole(*e.shape) for e in more]
        + [pl.BlockSpec((1, size, width), lambda i: (i + start, 0, 0))] * len(old),
        out_specs=pl.BlockSpec((1, full, width), lambda i: (i, 0, 0)),
        out_shape=jax.ShapeDtypeStruct((count, full, width), bf16 if old else f32),
        compiler_params=params(),
        cost_estimate=cost(2.5 + count * sum(c[2] for c in cells) * 2.5e-4),
        name="scatter",
    )(coord, ids, *grads, *more, *old)


def unpack_kernel(F, gene_n, pos_n, line_n, down_n, coord_ref, *refs):
    pieces, refs = refs[: INNER + 2], refs[INNER + 2 :]
    gene, pos, qkv, up, out, down, expr, study = refs[:8]
    vectors, misc = refs[8:17], refs[17]
    p = coord_ref[1]
    width = gene.shape[1]
    for j in range(INNER):
        pj = lax.bitwise_xor(p, j)
        if j < 6:
            here = [(pieces[j], 0)]
        else:
            top, bottom = pieces[6 + 2 * (j - 6)], pieces[7 + 2 * (j - 6)]
            here = [(top, 0), (bottom, top.shape[0])]
        for ref, first in here:
            count = min(ref.shape[0], gene_n - first)
            gene[pl.ds(aligned(gene_n * pj + first, 16), count), :] = ref[0:count, :].astype(f32)
        ref, first = here[-1]
        at = gene_n - first
        tail = ref[at : at + pos_n, :].astype(f32)
        pos[pl.ds(aligned(pos_n * pj, 16), pos_n), :] = tail
        at += pos_n
        tail = ref[at:, :].astype(f32)
        row = pl.ds(aligned(line_n * pj, 8), line_n)
        at = 0
        for s in range(up.shape[1] // width):
            up[row, s * width : (s + 1) * width] = tail[at : at + line_n, :]
            at += line_n
        out[row, :] = tail[at : at + line_n, :]
        at += line_n
        down[pl.ds(aligned(pj * down_n, 16), down_n), :] = tail[at : at + down_n, :]
        at += down_n
        for s in range(3):
            qkv[row, s * width : (s + 1) * width] = tail[at : at + line_n, :]
            at += line_n
        misc[pj] = tail[at : at + 8, :]
    for t in range(2):
        expr[8 * t : 8 * t + 8, :] = misc[t]
        study[8 * t : 8 * t + 8, :] = misc[2 + t]
    small = misc[4]
    sub = width // F
    for i in range(8):
        vectors[i][...] = small[i // F : i // F + 1, sub * (i % F) : sub * (i % F + 1)]
    vectors[8][...] = small[8 // F : 8 // F + 1, 0 : vectors[8].shape[1]]


def unpack(coord, pieces, F, gene_n, pos_n, line_n, down_n, up_width):
    width = pieces[0].shape[1]
    vmem = pl.BlockSpec(memory_space=pltpu.VMEM)
    shapes = [
        (gene_n * INNER, width),
        (pos_n * INNER, width),
        (line_n * INNER, 3 * width),
        (line_n * INNER, up_width),
        (line_n * INNER, width),
        (down_n * INNER, width),
        (MISC, width),
        (MISC, width),
    ]
    shapes += [(1, width // F)] * 8 + [(1, up_width // F)]
    return pl.pallas_call(
        functools.partial(unpack_kernel, F, gene_n, pos_n, line_n, down_n),
        in_specs=[smem()] + [vmem] * len(pieces),
        out_shape=[jax.ShapeDtypeStruct(s, f32) for s in shapes],
        scratch_shapes=[pltpu.VMEM((INNER, 8, width), f32)],
        compiler_params=params(),
        cost_estimate=cost(3.7),
        name="unpack",
    )(coord, *pieces)


def swap(array, bit):
    return lax.ppermute(array, "inner", [(i, i ^ bit) for i in range(INNER)])


def along(array, step, F):
    return lax.ppermute(array, "fsdp", [(i, (i + step) % F) for i in range(F)])


def after(arrays, work):
    return lax.optimization_barrier((arrays, work))[0]


def spread(piece, use=None):
    if use is None:
        use = lambda step, arrays: ()
    cut = piece.shape[0] // 32 * 16
    near, other, core = swap(piece, 2), swap(piece, 4), swap(piece, 1)
    near, other = after((near, other), use(0, [piece, core]))
    upper, lower = swap(near[:cut], 4), swap(other[cut:], 2)
    near1, other1 = swap(near, 1), swap(other, 1)
    upper, lower = after((upper, lower), use(1, [core, near, other, near1, other1]))
    upper1, lower1 = swap(upper, 1), swap(lower, 1)
    return [piece, core, near, near1, other, other1, upper, lower, upper1, lower1]


def plus(left, right):
    return (left.astype(f32) + right.astype(f32)).astype(bf16)


def pick(array, index, axis):
    return lax.dynamic_index_in_dim(array, index, axis, keepdims=False)


def fold_core(array, p):
    mine = lax.bitwise_and(p, 1)
    return plus(pick(array, mine, 0), swap(pick(array, 1 - mine, 0), 1))


def fold_plane(array, p):
    x, y = (lax.bitwise_and(lax.shift_right_logical(p, b), 1) for b in (1, 2))
    terms = []
    for bits in range(4):
        dx, dy = bits & 1, bits >> 1
        term = pick(pick(array, lax.bitwise_xor(x, dx), 0), lax.bitwise_xor(y, dy), 0)
        terms.append(swap(term, 2 * bits) if bits else term)
    return terms


def sum_low(terms):
    total = terms[0].astype(f32)
    for term in terms[1:]:
        total = total + term.astype(f32)
    return total.astype(bf16)


def body(
    outer, F,
    gene_ids, expr_bins, study_ids, lengths, prior_embed, cotangent,
    gene_table, expr_table, study_table, position_table,
    norm1_gain, norm1_shift, w_qkv, bias_query, bias_value, w_output, bias_output,
    norm2_gain, norm2_shift, w_up_proj, bias_up, w_down_proj, bias_down,
):
    n = gene_ids.shape[1]
    z, p = lax.axis_index("fsdp"), lax.axis_index("inner")
    gene_n = gene_table.shape[0] // INNER
    pos_n = position_table.shape[0] // INNER
    down_n = w_down_proj.shape[0] // INNER
    line_n = w_qkv.shape[0] // INNER
    prior, cot = prior_embed[0], cotangent[0]
    coord = jnp.stack([z.astype(i32), p.astype(i32), lengths[0], study_ids[0]])

    vectors = [
        v.reshape(1, -1)
        for v in (norm1_gain, norm1_shift, bias_query, bias_value,
                  bias_output, norm2_gain, norm2_shift, bias_down, bias_up)
    ]
    piece, small = prepare(
        coord, gene_ids, gene_table, position_table, w_qkv, w_up_proj, w_output, w_down_proj,
        expr_table, study_table, vectors,
    )
    got = [along(piece, k, F) for k in range(1, F)]
    gene_total = (F - 1) * gene_n

    def plan(j, first=0, count=gene_total):
        parts = []
        for k in range(F - 1):
            low, high = max(first, k * gene_n), min(first + count, (k + 1) * gene_n)
            if low < high:
                parts.append((k + 1, j, low - k * gene_n, high - low))
        return tuple(parts)

    def find(tables, plans):
        return lookup(coord, gene_ids, tables, tuple(plans), F, gene_n)

    found = [find([gene_table], [((0, None, 0, gene_table.shape[0]),)])]
    got = after(got, found[0])
    genes = piece[piece.shape[0] - 2 * n // gene_table.shape[1] :]
    stack = jnp.concatenate([g[gene_n:] for g in got] + [genes] + [g[:gene_n] for g in got])
    rest = stack.shape[0] - gene_total
    cut = stack.shape[0] // 32 * 16
    top, bottom = (0, cut - rest), (cut - rest, stack.shape[0] - cut)

    def look(step, arrays):
        if step == 0:
            found.append(find(arrays[:1], [plan(0)]))
        else:
            found.append(find(arrays[:3], [plan(1), plan(2), plan(4)]))
        return found[-1]

    pieces = spread(stack, look)
    inputs, query, keys, values, pos, cat, down, expr, study, vec, up_vec, ids = embed(
        coord, gene_ids, expr_bins, prior, found,
        [position_table, w_qkv, w_up_proj, w_output, w_down_proj, expr_table, study_table, small],
        [pieces[0], pieces[1], pieces[2], pieces[4], pieces[3], pieces[5], *pieces[6:]],
        (0, 1, 2, 4, 3, 5, 6, 8),
        (plan(3), plan(5), plan(6, *top), plan(6, *bottom), plan(7, *top), plan(7, *bottom)),
        F, gene_n, rest,
    )
    attended, wide, lse = attend(lengths, query, keys, values)
    hidden, mid, grad_attended, wg_feed, *grads = feed(
        coord, attended, inputs, cot, cat, down, vec, up_vec, F
    )
    back = (lengths, query, keys, values, wide, grad_attended, lse)
    wg_feed = fold_core(wg_feed, p)
    dqkv = attend_back(*back, 0, [])
    wg_feed, dqkv = lax.optimization_barrier((wg_feed, dqkv))
    wg_feed = fold_plane(wg_feed, p)
    dqkv = attend_back(*back, 1, dqkv)
    wg_feed, dqkv = lax.optimization_barrier((wg_feed, dqkv))
    grad, norm = inputs_back(coord, *dqkv, inputs, mid, cat, vec)

    cut = n // 2

    def add_rows(cells, arrays, old=(), start=0, extra=None):
        return scatter(coord, tuple(cells), ids, arrays, old, extra, F, gene_n, pos_n, start)

    near, other = swap(grad, 2), swap(grad, 4)
    wg = weights_back(
        coord, expr_bins, *dqkv, inputs, grad, norm, vec, grads, w_qkv.shape[1], expr.shape[0], F
    )
    first = add_rows([(0, 0, n)], [grad])
    wg = fold_plane(fold_core(wg, p), p)
    near, other, wg = after((near, other, wg), first)
    upper, lower = swap(near[:cut], 4), swap(other[cut:], 2)
    lines = jnp.concatenate([sum_low(wg_feed), sum_low(wg)], axis=1)
    second = add_rows([(2, 0, n), (4, 0, n)], [near, other])
    upper, lower = after((upper, lower), second)
    last = [(6, 0, cut), (6, cut, n - cut)]
    theirs = add_rows(last, [upper, lower], [first, second], 0)
    blocks = add_rows(last, [upper, lower], [first, second], F, lines)
    theirs = after(swap(theirs, 1), blocks)
    blocks = plus(blocks, jnp.pad(theirs, ((0, 0), (0, lines.shape[1]), (0, 0))))
    got = [along(blocks[k], k, F) for k in range(1, F)]
    own = count_rows(coord, after(ids, blocks), gene_table.shape[0])
    got = after(got, own)
    own = own.reshape(-1)
    if outer > 1:
        own = lax.psum(own, "outer")
    total = blocks[0].astype(f32)
    for g in got:
        total = total + g.astype(f32)
    if outer > 1:
        total = lax.psum(total, "outer")
    done = spread(total.astype(bf16))
    gene, pos, qkv, up, out, down, expr, study, *small = unpack(
        coord, done, F, gene_n, pos_n, line_n, down_n, w_up_proj.shape[1]
    )
    small = [s.reshape(-1) for s in small]
    return (
        hidden[None], gene, own, expr, study, pos, small[0], small[1], qkv, small[2], small[3],
        out, small[4], small[5], small[6], up, small[8], down, small[7],
    )


def solution(mesh):
    dp, F = mesh.devices.shape
    outer = dp // INNER
    mesh = Mesh(mesh.devices.reshape(outer, INNER, F), ("outer", "inner", "fsdp"))
    cells = ("outer", "inner", "fsdp")
    row, line = P("fsdp", None), P("fsdp")
    tables = (row,) * 4 + (line,) * 2 + (row, line, line, row, line, line, line, row, line, row, line)
    return jax.shard_map(
        functools.partial(body, outer, F),
        mesh=mesh,
        in_specs=(P(cells, None), P(cells, None), P(cells), P(cells), P(cells, None, None), P(cells, None, None))
        + tables,
        out_specs=(P(cells, None, None), row, line) + tables[1:],
        check_vma=False,
    )
```

```python
import functools

import jax
import jax.numpy as jnp
from jax import lax
from jax.experimental import pallas as pl
from jax.experimental.pallas import tpu as pltpu
from jax.sharding import Mesh
from jax.sharding import PartitionSpec as P

HEADS = 4
INNER = 8
MISC = 16
epsilon = 1e-05
LOG2E = 1.4426950408889634
bf16 = jnp.bfloat16
f32 = jnp.float32
i32 = jnp.int32


def params():
    return pltpu.CompilerParams(vmem_limit_bytes=56 << 20)


def cost(us):
    return pl.CostEstimate(flops=int(us * 5e7), bytes_accessed=0, transcendentals=0)


def dg(left, right, a, b):
    return lax.dot_general(left, right, (((a,), (b,)), ((), ())), preferred_element_type=f32)


def smem():
    return pl.BlockSpec(memory_space=pltpu.SMEM)


def whole(*shape):
    return pl.BlockSpec(shape, lambda *_: (0,) * len(shape))


def rows(size, width):
    return pl.BlockSpec((size, width), lambda i, *_: (i, 0))


def lanes(size):
    return pl.BlockSpec((1, size), lambda i, *_: (0, i))


def aligned(index, step):
    return pl.multiple_of(index, step)


def onehot(ids, base, count):
    number = lax.broadcasted_iota(i32, (count, ids.shape[1]), 0)
    return jnp.where(number == ids - base, 1.0, 0.0).astype(bf16)


def source(coord_ref, k, j, F):
    z = lax.rem(coord_ref[0] + F - k, F)
    return z * INNER + lax.bitwise_xor(coord_ref[1], j)


def lookup_kernel(plan, F, gene_n, coord_ref, ids_ref, *refs):
    total = find_rows(plan, F, gene_n, coord_ref, ids_ref[...], refs[:-1])
    refs[-1][...] = total.astype(bf16)


def lookup(coord, ids, tables, plan, F, gene_n, block=512):
    n, width = ids.shape[1], tables[0].shape[1]
    used = sum(part[3] for parts in plan for part in parts)
    return pl.pallas_call(
        functools.partial(lookup_kernel, plan, F, gene_n),
        grid=(n // block,),
        in_specs=[smem(), lanes(block)] + [whole(*t.shape) for t in tables],
        out_specs=rows(block, width),
        out_shape=jax.ShapeDtypeStruct((n, width), bf16),
        compiler_params=params(),
        cost_estimate=cost(2.1 + n * used * 6.5e-7),
        name="lookup",
    )(coord, ids, *tables)


def count_kernel(size, coord_ref, ids_ref, out_ref):
    high_n = out_ref.shape[0]
    lines = -(-high_n // 16) * 16
    total = None
    for i in range(size):
        ids = ids_ref[i : i + 1, :]
        left = onehot(lax.shift_right_logical(ids, 7), coord_ref[0] * high_n, lines)
        right = onehot(lax.bitwise_and(ids, 127), 0, 128)
        term = dg(left, right, 1, 1)
        total = term if total is None else total + term
    add_to(out_ref, total[0:high_n, :].astype(i32))


def count_rows(coord, ids, own, size=8):
    cells, n = ids.shape
    return pl.pallas_call(
        functools.partial(count_kernel, size),
        grid=(cells // size,),
        in_specs=[smem(), rows(size, n)],
        out_specs=whole(own // 128, 128),
        out_shape=jax.ShapeDtypeStruct((own // 128, 128), i32),
        compiler_params=params(),
        cost_estimate=cost(1.15e-4 * cells * n),
        name="count_rows",
    )(coord, ids)


def add_to(ref, value):
    @pl.when(pl.program_id(0) == 0)
    def _():
        ref[...] = value

    @pl.when(pl.program_id(0) != 0)
    def _():
        ref[...] += value


def prepare_kernel(
    coord_ref, ids_ref, gene, pos, qkv, up, out, down, expr, study, *refs
):
    vectors, piece_ref, small_ref = refs[:9], refs[9], refs[10]
    p = coord_ref[1]
    width = gene.shape[1]
    sub = vectors[0].shape[1]
    per = width // sub
    lines = [
        jnp.concatenate([vectors[per * r + i][...] for i in range(per)], axis=1)
        for r in range(8 // per)
    ]
    last = vectors[8][...]
    lines.append(jnp.concatenate([last, jnp.zeros((1, width - last.shape[1]), bf16)], axis=1))
    small_ref[...] = jnp.concatenate(
        lines + [jnp.zeros((MISC - len(lines), width), bf16)], axis=0
    )
    at = 0
    for ref in (gene, pos):
        piece_ref[at : at + ref.shape[0], :] = ref[...]
        at += ref.shape[0]
    even = lax.bitwise_and(p, 1) == 0
    odd = [up[:, t * width : (t + 1) * width] for t in range(up.shape[1] // width)] + [out[...]]
    for t in range(qkv.shape[1] // width):
        piece_ref[at : at + qkv.shape[0], :] = jnp.where(
            even, qkv[:, t * width : (t + 1) * width], odd[t]
        )
        at += qkv.shape[0]
    piece_ref[at : at + down.shape[0], :] = down[...]
    at += down.shape[0]
    misc = jnp.where(p == 0, expr[...], jnp.where(p == 1, study[...], small_ref[...]))
    piece_ref[at : at + MISC, :] = jnp.where(p < 3, misc, jnp.zeros_like(misc))
    at += MISC
    n = ids_ref.shape[1]
    slot = lax.broadcasted_iota(i32, (1, n), 1)
    ids = jnp.where(slot < coord_ref[2], ids_ref[...], 255 * 128)
    for part in (lax.shift_right_logical(ids, 7), lax.bitwise_and(ids, 127)):
        part = part.astype(f32)
        lines = [part[:, t * width : (t + 1) * width] for t in range(n // width)]
        piece_ref[at : at + n // width, :] = jnp.concatenate(lines, axis=0).astype(bf16)
        at += n // width


def prepare(coord, ids, gene, pos, qkv, up, out, down, expr, study, vectors):
    width = gene.shape[1]
    eighth = [(a.shape[0] // INNER, a.shape[1]) for a in (gene, pos, down)]
    fourth = [(a.shape[0] // (INNER // 2), a.shape[1]) for a in (qkv, up, out)]
    mine = [pl.BlockSpec(s, lambda i, c: (c[1], 0)) for s in eighth]
    pair = [pl.BlockSpec(s, lambda i, c: (lax.shift_right_logical(c[1], 1), 0)) for s in fourth]
    total = sum(s[0] for s in eighth) + fourth[0][0] * fourth[0][1] // width + MISC
    total += 2 * ids.shape[1] // width
    return pl.pallas_call(
        prepare_kernel,
        grid_spec=pltpu.PrefetchScalarGridSpec(
            num_scalar_prefetch=1,
            grid=(1,),
            in_specs=[whole(*ids.shape)] + mine[0:2] + pair + mine[2:]
            + [whole(*a.shape) for a in (expr, study, *vectors)],
            out_specs=[whole(total, width), whole(MISC, width)],
        ),
        out_shape=[
            jax.ShapeDtypeStruct((total, width), bf16),
            jax.ShapeDtypeStruct((MISC, width), bf16),
        ],
        compiler_params=params(),
        cost_estimate=cost(2.5),
        name="prepare",
    )(coord, ids, gene, pos, qkv, up, out, down, expr, study, *vectors)


def assemble(F, n, coord_ref, local, pieces, outs, misc):
    pos_loc, qkv_loc, up_loc, out_loc, down_loc, *misc_loc = local
    pos, cat, down, expr, study, vec, up_vec, ids = outs
    z, p = coord_ref[0], coord_ref[1]
    width = pos.shape[1]
    pos_n, cat_n = pos_loc.shape[0] // INNER, qkv_loc.shape[0] // (INNER // 2)
    down_n = down_loc.shape[0] // INNER
    half = cat.shape[2]
    parts = half // width
    rows_z = cat_n * (INNER // 2)
    lines = n // width
    rest_n = pos_n + cat_n * parts + down_n + MISC + 2 * lines

    def genes(row, ref, at):
        high, low = ref[at : at + lines, :], ref[at + lines : at + 2 * lines, :]
        number = (high.astype(f32) * 128.0 + low.astype(f32)).astype(i32)
        for t in range(lines):
            ids[row : row + 1, t * width : (t + 1) * width] = number[t : t + 1, :]

    pos[pl.ds(aligned(z * pos_n * INNER, 16), pos_n * INNER), :] = pos_loc[...]
    down[pl.ds(aligned(z * down_n * INNER, 16), down_n * INNER), :] = down_loc[...]
    span = pl.ds(aligned(z * rows_z, 16), rows_z)
    cat[0, span, :] = qkv_loc[...]
    cat[1, span, 0 : half - width] = up_loc[...]
    cat[1, span, half - width :] = out_loc[...]
    for t in range(3):
        misc[z * INNER + t] = misc_loc[t][...]
    for j in range(INNER):
        pj = lax.bitwise_xor(p, j)
        ref = pieces[j]
        for k in range(1, F):
            zk = lax.rem(z + F - k, F)
            at = rest_n * (k - 1)
            pos[pl.ds(aligned((zk * INNER + pj) * pos_n, 16), pos_n), :] = ref[at : at + pos_n, :]
            at += pos_n
            row = aligned(zk * rows_z + lax.shift_right_logical(pj, 1) * cat_n, 16)
            side = lax.bitwise_and(pj, 1)
            for s in range(parts):
                cat[side, pl.ds(row, cat_n), s * width : (s + 1) * width] = ref[at : at + cat_n, :]
                at += cat_n
            down[pl.ds(aligned((zk * INNER + pj) * down_n, 16), down_n), :] = ref[at : at + down_n, :]
            at += down_n
            misc[zk * INNER + pj] = ref[at : at + MISC, :]
            genes(k * INNER + j, ref, at + MISC)
        genes(j, ref, rest_n * (F - 1))
    sub = width // F
    for zz in range(F):
        expr[MISC * zz : MISC * zz + MISC, :] = misc[zz * INNER]
        study[MISC * zz : MISC * zz + MISC, :] = misc[zz * INNER + 1]
    small = [misc[zz * INNER + 2].astype(f32) for zz in range(F)]
    for i in range(8):
        r, c = i // F, sub * (i % F)
        vec[i : i + 1, :] = jnp.concatenate([s[r : r + 1, c : c + sub] for s in small], axis=1)
    r = 8 // F
    up_vec[...] = jnp.concatenate(
        [s[r : r + 1, 0 : up_vec.shape[1] // F] for s in small], axis=1
    )


def standard(values):
    average = jnp.mean(values, axis=1, keepdims=True)
    centered = values - average
    scale = lax.rsqrt(jnp.mean(centered * centered, axis=1, keepdims=True) + epsilon)
    return centered * scale, scale


def slot_mask(len_ref, size):
    slot = pl.program_id(0) * size + lax.broadcasted_iota(i32, (size, 1), 0)
    return (slot < len_ref[2]).astype(f32)


def find_rows(plan, F, gene_n, coord_ref, ids, tables):
    total = None
    for table, parts in zip(tables, plan):
        hits = [
            onehot(ids, source(coord_ref, k, j, F) * gene_n + off, count)
            if j is not None
            else onehot(ids, coord_ref[0] * gene_n * INNER, count)
            for k, j, off, count in parts
        ]
        hits = hits[0] if len(hits) == 1 else jnp.concatenate(hits, axis=0)
        term = dg(hits, table[table.shape[0] - hits.shape[0] :, :], 0, 0)
        total = term if total is None else total + term
    return total


def embed_kernel(F, n, gene_n, plan, use, sizes, coord_ref, ids_ref, bins_ref, prior, *refs):
    size, found_n, local_n, piece_n = sizes
    found, refs = refs[:found_n], refs[found_n:]
    local, refs = refs[:local_n], refs[local_n:]
    pieces, refs = refs[:piece_n], refs[piece_n:]
    inputs_ref, q_ref, k_ref, v_ref = refs[0:4]
    pos, cat, down, expr, study, vec, up_vec, ids_all, misc = refs[4:]
    width = prior.shape[1]

    @pl.when(pl.program_id(0) == 0)
    def _():
        assemble(F, n, coord_ref, local, [pieces[t] for t in use], refs[4:-1], misc)

    total = find_rows(plan, F, gene_n, coord_ref, ids_ref[...], pieces[piece_n - len(plan) :])
    total = total + dg(onehot(bins_ref[...], 0, expr.shape[0]), expr[...], 0, 0)
    for ref in found:
        total = total + ref[...].astype(f32)
    here = (lax.broadcasted_iota(i32, (8, study.shape[0]), 1) == coord_ref[3]).astype(bf16)
    total = total + dg(here, study[...], 1, 0)[0:1, :]
    slots = pl.ds(aligned(pl.program_id(0) * size, size), size)
    total = total + pos[slots, :].astype(f32) + prior[...].astype(f32)
    total = total * slot_mask(coord_ref, size)
    inputs_ref[...] = total
    normed, _ = standard(total)
    normed = (normed * vec[0:1, :] + vec[1:2, :]).astype(bf16)
    mixed = dg(normed, cat[0], 1, 0)
    q_ref[...] = (mixed[:, 0:width] + vec[2:3, :]).astype(bf16)
    k_ref[...] = mixed[:, width : 2 * width].astype(bf16)
    v_ref[...] = (mixed[:, 2 * width :] + vec[3:4, :]).astype(bf16)


def embed(coord, ids, bins, prior, found, local, pieces, use, plan, F, gene_n, rest, size=1024):
    n, width = prior.shape
    pos, qkv, up, out, down, *_ = local
    block = rows(size, width)
    outs = [
        ((F * pos.shape[0], width), bf16),
        ((2, F * qkv.shape[0], qkv.shape[1]), bf16),
        ((F * down.shape[0], width), bf16),
        ((F * MISC, width), bf16),
        ((F * MISC, width), bf16),
        ((8, width), f32),
        ((1, up.shape[1]), f32),
        ((F * INNER, n), i32),
    ]
    short = len(pieces) - len(plan)
    kernel = functools.partial(
        embed_kernel, F, n, gene_n, plan, use, (size, len(found), len(local), len(pieces))
    )
    return pl.pallas_call(
        kernel,
        grid=(n // size,),
        in_specs=[smem(), lanes(size), lanes(size)]
        + [block] * (1 + len(found))
        + [whole(*a.shape) for a in local]
        + [whole(rest, width)] * short
        + [whole(*a.shape) for a in pieces[short:]],
        out_specs=[block] * 4 + [whole(*s) for s, _ in outs],
        out_shape=[jax.ShapeDtypeStruct((n, width), f32)]
        + [jax.ShapeDtypeStruct((n, width), bf16)] * 3
        + [jax.ShapeDtypeStruct(*s) for s in outs],
        scratch_shapes=[pltpu.VMEM((F * INNER, MISC, width), bf16)],
        compiler_params=params(),
        cost_estimate=cost(15.5),
        name="embed",
    )(coord, ids, bins, prior, *found, *local, *pieces)


def extend(pair, half, spare):
    size = pair.shape[1] // 2
    lane = lax.broadcasted_iota(i32, pair.shape, 1)
    base = size * (1 - half)
    out = jnp.where((lane >= size * half) & (lane < size * half + size), pair, jnp.zeros_like(pair))
    for t, value in enumerate(spare):
        out = jnp.where(lane == base + t, jnp.broadcast_to(value, pair.shape), out)
    return out


def one():
    return jnp.ones((1, 1), bf16)


def split3(value):
    high = value.astype(bf16)
    rest = value - high.astype(f32)
    middle = rest.astype(bf16)
    return high, middle, (rest - middle.astype(f32)).astype(bf16)


def attend_kernel(len_ref, q_ref, k_ref, v_ref, o_ref, wide_ref, inv_ref, e_ref, kx, vx):
    n, pair = k_ref.shape
    size = pair // 2
    factor = size ** (-0.5) * LOG2E

    @pl.when(pl.program_id(1) == 0)
    def _():
        slot = lax.broadcasted_iota(i32, (n, 1), 0)
        bias = jnp.where(slot < len_ref[0], 0.0, -1e9).astype(bf16)
        lane = lax.broadcasted_iota(i32, (n, pair), 1)
        for h in range(2):
            kx[h] = extend(k_ref[...], h, [bias])
            own = (lane >= size * h) & (lane < size * h + size)
            vx[h] = jnp.where(own, v_ref[...], jnp.ones_like(v_ref[...]))

    scores = [dg(extend(q_ref[...], h, [one()]), kx[h], 1, 1) for h in range(2)]
    peaks = [jnp.max(s, axis=1, keepdims=True) for s in scores]
    raised = [jnp.exp2((s - p) * factor).astype(bf16) for s, p in zip(scores, peaks)]
    outs, totals = [], []
    for h in range(2):
        e_ref[h] = raised[h]
        out = dg(raised[h], vx[h], 1, 0)
        outs.append(out)
        totals.append(jnp.concatenate([out[:, size:], out[:, :size]], axis=1))
    low = lax.broadcasted_iota(i32, outs[0].shape, 1) < size
    inverse = 1.0 / jnp.where(low, totals[0], totals[1])
    out = jnp.where(low, outs[0], outs[1]) * inverse
    inv_ref[...] = inverse
    wide_ref[...] = out
    o_ref[...] = out.astype(bf16)


def attend(length, q, k, v, size=512):
    n, width = q.shape
    two = 2 * width // HEADS
    block = pl.BlockSpec((size, two), lambda j, i: (i, j))
    full = pl.BlockSpec((n, two), lambda j, i: (0, j))
    return pl.pallas_call(
        attend_kernel,
        grid=(HEADS // 2, n // size),
        in_specs=[smem(), block, full, full],
        out_specs=[block] * 3 + [pl.BlockSpec((2, size, n), lambda j, i: (j, i, 0))],
        out_shape=[
            jax.ShapeDtypeStruct((n, width), bf16),
            jax.ShapeDtypeStruct((n, width), f32),
            jax.ShapeDtypeStruct((n, width), f32),
            jax.ShapeDtypeStruct((HEADS, n, n), bf16),
        ],
        scratch_shapes=[pltpu.VMEM((2, n, two), bf16)] * 2,
        compiler_params=params(),
        cost_estimate=cost(32),
        name="attend",
    )(length, q, k, v)


def attend_back_kernel(q_ref, k_ref, v_ref, o_ref, do_ref, inv_ref, e_ref, *refs):
    dq_ref, dk_ref, dv_ref, vx, dkt, dvt = refs[-6:]
    n, pair = k_ref.shape
    size = pair // 2
    scale = size ** (-0.5)

    @pl.when(pl.program_id(0) == 0)
    def _():
        for h in range(2):
            vx[h] = extend(v_ref[...], h, [one(), one(), one()])
        dkt[...] = jnp.zeros_like(dkt)
        dvt[...] = jnp.zeros_like(dvt)

    grad = (do_ref[...].astype(f32) * inv_ref[...]).astype(bf16)
    product = grad.astype(f32) * o_ref[...]
    qt = q_ref[...].T
    gt = grad.T
    grads = []
    for h in range(2):
        span = slice(size * h, size * h + size)
        inner = jnp.sum(product[:, span], axis=1, keepdims=True)
        raised = e_ref[h]
        back = dg(extend(grad, h, [*split3(-inner)]), vx[h], 1, 1)
        grad_scores = (raised.astype(f32) * back).astype(bf16)
        dvt[span, :] += dg(gt[span, :], raised, 1, 0)
        dkt[span, :] += dg(qt[span, :], grad_scores, 1, 0)
        grads.append(dg(grad_scores, k_ref[...], 1, 0))
    low = lax.broadcasted_iota(i32, grads[0].shape, 1) < size
    dq_ref[...] = (jnp.where(low, grads[0], grads[1]) * scale).astype(bf16)

    @pl.when(pl.program_id(0) == pl.num_programs(0) - 1)
    def _():
        dk_ref[...] = (dkt[...] * scale).T.astype(bf16)
        dv_ref[...] = dvt[...].T.astype(bf16)


def attend_back(q, k, v, o, do, inverse, raised, pair, old, size=256):
    n, width = q.shape
    two = 2 * width // HEADS
    block = pl.BlockSpec((size, two), lambda i: (i, pair))
    full = pl.BlockSpec((n, two), lambda i: (0, pair))
    return pl.pallas_call(
        attend_back_kernel,
        grid=(n // size,),
        in_specs=[block, full, full, block, block, block]
        + [pl.BlockSpec((2, size, n), lambda i: (pair, i, 0))]
        + [pl.BlockSpec(memory_space=pl.ANY)] * len(old),
        out_specs=[block, full, full],
        out_shape=[jax.ShapeDtypeStruct((n, width), bf16)] * 3,
        input_output_aliases={7 + i: i for i in range(len(old))},
        scratch_shapes=[pltpu.VMEM((2, n, two), bf16)] + [pltpu.VMEM((two, n), f32)] * 2,
        compiler_params=params(),
        cost_estimate=cost(20),
        name="attend_back",
    )(q, k, v, o, do, inverse, raised, *old)


def feed_kernel(
    size, len_ref, att_ref, in_ref, cot_ref, cat, down, vec, up_vec,
    hidden_ref, mid_ref, datt_ref, wg_ref, g_vec, g_up_vec, g_down, g_up, g_out,
):
    width = att_ref.shape[1]
    up_width = down.shape[0]
    w_up, w_out = cat[1, :, 0:up_width], cat[1, :, up_width:]
    mask = slot_mask(len_ref, size)
    att = att_ref[...]
    middle = in_ref[...] + dg(att, w_out, 1, 0) + vec[4:5, :]
    normed, scale = standard(middle)
    low = (normed * vec[5:6, :] + vec[6:7, :]).astype(bf16)
    upward = dg(low, w_up, 1, 0) + up_vec[...]
    share = 0.5 * (1.0 + lax.erf(upward * (0.5**0.5)))
    active = (upward * share).astype(bf16)
    result = middle + dg(active, down[...], 1, 0) + vec[7:8, :]
    hidden_ref[...] = (result * mask).astype(bf16)
    grad_low = (cot_ref[...].astype(f32) * mask).astype(bf16)
    grad = grad_low.astype(f32)
    bell = jnp.exp(upward * upward * -0.5) * 0.3989422804014327
    grad_up = ((share + upward * bell) * dg(grad_low, down[...], 1, 1)).astype(bf16)
    grad_norm = dg(grad_up, w_up, 1, 1)
    scaled = grad_norm * vec[5:6, :]
    back = scaled - jnp.mean(scaled, axis=1, keepdims=True)
    back = back - normed * jnp.mean(scaled * normed, axis=1, keepdims=True)
    grad_mid = grad + scale * back
    branch = grad_mid.astype(bf16)
    mid_ref[...] = grad_mid
    datt_ref[...] = dg(branch, w_out, 1, 1).astype(bf16)
    add_to(g_down, dg(active, grad_low, 0, 0))
    add_to(g_up, dg(low, grad_up, 0, 0))
    add_to(g_out, dg(att, branch, 0, 0))
    sums = [
        jnp.sum(t, axis=0, keepdims=True)
        for t in (branch.astype(f32), grad_norm * normed, grad_norm, grad)
    ]
    add_to(g_vec, jnp.concatenate(sums + sums, axis=0))
    add_to(g_up_vec, jnp.sum(grad_up.astype(f32), axis=0, keepdims=True))

    @pl.when(pl.program_id(0) == pl.num_programs(0) - 1)
    def _():
        F = wg_ref.shape[3]
        line_n, down_n = width // F // INNER, up_width // F // INNER
        for z in range(F):
            for p in range(INNER):
                at = line_n * (INNER * z + p)
                blocks = [
                    g_up[at : at + line_n, t * width : (t + 1) * width]
                    for t in range(up_width // width)
                ]
                blocks.append(g_out[at : at + line_n, :])
                at = down_n * (INNER * z + p)
                blocks.append(g_down[at : at + down_n, :])
                at = 0
                for b in blocks:
                    wg_ref[p % 2, p // 2 % 2, p // 4, z, at : at + b.shape[0], :] = b.astype(bf16)
                    at += b.shape[0]


def feed(coord, att, inputs, cot, cat, down, vec, up_vec, F, size=1024):
    n, width = att.shape
    up_width = down.shape[0]
    block = rows(size, width)
    w_rows = (width * (up_width + width) // width + up_width) // F // INNER
    shapes = [(2, 2, 2, F, w_rows, width), (8, width), (1, up_width)]
    return pl.pallas_call(
        functools.partial(feed_kernel, size),
        grid=(n // size,),
        in_specs=[smem(), block, block, block]
        + [whole(*a.shape) for a in (cat, down, vec, up_vec)],
        out_specs=[block] * 3 + [whole(*s) for s in shapes],
        out_shape=[
            jax.ShapeDtypeStruct((n, width), bf16),
            jax.ShapeDtypeStruct((n, width), f32),
            jax.ShapeDtypeStruct((n, width), bf16),
        ]
        + [jax.ShapeDtypeStruct(shapes[0], bf16)]
        + [jax.ShapeDtypeStruct(s, f32) for s in shapes[1:]],
        scratch_shapes=[
            pltpu.VMEM((up_width, width), f32),
            pltpu.VMEM((width, up_width), f32),
            pltpu.VMEM((width, width), f32),
        ],
        compiler_params=params(),
        cost_estimate=cost(20),
        name="feed",
    )(coord, att, inputs, cot, cat, down, vec, up_vec)


def inputs_back_kernel(size, coord_ref, dq_ref, dk_ref, dv_ref, in_ref, mid_ref, cat, vec, out_ref, norm_ref):
    width = dq_ref.shape[1]
    normed, scale = standard(in_ref[...])
    grad_norm = None
    for t, part in enumerate((dq_ref, dk_ref, dv_ref)):
        term = dg(part[...], cat[0, :, t * width : (t + 1) * width], 1, 1)
        grad_norm = term if grad_norm is None else grad_norm + term
    scaled = grad_norm * vec[0:1, :]
    back = scaled - jnp.mean(scaled, axis=1, keepdims=True)
    back = back - normed * jnp.mean(scaled * normed, axis=1, keepdims=True)
    out_ref[...] = ((mid_ref[...] + scale * back) * slot_mask(coord_ref, size)).astype(bf16)
    norm_ref[...] = grad_norm


def inputs_back(coord, dq, dk, dv, inputs, mid, cat, vec, size=1024):
    n, width = dq.shape
    block = rows(size, width)
    return pl.pallas_call(
        functools.partial(inputs_back_kernel, size),
        grid=(n // size,),
        in_specs=[smem()] + [block] * 5
        + [pl.BlockSpec((1, *cat.shape[1:]), lambda i: (0, 0, 0)), whole(*vec.shape)],
        out_specs=[block] * 2,
        out_shape=[jax.ShapeDtypeStruct((n, width), t) for t in (bf16, f32)],
        compiler_params=params(),
        cost_estimate=cost(6.4),
        name="inputs_back",
    )(coord, dq, dk, dv, inputs, mid, cat, vec)


def weights_back_kernel(
    size, F, scalar_ref, bins_ref, dq_ref, dk_ref, dv_ref, in_ref, grad_ref, norm_ref, vec,
    g_vec2, g_up_vec, wg_ref, g_qkv, g_vec, g_expr,
):
    width = dq_ref.shape[1]
    normed, _ = standard(in_ref[...])
    low = (normed * vec[0:1, :] + vec[1:2, :]).astype(bf16)
    for t, part in enumerate((dq_ref, dk_ref, dv_ref)):
        add_to(g_qkv.at[:, t * width : (t + 1) * width], dg(low, part[...], 0, 0))
    grad_norm, grad = norm_ref[...], grad_ref[...]
    sums = [
        jnp.sum(t, axis=0, keepdims=True)
        for t in (
            grad_norm * normed,
            grad_norm,
            dq_ref[...].astype(f32),
            dv_ref[...].astype(f32),
            grad.astype(f32),
        )
    ]
    add_to(g_vec, jnp.concatenate(sums + sums[0:3], axis=0))
    add_to(g_expr, dg(onehot(bins_ref[...], 0, g_expr.shape[0]), grad, 1, 0))

    @pl.when(pl.program_id(0) == pl.num_programs(0) - 1)
    def _():
        line_n = width // F // INNER
        sub = width // F
        up_sub = g_up_vec.shape[1] // F
        groups = g_expr.shape[0]
        here = lax.broadcasted_iota(i32, (groups, width), 0) == scalar_ref[3]
        g_study = jnp.where(here, jnp.broadcast_to(g_vec[4:5, :], (groups, width)), 0.0)
        vectors = [g_vec[i : i + 1, :] for i in range(4)] + [g_vec2[i : i + 1, :] for i in range(4)]
        for z in range(F):
            small = []
            for r in range(8 // F):
                small.append(
                    jnp.concatenate(
                        [vectors[r * F + i][:, z * sub : (z + 1) * sub] for i in range(F)], axis=1
                    )
                )
            up_row = g_up_vec[:, z * up_sub : (z + 1) * up_sub]
            small.append(jnp.concatenate([up_row, jnp.zeros((1, width - up_sub), f32)], axis=1))
            small.append(jnp.zeros((8 - len(small), width), f32))
            at = MISC * z
            misc = [
                g_expr[at : at + 8, :],
                g_expr[at + 8 : at + 16, :],
                g_study[at : at + 8, :],
                g_study[at + 8 : at + 16, :],
                jnp.concatenate(small, axis=0),
            ]
            for p in range(INNER):
                at = line_n * (INNER * z + p)
                blocks = [
                    g_qkv[at : at + line_n, t * width : (t + 1) * width] for t in range(3)
                ] + [misc[p] if p < 5 else jnp.zeros((8, width), f32)]
                wg_ref[p % 2, p // 2 % 2, p // 4, z] = jnp.concatenate(blocks, axis=0).astype(bf16)


def weights_back(coord, bins, dq, dk, dv, inputs, grad, norm, vec, grads, half, bins_total, F, size=512):
    n, width = dq.shape
    block = rows(size, width)
    shape = (2, 2, 2, F, half // F // INNER + 8, width)
    return pl.pallas_call(
        functools.partial(weights_back_kernel, size, F),
        grid=(n // size,),
        in_specs=[smem(), lanes(size)] + [block] * 6 + [whole(*a.shape) for a in (vec, *grads)],
        out_specs=whole(*shape),
        out_shape=jax.ShapeDtypeStruct(shape, bf16),
        scratch_shapes=[
            pltpu.VMEM((width, half), f32),
            pltpu.VMEM((8, width), f32),
            pltpu.VMEM((bins_total, width), f32),
        ],
        compiler_params=params(),
        cost_estimate=cost(9),
        name="weights_back",
    )(coord, bins, dq, dk, dv, inputs, grad, norm, vec, *grads)


def scatter_kernel(cells, F, gene_n, pos_n, start_at, extra, coord_ref, *refs):
    ids, refs = refs[0], refs[1:]
    grads, refs = refs[: len(cells)], refs[len(cells) :]
    lines, old, out_ref = refs[:extra], refs[extra:-1], refs[-1]
    number = pl.program_id(0) + start_at
    z = lax.rem(coord_ref[0] + number, F)
    other = (number < F).astype(i32)
    place = z * INNER + lax.bitwise_xor(coord_ref[1], other)
    total = None
    for (cell, start, size), ref in zip(cells, grads):
        hits = onehot(ids[cell : cell + 1, start : start + size], place * gene_n, gene_n)
        term = dg(hits, ref[0:size, :], 1, 0)
        total = term if total is None else total + term
    line = None
    for (cell, start, size), ref in zip(cells, grads):
        inside = (place * pos_n >= start) & (place * pos_n < start + size)
        at = aligned(jnp.where(inside, place * pos_n - start, 0), 16)
        term = jnp.where(inside, ref[pl.ds(at, pos_n), :].astype(f32), 0.0)
        line = term if line is None else line + term
    for ref in old:
        total = total + ref[0, 0:gene_n, :]
        line = line + ref[0, gene_n : gene_n + pos_n, :]

    out_ref[0, 0:gene_n, :] = total.astype(out_ref.dtype)
    out_ref[0, gene_n : gene_n + pos_n, :] = line.astype(out_ref.dtype)
    for ref in lines:
        out_ref[0, gene_n + pos_n :, :] = ref[z]


def scatter(coord, cells, ids, grads, old, extra, F, gene_n, pos_n, start):
    width = grads[0].shape[1]
    size = gene_n + pos_n
    count = F if old else 2 * F
    more = [] if extra is None else [extra]
    full = size + sum(e.shape[1] for e in more)
    return pl.pallas_call(
        functools.partial(scatter_kernel, cells, F, gene_n, pos_n, start, len(more)),
        grid=(count,),
        in_specs=[smem(), whole(INNER, ids.shape[1])]
        + [whole(*g.shape) for g in grads]
        + [whole(*e.shape) for e in more]
        + [pl.BlockSpec((1, size, width), lambda i: (i + start, 0, 0))] * len(old),
        out_specs=pl.BlockSpec((1, full, width), lambda i: (i, 0, 0)),
        out_shape=jax.ShapeDtypeStruct((count, full, width), bf16 if old else f32),
        compiler_params=params(),
        cost_estimate=cost(2.5 + count * sum(c[2] for c in cells) * 2.5e-4),
        name="scatter",
    )(coord, ids, *grads, *more, *old)


def unpack_kernel(F, gene_n, pos_n, line_n, down_n, coord_ref, *refs):
    pieces, refs = refs[: INNER + 2], refs[INNER + 2 :]
    gene, pos, qkv, up, out, down, expr, study = refs[:8]
    vectors, misc = refs[8:17], refs[17]
    p = coord_ref[1]
    width = gene.shape[1]
    for j in range(INNER):
        pj = lax.bitwise_xor(p, j)
        if j < 6:
            here = [(pieces[j], 0)]
        else:
            top, bottom = pieces[6 + 2 * (j - 6)], pieces[7 + 2 * (j - 6)]
            here = [(top, 0), (bottom, top.shape[0])]
        for ref, first in here:
            count = min(ref.shape[0], gene_n - first)
            gene[pl.ds(aligned(gene_n * pj + first, 16), count), :] = ref[0:count, :].astype(f32)
        ref, first = here[-1]
        at = gene_n - first
        tail = ref[at : at + pos_n, :].astype(f32)
        pos[pl.ds(aligned(pos_n * pj, 16), pos_n), :] = tail
        at += pos_n
        tail = ref[at:, :].astype(f32)
        row = pl.ds(aligned(line_n * pj, 8), line_n)
        at = 0
        for s in range(up.shape[1] // width):
            up[row, s * width : (s + 1) * width] = tail[at : at + line_n, :]
            at += line_n
        out[row, :] = tail[at : at + line_n, :]
        at += line_n
        down[pl.ds(aligned(pj * down_n, 16), down_n), :] = tail[at : at + down_n, :]
        at += down_n
        for s in range(3):
            qkv[row, s * width : (s + 1) * width] = tail[at : at + line_n, :]
            at += line_n
        misc[pj] = tail[at : at + 8, :]
    for t in range(2):
        expr[8 * t : 8 * t + 8, :] = misc[t]
        study[8 * t : 8 * t + 8, :] = misc[2 + t]
    small = misc[4]
    sub = width // F
    for i in range(8):
        vectors[i][...] = small[i // F : i // F + 1, sub * (i % F) : sub * (i % F + 1)]
    vectors[8][...] = small[8 // F : 8 // F + 1, 0 : vectors[8].shape[1]]


def unpack(coord, pieces, F, gene_n, pos_n, line_n, down_n, up_width):
    width = pieces[0].shape[1]
    vmem = pl.BlockSpec(memory_space=pltpu.VMEM)
    shapes = [
        (gene_n * INNER, width),
        (pos_n * INNER, width),
        (line_n * INNER, 3 * width),
        (line_n * INNER, up_width),
        (line_n * INNER, width),
        (down_n * INNER, width),
        (MISC, width),
        (MISC, width),
    ]
    shapes += [(1, width // F)] * 8 + [(1, up_width // F)]
    return pl.pallas_call(
        functools.partial(unpack_kernel, F, gene_n, pos_n, line_n, down_n),
        in_specs=[smem()] + [vmem] * len(pieces),
        out_shape=[jax.ShapeDtypeStruct(s, f32) for s in shapes],
        scratch_shapes=[pltpu.VMEM((INNER, 8, width), f32)],
        compiler_params=params(),
        cost_estimate=cost(3.7),
        name="unpack",
    )(coord, *pieces)


def swap(array, bit):
    return lax.ppermute(array, "inner", [(i, i ^ bit) for i in range(INNER)])


def along(array, step, F):
    return lax.ppermute(array, "fsdp", [(i, (i + step) % F) for i in range(F)])


def after(arrays, work):
    return lax.optimization_barrier((arrays, work))[0]


def spread(piece, use=None):
    if use is None:
        use = lambda step, arrays: ()
    cut = piece.shape[0] // 32 * 16
    near, other, core = swap(piece, 2), swap(piece, 4), swap(piece, 1)
    near, other = after((near, other), use(0, [piece, core]))
    upper, lower = swap(near[:cut], 4), swap(other[cut:], 2)
    near1, other1 = swap(near, 1), swap(other, 1)
    upper, lower = after((upper, lower), use(1, [core, near, other, near1, other1]))
    upper1, lower1 = swap(upper, 1), swap(lower, 1)
    return [piece, core, near, near1, other, other1, upper, lower, upper1, lower1]


def plus(left, right):
    return (left.astype(f32) + right.astype(f32)).astype(bf16)


def pick(array, index, axis):
    return lax.dynamic_index_in_dim(array, index, axis, keepdims=False)


def fold_core(array, p):
    mine = lax.bitwise_and(p, 1)
    return plus(pick(array, mine, 0), swap(pick(array, 1 - mine, 0), 1))


def fold_plane(array, p):
    x, y = (lax.bitwise_and(lax.shift_right_logical(p, b), 1) for b in (1, 2))
    terms = []
    for bits in range(4):
        dx, dy = bits & 1, bits >> 1
        term = pick(pick(array, lax.bitwise_xor(x, dx), 0), lax.bitwise_xor(y, dy), 0)
        terms.append(swap(term, 2 * bits) if bits else term)
    return terms


def sum_low(terms):
    total = terms[0].astype(f32)
    for term in terms[1:]:
        total = total + term.astype(f32)
    return total.astype(bf16)


def body(
    outer, F,
    gene_ids, expr_bins, study_ids, lengths, prior_embed, cotangent,
    gene_table, expr_table, study_table, position_table,
    norm1_gain, norm1_shift, w_qkv, bias_query, bias_value, w_output, bias_output,
    norm2_gain, norm2_shift, w_up_proj, bias_up, w_down_proj, bias_down,
):
    n = gene_ids.shape[1]
    z, p = lax.axis_index("fsdp"), lax.axis_index("inner")
    gene_n = gene_table.shape[0] // INNER
    pos_n = position_table.shape[0] // INNER
    down_n = w_down_proj.shape[0] // INNER
    line_n = w_qkv.shape[0] // INNER
    prior, cot = prior_embed[0], cotangent[0]
    coord = jnp.stack([z.astype(i32), p.astype(i32), lengths[0], study_ids[0]])

    vectors = [
        v.reshape(1, -1)
        for v in (norm1_gain, norm1_shift, bias_query, bias_value,
                  bias_output, norm2_gain, norm2_shift, bias_down, bias_up)
    ]
    piece, small = prepare(
        coord, gene_ids, gene_table, position_table, w_qkv, w_up_proj, w_output, w_down_proj,
        expr_table, study_table, vectors,
    )
    got = [along(piece, k, F) for k in range(1, F)]
    gene_total = (F - 1) * gene_n

    def plan(j, first=0, count=gene_total):
        parts = []
        for k in range(F - 1):
            low, high = max(first, k * gene_n), min(first + count, (k + 1) * gene_n)
            if low < high:
                parts.append((k + 1, j, low - k * gene_n, high - low))
        return tuple(parts)

    def find(tables, plans):
        return lookup(coord, gene_ids, tables, tuple(plans), F, gene_n)

    found = [find([gene_table], [((0, None, 0, gene_table.shape[0]),)])]
    got = after(got, found[0])
    genes = piece[piece.shape[0] - 2 * n // gene_table.shape[1] :]
    stack = jnp.concatenate([g[gene_n:] for g in got] + [genes] + [g[:gene_n] for g in got])
    rest = stack.shape[0] - gene_total
    cut = stack.shape[0] // 32 * 16
    top, bottom = (0, cut - rest), (cut - rest, stack.shape[0] - cut)

    def look(step, arrays):
        if step == 0:
            found.append(find(arrays[:1], [plan(0)]))
        else:
            found.append(find(arrays[:3], [plan(1), plan(2), plan(4)]))
        return found[-1]

    pieces = spread(stack, look)
    inputs, query, keys, values, pos, cat, down, expr, study, vec, up_vec, ids = embed(
        coord, gene_ids, expr_bins, prior, found,
        [position_table, w_qkv, w_up_proj, w_output, w_down_proj, expr_table, study_table, small],
        [pieces[0], pieces[1], pieces[2], pieces[4], pieces[3], pieces[5], *pieces[6:]],
        (0, 1, 2, 4, 3, 5, 6, 8),
        (plan(3), plan(5), plan(6, *top), plan(6, *bottom), plan(7, *top), plan(7, *bottom)),
        F, gene_n, rest,
    )
    attended, wide, inverse, raised = attend(lengths, query, keys, values)
    hidden, mid, grad_attended, wg_feed, *grads = feed(
        coord, attended, inputs, cot, cat, down, vec, up_vec, F
    )
    back = (query, keys, values, wide, grad_attended, inverse, raised)
    wg_feed = fold_core(wg_feed, p)
    dqkv = attend_back(*back, 0, [])
    wg_feed, dqkv = lax.optimization_barrier((wg_feed, dqkv))
    wg_feed = fold_plane(wg_feed, p)
    dqkv = attend_back(*back, 1, dqkv)
    wg_feed, dqkv = lax.optimization_barrier((wg_feed, dqkv))
    grad, norm = inputs_back(coord, *dqkv, inputs, mid, cat, vec)

    cut = n // 2

    def add_rows(cells, arrays, old=(), start=0, extra=None):
        return scatter(coord, tuple(cells), ids, arrays, old, extra, F, gene_n, pos_n, start)

    near, other = swap(grad, 2), swap(grad, 4)
    wg = weights_back(
        coord, expr_bins, *dqkv, inputs, grad, norm, vec, grads, w_qkv.shape[1], expr.shape[0], F
    )
    first = add_rows([(0, 0, n)], [grad])
    wg = fold_plane(fold_core(wg, p), p)
    near, other, wg = after((near, other, wg), first)
    upper, lower = swap(near[:cut], 4), swap(other[cut:], 2)
    lines = jnp.concatenate([sum_low(wg_feed), sum_low(wg)], axis=1)
    second = add_rows([(2, 0, n), (4, 0, n)], [near, other])
    upper, lower = after((upper, lower), second)
    last = [(6, 0, cut), (6, cut, n - cut)]
    theirs = add_rows(last, [upper, lower], [first, second], 0)
    blocks = add_rows(last, [upper, lower], [first, second], F, lines)
    theirs = after(swap(theirs, 1), blocks)
    blocks = plus(blocks, jnp.pad(theirs, ((0, 0), (0, lines.shape[1]), (0, 0))))
    got = [along(blocks[k], k, F) for k in range(1, F)]
    own = count_rows(coord, after(ids, blocks), gene_table.shape[0])
    got = after(got, own)
    own = own.reshape(-1)
    if outer > 1:
        own = lax.psum(own, "outer")
    total = blocks[0].astype(f32)
    for g in got:
        total = total + g.astype(f32)
    if outer > 1:
        total = lax.psum(total, "outer")
    done = spread(total.astype(bf16))
    gene, pos, qkv, up, out, down, expr, study, *small = unpack(
        coord, done, F, gene_n, pos_n, line_n, down_n, w_up_proj.shape[1]
    )
    small = [s.reshape(-1) for s in small]
    return (
        hidden[None], gene, own, expr, study, pos, small[0], small[1], qkv, small[2], small[3],
        out, small[4], small[5], small[6], up, small[8], down, small[7],
    )


def solution(mesh):
    dp, F = mesh.devices.shape
    outer = dp // INNER
    mesh = Mesh(mesh.devices.reshape(outer, INNER, F), ("outer", "inner", "fsdp"))
    cells = ("outer", "inner", "fsdp")
    row, line = P("fsdp", None), P("fsdp")
    tables = (row,) * 4 + (line,) * 2 + (row, line, line, row, line, line, line, row, line, row, line)
    return jax.shard_map(
        functools.partial(body, outer, F),
        mesh=mesh,
        in_specs=(P(cells, None), P(cells, None), P(cells), P(cells), P(cells, None, None), P(cells, None, None))
        + tables,
        out_specs=(P(cells, None, None), row, line) + tables[1:],
        check_vma=False,
    )
```

```python
import functools

import jax
import jax.numpy as jnp
from jax import lax
from jax.experimental import pallas as pl
from jax.experimental.pallas import tpu as pltpu
from jax.sharding import Mesh
from jax.sharding import PartitionSpec as P

HEADS = 4
INNER = 8
MISC = 16
epsilon = 1e-05
LOG2E = 1.4426950408889634
bf16 = jnp.bfloat16
f32 = jnp.float32
i32 = jnp.int32


def params():
    return pltpu.CompilerParams(vmem_limit_bytes=56 << 20)


def cost(us):
    return pl.CostEstimate(flops=int(us * 5e7), bytes_accessed=0, transcendentals=0)


def dg(left, right, a, b):
    return lax.dot_general(left, right, (((a,), (b,)), ((), ())), preferred_element_type=f32)


def smem():
    return pl.BlockSpec(memory_space=pltpu.SMEM)


def whole(*shape):
    return pl.BlockSpec(shape, lambda *_: (0,) * len(shape))


def rows(size, width):
    return pl.BlockSpec((size, width), lambda i, *_: (i, 0))


def lanes(size):
    return pl.BlockSpec((1, size), lambda i, *_: (0, i))


def aligned(index, step):
    return pl.multiple_of(index, step)


def onehot(ids, base, count):
    number = lax.broadcasted_iota(i32, (count, ids.shape[1]), 0)
    return jnp.where(number == ids - base, 1.0, 0.0).astype(bf16)


def source(coord_ref, k, j, F):
    z = lax.rem(coord_ref[0] + F - k, F)
    return z * INNER + lax.bitwise_xor(coord_ref[1], j)


def lookup_kernel(plan, F, gene_n, coord_ref, ids_ref, *refs):
    total = find_rows(plan, F, gene_n, coord_ref, ids_ref[...], refs[:-1])
    refs[-1][...] = total.astype(bf16)


def lookup(coord, ids, tables, plan, F, gene_n, block=512):
    n, width = ids.shape[1], tables[0].shape[1]
    used = sum(part[3] for parts in plan for part in parts)
    return pl.pallas_call(
        functools.partial(lookup_kernel, plan, F, gene_n),
        grid=(n // block,),
        in_specs=[smem(), lanes(block)] + [whole(*t.shape) for t in tables],
        out_specs=rows(block, width),
        out_shape=jax.ShapeDtypeStruct((n, width), bf16),
        compiler_params=params(),
        cost_estimate=cost(2.1 + n * used * 6.5e-7),
        name="lookup",
    )(coord, ids, *tables)


def count_kernel(size, coord_ref, ids_ref, out_ref):
    high_n = out_ref.shape[0]
    lines = -(-high_n // 16) * 16
    total = None
    for i in range(size):
        ids = ids_ref[i : i + 1, :]
        left = onehot(lax.shift_right_logical(ids, 7), coord_ref[0] * high_n, lines)
        right = onehot(lax.bitwise_and(ids, 127), 0, 128)
        term = dg(left, right, 1, 1)
        total = term if total is None else total + term
    add_to(out_ref, total[0:high_n, :].astype(i32))


def count_rows(coord, ids, own, size=8):
    cells, n = ids.shape
    return pl.pallas_call(
        functools.partial(count_kernel, size),
        grid=(cells // size,),
        in_specs=[smem(), rows(size, n)],
        out_specs=whole(own // 128, 128),
        out_shape=jax.ShapeDtypeStruct((own // 128, 128), i32),
        compiler_params=params(),
        cost_estimate=cost(1.15e-4 * cells * n),
        name="count_rows",
    )(coord, ids)


def add_to(ref, value):
    @pl.when(pl.program_id(0) == 0)
    def _():
        ref[...] = value

    @pl.when(pl.program_id(0) != 0)
    def _():
        ref[...] += value


def prepare_kernel(
    coord_ref, ids_ref, gene, pos, qkv, up, out, down, expr, study, *refs
):
    vectors, piece_ref, small_ref = refs[:9], refs[9], refs[10]
    p = coord_ref[1]
    width = gene.shape[1]
    sub = vectors[0].shape[1]
    per = width // sub
    lines = [
        jnp.concatenate([vectors[per * r + i][...] for i in range(per)], axis=1)
        for r in range(8 // per)
    ]
    last = vectors[8][...]
    lines.append(jnp.concatenate([last, jnp.zeros((1, width - last.shape[1]), bf16)], axis=1))
    small_ref[...] = jnp.concatenate(
        lines + [jnp.zeros((MISC - len(lines), width), bf16)], axis=0
    )
    at = 0
    for ref in (gene, pos):
        piece_ref[at : at + ref.shape[0], :] = ref[...]
        at += ref.shape[0]
    even = lax.bitwise_and(p, 1) == 0
    odd = [up[:, t * width : (t + 1) * width] for t in range(up.shape[1] // width)] + [out[...]]
    for t in range(qkv.shape[1] // width):
        piece_ref[at : at + qkv.shape[0], :] = jnp.where(
            even, qkv[:, t * width : (t + 1) * width], odd[t]
        )
        at += qkv.shape[0]
    piece_ref[at : at + down.shape[0], :] = down[...]
    at += down.shape[0]
    misc = jnp.where(p == 0, expr[...], jnp.where(p == 1, study[...], small_ref[...]))
    piece_ref[at : at + MISC, :] = jnp.where(p < 3, misc, jnp.zeros_like(misc))
    at += MISC
    n = ids_ref.shape[1]
    slot = lax.broadcasted_iota(i32, (1, n), 1)
    ids = jnp.where(slot < coord_ref[2], ids_ref[...], 255 * 128)
    for part in (lax.shift_right_logical(ids, 7), lax.bitwise_and(ids, 127)):
        part = part.astype(f32)
        lines = [part[:, t * width : (t + 1) * width] for t in range(n // width)]
        piece_ref[at : at + n // width, :] = jnp.concatenate(lines, axis=0).astype(bf16)
        at += n // width


def prepare(coord, ids, gene, pos, qkv, up, out, down, expr, study, vectors):
    width = gene.shape[1]
    eighth = [(a.shape[0] // INNER, a.shape[1]) for a in (gene, pos, down)]
    fourth = [(a.shape[0] // (INNER // 2), a.shape[1]) for a in (qkv, up, out)]
    mine = [pl.BlockSpec(s, lambda i, c: (c[1], 0)) for s in eighth]
    pair = [pl.BlockSpec(s, lambda i, c: (lax.shift_right_logical(c[1], 1), 0)) for s in fourth]
    total = sum(s[0] for s in eighth) + fourth[0][0] * fourth[0][1] // width + MISC
    total += 2 * ids.shape[1] // width
    return pl.pallas_call(
        prepare_kernel,
        grid_spec=pltpu.PrefetchScalarGridSpec(
            num_scalar_prefetch=1,
            grid=(1,),
            in_specs=[whole(*ids.shape)] + mine[0:2] + pair + mine[2:]
            + [whole(*a.shape) for a in (expr, study, *vectors)],
            out_specs=[whole(total, width), whole(MISC, width)],
        ),
        out_shape=[
            jax.ShapeDtypeStruct((total, width), bf16),
            jax.ShapeDtypeStruct((MISC, width), bf16),
        ],
        compiler_params=params(),
        cost_estimate=cost(2.5),
        name="prepare",
    )(coord, ids, gene, pos, qkv, up, out, down, expr, study, *vectors)


def assemble(F, n, coord_ref, local, pieces, outs, misc):
    pos_loc, qkv_loc, up_loc, out_loc, down_loc, *misc_loc = local
    pos, cat, down, expr, study, vec, up_vec, ids = outs
    z, p = coord_ref[0], coord_ref[1]
    width = pos.shape[1]
    pos_n, cat_n = pos_loc.shape[0] // INNER, qkv_loc.shape[0] // (INNER // 2)
    down_n = down_loc.shape[0] // INNER
    half = cat.shape[2]
    parts = half // width
    rows_z = cat_n * (INNER // 2)
    lines = n // width
    rest_n = pos_n + cat_n * parts + down_n + MISC + 2 * lines

    def genes(row, ref, at):
        high, low = ref[at : at + lines, :], ref[at + lines : at + 2 * lines, :]
        number = (high.astype(f32) * 128.0 + low.astype(f32)).astype(i32)
        for t in range(lines):
            ids[row : row + 1, t * width : (t + 1) * width] = number[t : t + 1, :]

    pos[pl.ds(aligned(z * pos_n * INNER, 16), pos_n * INNER), :] = pos_loc[...]
    down[pl.ds(aligned(z * down_n * INNER, 16), down_n * INNER), :] = down_loc[...]
    span = pl.ds(aligned(z * rows_z, 16), rows_z)
    cat[0, span, :] = qkv_loc[...]
    cat[1, span, 0 : half - width] = up_loc[...]
    cat[1, span, half - width :] = out_loc[...]
    for t in range(3):
        misc[z * INNER + t] = misc_loc[t][...]
    for j in range(INNER):
        pj = lax.bitwise_xor(p, j)
        ref = pieces[j]
        for k in range(1, F):
            zk = lax.rem(z + F - k, F)
            at = rest_n * (k - 1)
            pos[pl.ds(aligned((zk * INNER + pj) * pos_n, 16), pos_n), :] = ref[at : at + pos_n, :]
            at += pos_n
            row = aligned(zk * rows_z + lax.shift_right_logical(pj, 1) * cat_n, 16)
            side = lax.bitwise_and(pj, 1)
            for s in range(parts):
                cat[side, pl.ds(row, cat_n), s * width : (s + 1) * width] = ref[at : at + cat_n, :]
                at += cat_n
            down[pl.ds(aligned((zk * INNER + pj) * down_n, 16), down_n), :] = ref[at : at + down_n, :]
            at += down_n
            misc[zk * INNER + pj] = ref[at : at + MISC, :]
            genes(k * INNER + j, ref, at + MISC)
        genes(j, ref, rest_n * (F - 1))
    sub = width // F
    for zz in range(F):
        expr[MISC * zz : MISC * zz + MISC, :] = misc[zz * INNER]
        study[MISC * zz : MISC * zz + MISC, :] = misc[zz * INNER + 1]
    small = [misc[zz * INNER + 2].astype(f32) for zz in range(F)]
    for i in range(8):
        r, c = i // F, sub * (i % F)
        vec[i : i + 1, :] = jnp.concatenate([s[r : r + 1, c : c + sub] for s in small], axis=1)
    r = 8 // F
    up_vec[...] = jnp.concatenate(
        [s[r : r + 1, 0 : up_vec.shape[1] // F] for s in small], axis=1
    )


def standard(values):
    average = jnp.mean(values, axis=1, keepdims=True)
    centered = values - average
    scale = lax.rsqrt(jnp.mean(centered * centered, axis=1, keepdims=True) + epsilon)
    return centered * scale, scale


def slot_mask(len_ref, size):
    slot = pl.program_id(0) * size + lax.broadcasted_iota(i32, (size, 1), 0)
    return (slot < len_ref[2]).astype(f32)


def find_rows(plan, F, gene_n, coord_ref, ids, tables):
    total = None
    for table, parts in zip(tables, plan):
        hits = [
            onehot(ids, source(coord_ref, k, j, F) * gene_n + off, count)
            if j is not None
            else onehot(ids, coord_ref[0] * gene_n * INNER, count)
            for k, j, off, count in parts
        ]
        hits = hits[0] if len(hits) == 1 else jnp.concatenate(hits, axis=0)
        term = dg(hits, table[table.shape[0] - hits.shape[0] :, :], 0, 0)
        total = term if total is None else total + term
    return total


def embed_kernel(F, n, gene_n, plan, use, sizes, coord_ref, ids_ref, bins_ref, prior, *refs):
    size, found_n, local_n, piece_n = sizes
    found, refs = refs[:found_n], refs[found_n:]
    local, refs = refs[:local_n], refs[local_n:]
    pieces, refs = refs[:piece_n], refs[piece_n:]
    inputs_ref, q_ref, k_ref, v_ref = refs[0:4]
    pos, cat, down, expr, study, vec, up_vec, ids_all, misc = refs[4:]
    width = prior.shape[1]

    @pl.when(pl.program_id(0) == 0)
    def _():
        assemble(F, n, coord_ref, local, [pieces[t] for t in use], refs[4:-1], misc)

    total = find_rows(plan, F, gene_n, coord_ref, ids_ref[...], pieces[piece_n - len(plan) :])
    total = total + dg(onehot(bins_ref[...], 0, expr.shape[0]), expr[...], 0, 0)
    for ref in found:
        total = total + ref[...].astype(f32)
    here = (lax.broadcasted_iota(i32, (8, study.shape[0]), 1) == coord_ref[3]).astype(bf16)
    total = total + dg(here, study[...], 1, 0)[0:1, :]
    slots = pl.ds(aligned(pl.program_id(0) * size, size), size)
    total = total + pos[slots, :].astype(f32) + prior[...].astype(f32)
    total = total * slot_mask(coord_ref, size)
    inputs_ref[...] = total
    normed, _ = standard(total)
    normed = (normed * vec[0:1, :] + vec[1:2, :]).astype(bf16)
    mixed = dg(normed, cat[0], 1, 0)
    q_ref[...] = (mixed[:, 0:width] + vec[2:3, :]).astype(bf16)
    k_ref[...] = mixed[:, width : 2 * width].astype(bf16)
    v_ref[...] = (mixed[:, 2 * width :] + vec[3:4, :]).astype(bf16)


def embed(coord, ids, bins, prior, found, local, pieces, use, plan, F, gene_n, rest, size=1024):
    n, width = prior.shape
    pos, qkv, up, out, down, *_ = local
    block = rows(size, width)
    outs = [
        ((F * pos.shape[0], width), bf16),
        ((2, F * qkv.shape[0], qkv.shape[1]), bf16),
        ((F * down.shape[0], width), bf16),
        ((F * MISC, width), bf16),
        ((F * MISC, width), bf16),
        ((8, width), f32),
        ((1, up.shape[1]), f32),
        ((F * INNER, n), i32),
    ]
    short = len(pieces) - len(plan)
    kernel = functools.partial(
        embed_kernel, F, n, gene_n, plan, use, (size, len(found), len(local), len(pieces))
    )
    return pl.pallas_call(
        kernel,
        grid=(n // size,),
        in_specs=[smem(), lanes(size), lanes(size)]
        + [block] * (1 + len(found))
        + [whole(*a.shape) for a in local]
        + [whole(rest, width)] * short
        + [whole(*a.shape) for a in pieces[short:]],
        out_specs=[block] * 4 + [whole(*s) for s, _ in outs],
        out_shape=[jax.ShapeDtypeStruct((n, width), f32)]
        + [jax.ShapeDtypeStruct((n, width), bf16)] * 3
        + [jax.ShapeDtypeStruct(*s) for s in outs],
        scratch_shapes=[pltpu.VMEM((F * INNER, MISC, width), bf16)],
        compiler_params=params(),
        cost_estimate=cost(15.5),
        name="embed",
    )(coord, ids, bins, prior, *found, *local, *pieces)


def extend(pair, half, spare):
    size = pair.shape[1] // 2
    lane = lax.broadcasted_iota(i32, pair.shape, 1)
    base = size * (1 - half)
    out = jnp.where((lane >= size * half) & (lane < size * half + size), pair, jnp.zeros_like(pair))
    for t, value in enumerate(spare):
        out = jnp.where(lane == base + t, jnp.broadcast_to(value, pair.shape), out)
    return out


def one():
    return jnp.ones((1, 1), bf16)


def split3(value):
    high = value.astype(bf16)
    rest = value - high.astype(f32)
    middle = rest.astype(bf16)
    return high, middle, (rest - middle.astype(f32)).astype(bf16)


def attend_kernel(len_ref, q_ref, k_ref, v_ref, o_ref, wide_ref, inv_ref, e_ref, kx, vx):
    n, pair = k_ref.shape
    size = pair // 2
    factor = size ** (-0.5) * LOG2E

    @pl.when(pl.program_id(1) == 0)
    def _():
        slot = lax.broadcasted_iota(i32, (n, 1), 0)
        bias = jnp.where(slot < len_ref[0], 0.0, -1e9).astype(bf16)
        lane = lax.broadcasted_iota(i32, (n, pair), 1)
        for h in range(2):
            kx[h] = extend(k_ref[...], h, [bias])
            own = (lane >= size * h) & (lane < size * h + size)
            vx[h] = jnp.where(own, v_ref[...], jnp.ones_like(v_ref[...]))

    scores = [dg(extend(q_ref[...], h, [one()]), kx[h], 1, 1) for h in range(2)]
    peaks = [jnp.max(s, axis=1, keepdims=True) for s in scores]
    raised = [jnp.exp2((s - p) * factor).astype(bf16) for s, p in zip(scores, peaks)]
    outs, totals = [], []
    for h in range(2):
        e_ref[h] = raised[h]
        out = dg(raised[h], vx[h], 1, 0)
        outs.append(out)
        totals.append(jnp.concatenate([out[:, size:], out[:, :size]], axis=1))
    low = lax.broadcasted_iota(i32, outs[0].shape, 1) < size
    inverse = 1.0 / jnp.where(low, totals[0], totals[1])
    out = jnp.where(low, outs[0], outs[1]) * inverse
    inv_ref[...] = inverse
    wide_ref[...] = out
    o_ref[...] = out.astype(bf16)


def attend(length, q, k, v, size=512):
    n, width = q.shape
    two = 2 * width // HEADS
    block = pl.BlockSpec((size, two), lambda j, i: (i, j))
    full = pl.BlockSpec((n, two), lambda j, i: (0, j))
    return pl.pallas_call(
        attend_kernel,
        grid=(HEADS // 2, n // size),
        in_specs=[smem(), block, full, full],
        out_specs=[block] * 3 + [pl.BlockSpec((2, size, n), lambda j, i: (j, i, 0))],
        out_shape=[
            jax.ShapeDtypeStruct((n, width), bf16),
            jax.ShapeDtypeStruct((n, width), f32),
            jax.ShapeDtypeStruct((n, width), f32),
            jax.ShapeDtypeStruct((HEADS, n, n), bf16),
        ],
        scratch_shapes=[pltpu.VMEM((2, n, two), bf16)] * 2,
        compiler_params=params(),
        cost_estimate=cost(32),
        name="attend",
    )(length, q, k, v)


def attend_back_kernel(
    q_ref, k_ref, v_ref, o_ref, do_ref, inv_ref, e_ref, dq_ref, dk_ref, dv_ref, vx, dkt, dvt
):
    n, pair = k_ref.shape
    size = pair // 2
    scale = size ** (-0.5)

    @pl.when(pl.program_id(1) == 0)
    def _():
        for h in range(2):
            vx[h] = extend(v_ref[...], h, [one(), one(), one()])
        dkt[...] = jnp.zeros_like(dkt)
        dvt[...] = jnp.zeros_like(dvt)

    grad = (do_ref[...].astype(f32) * inv_ref[...]).astype(bf16)
    product = grad.astype(f32) * o_ref[...]
    qt = q_ref[...].T
    gt = grad.T
    grads = []
    for h in range(2):
        span = slice(size * h, size * h + size)
        inner = jnp.sum(product[:, span], axis=1, keepdims=True)
        raised = e_ref[h]
        back = dg(extend(grad, h, [*split3(-inner)]), vx[h], 1, 1)
        grad_scores = (raised.astype(f32) * back).astype(bf16)
        dvt[span, :] += dg(gt[span, :], raised, 1, 0)
        dkt[span, :] += dg(qt[span, :], grad_scores, 1, 0)
        grads.append(dg(grad_scores, k_ref[...], 1, 0))
    low = lax.broadcasted_iota(i32, grads[0].shape, 1) < size
    dq_ref[...] = (jnp.where(low, grads[0], grads[1]) * scale).astype(bf16)

    @pl.when(pl.program_id(1) == pl.num_programs(1) - 1)
    def _():
        dk_ref[...] = (dkt[...] * scale).T.astype(bf16)
        dv_ref[...] = dvt[...].T.astype(bf16)


def attend_back(q, k, v, o, do, inverse, raised, size=256):
    n, width = q.shape
    two = 2 * width // HEADS
    block = pl.BlockSpec((size, two), lambda j, i: (i, j))
    full = pl.BlockSpec((n, two), lambda j, i: (0, j))
    return pl.pallas_call(
        attend_back_kernel,
        grid=(HEADS // 2, n // size),
        in_specs=[block, full, full, block, block, block]
        + [pl.BlockSpec((2, size, n), lambda j, i: (j, i, 0))],
        out_specs=[block, full, full],
        out_shape=[jax.ShapeDtypeStruct((n, width), bf16)] * 3,
        scratch_shapes=[pltpu.VMEM((2, n, two), bf16)] + [pltpu.VMEM((two, n), f32)] * 2,
        compiler_params=params(),
        cost_estimate=cost(40),
        name="attend_back",
    )(q, k, v, o, do, inverse, raised)


def feed_kernel(
    size, len_ref, att_ref, in_ref, cot_ref, cat, down, vec, up_vec,
    hidden_ref, mid_ref, datt_ref, wg_ref, g_vec, g_up_vec, g_down, g_up, g_out,
):
    width = att_ref.shape[1]
    up_width = down.shape[0]
    w_up, w_out = cat[1, :, 0:up_width], cat[1, :, up_width:]
    mask = slot_mask(len_ref, size)
    att = att_ref[...]
    middle = in_ref[...] + dg(att, w_out, 1, 0) + vec[4:5, :]
    normed, scale = standard(middle)
    low = (normed * vec[5:6, :] + vec[6:7, :]).astype(bf16)
    upward = dg(low, w_up, 1, 0) + up_vec[...]
    share = 0.5 * (1.0 + lax.erf(upward * (0.5**0.5)))
    active = (upward * share).astype(bf16)
    result = middle + dg(active, down[...], 1, 0) + vec[7:8, :]
    hidden_ref[...] = (result * mask).astype(bf16)
    grad_low = (cot_ref[...].astype(f32) * mask).astype(bf16)
    grad = grad_low.astype(f32)
    bell = jnp.exp(upward * upward * -0.5) * 0.3989422804014327
    grad_up = ((share + upward * bell) * dg(grad_low, down[...], 1, 1)).astype(bf16)
    grad_norm = dg(grad_up, w_up, 1, 1)
    scaled = grad_norm * vec[5:6, :]
    back = scaled - jnp.mean(scaled, axis=1, keepdims=True)
    back = back - normed * jnp.mean(scaled * normed, axis=1, keepdims=True)
    grad_mid = grad + scale * back
    branch = grad_mid.astype(bf16)
    mid_ref[...] = grad_mid
    datt_ref[...] = dg(branch, w_out, 1, 1).astype(bf16)
    add_to(g_down, dg(active, grad_low, 0, 0))
    add_to(g_up, dg(low, grad_up, 0, 0))
    add_to(g_out, dg(att, branch, 0, 0))
    sums = [
        jnp.sum(t, axis=0, keepdims=True)
        for t in (branch.astype(f32), grad_norm * normed, grad_norm, grad)
    ]
    add_to(g_vec, jnp.concatenate(sums + sums, axis=0))
    add_to(g_up_vec, jnp.sum(grad_up.astype(f32), axis=0, keepdims=True))

    @pl.when(pl.program_id(0) == pl.num_programs(0) - 1)
    def _():
        F = wg_ref.shape[3]
        line_n, down_n = width // F // INNER, up_width // F // INNER
        for z in range(F):
            for p in range(INNER):
                at = line_n * (INNER * z + p)
                blocks = [
                    g_up[at : at + line_n, t * width : (t + 1) * width]
                    for t in range(up_width // width)
                ]
                blocks.append(g_out[at : at + line_n, :])
                at = down_n * (INNER * z + p)
                blocks.append(g_down[at : at + down_n, :])
                at = 0
                for b in blocks:
                    wg_ref[p % 2, p // 2 % 2, p // 4, z, at : at + b.shape[0], :] = b.astype(bf16)
                    at += b.shape[0]


def feed(coord, att, inputs, cot, cat, down, vec, up_vec, F, size=1024):
    n, width = att.shape
    up_width = down.shape[0]
    block = rows(size, width)
    w_rows = (width * (up_width + width) // width + up_width) // F // INNER
    shapes = [(2, 2, 2, F, w_rows, width), (8, width), (1, up_width)]
    return pl.pallas_call(
        functools.partial(feed_kernel, size),
        grid=(n // size,),
        in_specs=[smem(), block, block, block]
        + [whole(*a.shape) for a in (cat, down, vec, up_vec)],
        out_specs=[block] * 3 + [whole(*s) for s in shapes],
        out_shape=[
            jax.ShapeDtypeStruct((n, width), bf16),
            jax.ShapeDtypeStruct((n, width), f32),
            jax.ShapeDtypeStruct((n, width), bf16),
        ]
        + [jax.ShapeDtypeStruct(shapes[0], bf16)]
        + [jax.ShapeDtypeStruct(s, f32) for s in shapes[1:]],
        scratch_shapes=[
            pltpu.VMEM((up_width, width), f32),
            pltpu.VMEM((width, up_width), f32),
            pltpu.VMEM((width, width), f32),
        ],
        compiler_params=params(),
        cost_estimate=cost(20),
        name="feed",
    )(coord, att, inputs, cot, cat, down, vec, up_vec)


def inputs_back_kernel(size, coord_ref, dq_ref, dk_ref, dv_ref, in_ref, mid_ref, cat, vec, out_ref, norm_ref):
    width = dq_ref.shape[1]
    normed, scale = standard(in_ref[...])
    grad_norm = None
    for t, part in enumerate((dq_ref, dk_ref, dv_ref)):
        term = dg(part[...], cat[0, :, t * width : (t + 1) * width], 1, 1)
        grad_norm = term if grad_norm is None else grad_norm + term
    scaled = grad_norm * vec[0:1, :]
    back = scaled - jnp.mean(scaled, axis=1, keepdims=True)
    back = back - normed * jnp.mean(scaled * normed, axis=1, keepdims=True)
    out_ref[...] = ((mid_ref[...] + scale * back) * slot_mask(coord_ref, size)).astype(bf16)
    norm_ref[...] = grad_norm


def inputs_back(coord, dq, dk, dv, inputs, mid, cat, vec, size=1024):
    n, width = dq.shape
    block = rows(size, width)
    return pl.pallas_call(
        functools.partial(inputs_back_kernel, size),
        grid=(n // size,),
        in_specs=[smem()] + [block] * 5
        + [pl.BlockSpec((1, *cat.shape[1:]), lambda i: (0, 0, 0)), whole(*vec.shape)],
        out_specs=[block] * 2,
        out_shape=[jax.ShapeDtypeStruct((n, width), t) for t in (bf16, f32)],
        compiler_params=params(),
        cost_estimate=cost(6.4),
        name="inputs_back",
    )(coord, dq, dk, dv, inputs, mid, cat, vec)


def weights_back_kernel(
    size, F, scalar_ref, bins_ref, dq_ref, dk_ref, dv_ref, in_ref, grad_ref, norm_ref, vec,
    g_vec2, g_up_vec, wg_ref, g_qkv, g_vec, g_expr,
):
    width = dq_ref.shape[1]
    normed, _ = standard(in_ref[...])
    low = (normed * vec[0:1, :] + vec[1:2, :]).astype(bf16)
    for t, part in enumerate((dq_ref, dk_ref, dv_ref)):
        add_to(g_qkv.at[:, t * width : (t + 1) * width], dg(low, part[...], 0, 0))
    grad_norm, grad = norm_ref[...], grad_ref[...]
    sums = [
        jnp.sum(t, axis=0, keepdims=True)
        for t in (
            grad_norm * normed,
            grad_norm,
            dq_ref[...].astype(f32),
            dv_ref[...].astype(f32),
            grad.astype(f32),
        )
    ]
    add_to(g_vec, jnp.concatenate(sums + sums[0:3], axis=0))
    add_to(g_expr, dg(onehot(bins_ref[...], 0, g_expr.shape[0]), grad, 1, 0))

    @pl.when(pl.program_id(0) == pl.num_programs(0) - 1)
    def _():
        line_n = width // F // INNER
        sub = width // F
        up_sub = g_up_vec.shape[1] // F
        groups = g_expr.shape[0]
        here = lax.broadcasted_iota(i32, (groups, width), 0) == scalar_ref[3]
        g_study = jnp.where(here, jnp.broadcast_to(g_vec[4:5, :], (groups, width)), 0.0)
        vectors = [g_vec[i : i + 1, :] for i in range(4)] + [g_vec2[i : i + 1, :] for i in range(4)]
        for z in range(F):
            small = []
            for r in range(8 // F):
                small.append(
                    jnp.concatenate(
                        [vectors[r * F + i][:, z * sub : (z + 1) * sub] for i in range(F)], axis=1
                    )
                )
            up_row = g_up_vec[:, z * up_sub : (z + 1) * up_sub]
            small.append(jnp.concatenate([up_row, jnp.zeros((1, width - up_sub), f32)], axis=1))
            small.append(jnp.zeros((8 - len(small), width), f32))
            at = MISC * z
            misc = [
                g_expr[at : at + 8, :],
                g_expr[at + 8 : at + 16, :],
                g_study[at : at + 8, :],
                g_study[at + 8 : at + 16, :],
                jnp.concatenate(small, axis=0),
            ]
            for p in range(INNER):
                at = line_n * (INNER * z + p)
                blocks = [
                    g_qkv[at : at + line_n, t * width : (t + 1) * width] for t in range(3)
                ] + [misc[p] if p < 5 else jnp.zeros((8, width), f32)]
                wg_ref[p % 2, p // 2 % 2, p // 4, z] = jnp.concatenate(blocks, axis=0).astype(bf16)


def weights_back(coord, bins, dq, dk, dv, inputs, grad, norm, vec, grads, half, bins_total, F, size=512):
    n, width = dq.shape
    block = rows(size, width)
    shape = (2, 2, 2, F, half // F // INNER + 8, width)
    return pl.pallas_call(
        functools.partial(weights_back_kernel, size, F),
        grid=(n // size,),
        in_specs=[smem(), lanes(size)] + [block] * 6 + [whole(*a.shape) for a in (vec, *grads)],
        out_specs=whole(*shape),
        out_shape=jax.ShapeDtypeStruct(shape, bf16),
        scratch_shapes=[
            pltpu.VMEM((width, half), f32),
            pltpu.VMEM((8, width), f32),
            pltpu.VMEM((bins_total, width), f32),
        ],
        compiler_params=params(),
        cost_estimate=cost(9),
        name="weights_back",
    )(coord, bins, dq, dk, dv, inputs, grad, norm, vec, *grads)


def scatter_kernel(cells, F, gene_n, pos_n, start_at, extra, coord_ref, *refs):
    ids, refs = refs[0], refs[1:]
    grads, refs = refs[: len(cells)], refs[len(cells) :]
    lines, old, out_ref = refs[:extra], refs[extra:-1], refs[-1]
    number = pl.program_id(0) + start_at
    z = lax.rem(coord_ref[0] + number, F)
    other = (number < F).astype(i32)
    place = z * INNER + lax.bitwise_xor(coord_ref[1], other)
    total = None
    for (cell, start, size), ref in zip(cells, grads):
        hits = onehot(ids[cell : cell + 1, start : start + size], place * gene_n, gene_n)
        term = dg(hits, ref[0:size, :], 1, 0)
        total = term if total is None else total + term
    line = None
    for (cell, start, size), ref in zip(cells, grads):
        inside = (place * pos_n >= start) & (place * pos_n < start + size)
        at = aligned(jnp.where(inside, place * pos_n - start, 0), 16)
        term = jnp.where(inside, ref[pl.ds(at, pos_n), :].astype(f32), 0.0)
        line = term if line is None else line + term
    for ref in old:
        total = total + ref[0, 0:gene_n, :]
        line = line + ref[0, gene_n : gene_n + pos_n, :]

    out_ref[0, 0:gene_n, :] = total.astype(out_ref.dtype)
    out_ref[0, gene_n : gene_n + pos_n, :] = line.astype(out_ref.dtype)
    for ref in lines:
        out_ref[0, gene_n + pos_n :, :] = ref[z]


def scatter(coord, cells, ids, grads, old, extra, F, gene_n, pos_n, start):
    width = grads[0].shape[1]
    size = gene_n + pos_n
    count = F if old else 2 * F
    more = [] if extra is None else [extra]
    full = size + sum(e.shape[1] for e in more)
    return pl.pallas_call(
        functools.partial(scatter_kernel, cells, F, gene_n, pos_n, start, len(more)),
        grid=(count,),
        in_specs=[smem(), whole(INNER, ids.shape[1])]
        + [whole(*g.shape) for g in grads]
        + [whole(*e.shape) for e in more]
        + [pl.BlockSpec((1, size, width), lambda i: (i + start, 0, 0))] * len(old),
        out_specs=pl.BlockSpec((1, full, width), lambda i: (i, 0, 0)),
        out_shape=jax.ShapeDtypeStruct((count, full, width), bf16 if old else f32),
        compiler_params=params(),
        cost_estimate=cost(2.5 + count * sum(c[2] for c in cells) * 2.5e-4),
        name="scatter",
    )(coord, ids, *grads, *more, *old)


def unpack_kernel(F, gene_n, pos_n, line_n, down_n, coord_ref, *refs):
    pieces, refs = refs[: INNER + 2], refs[INNER + 2 :]
    gene, pos, qkv, up, out, down, expr, study = refs[:8]
    vectors, misc = refs[8:17], refs[17]
    p = coord_ref[1]
    width = gene.shape[1]
    for j in range(INNER):
        pj = lax.bitwise_xor(p, j)
        if j < 6:
            here = [(pieces[j], 0)]
        else:
            top, bottom = pieces[6 + 2 * (j - 6)], pieces[7 + 2 * (j - 6)]
            here = [(top, 0), (bottom, top.shape[0])]
        for ref, first in here:
            count = min(ref.shape[0], gene_n - first)
            gene[pl.ds(aligned(gene_n * pj + first, 16), count), :] = ref[0:count, :].astype(f32)
        ref, first = here[-1]
        at = gene_n - first
        tail = ref[at : at + pos_n, :].astype(f32)
        pos[pl.ds(aligned(pos_n * pj, 16), pos_n), :] = tail
        at += pos_n
        tail = ref[at:, :].astype(f32)
        row = pl.ds(aligned(line_n * pj, 8), line_n)
        at = 0
        for s in range(up.shape[1] // width):
            up[row, s * width : (s + 1) * width] = tail[at : at + line_n, :]
            at += line_n
        out[row, :] = tail[at : at + line_n, :]
        at += line_n
        down[pl.ds(aligned(pj * down_n, 16), down_n), :] = tail[at : at + down_n, :]
        at += down_n
        for s in range(3):
            qkv[row, s * width : (s + 1) * width] = tail[at : at + line_n, :]
            at += line_n
        misc[pj] = tail[at : at + 8, :]
    for t in range(2):
        expr[8 * t : 8 * t + 8, :] = misc[t]
        study[8 * t : 8 * t + 8, :] = misc[2 + t]
    small = misc[4]
    sub = width // F
    for i in range(8):
        vectors[i][...] = small[i // F : i // F + 1, sub * (i % F) : sub * (i % F + 1)]
    vectors[8][...] = small[8 // F : 8 // F + 1, 0 : vectors[8].shape[1]]


def unpack(coord, pieces, F, gene_n, pos_n, line_n, down_n, up_width):
    width = pieces[0].shape[1]
    vmem = pl.BlockSpec(memory_space=pltpu.VMEM)
    shapes = [
        (gene_n * INNER, width),
        (pos_n * INNER, width),
        (line_n * INNER, 3 * width),
        (line_n * INNER, up_width),
        (line_n * INNER, width),
        (down_n * INNER, width),
        (MISC, width),
        (MISC, width),
    ]
    shapes += [(1, width // F)] * 8 + [(1, up_width // F)]
    return pl.pallas_call(
        functools.partial(unpack_kernel, F, gene_n, pos_n, line_n, down_n),
        in_specs=[smem()] + [vmem] * len(pieces),
        out_shape=[jax.ShapeDtypeStruct(s, f32) for s in shapes],
        scratch_shapes=[pltpu.VMEM((INNER, 8, width), f32)],
        compiler_params=params(),
        cost_estimate=cost(3.7),
        name="unpack",
    )(coord, *pieces)


def swap(array, bit):
    return lax.ppermute(array, "inner", [(i, i ^ bit) for i in range(INNER)])


def along(array, step, F):
    return lax.ppermute(array, "fsdp", [(i, (i + step) % F) for i in range(F)])


def after(arrays, work):
    return lax.optimization_barrier((arrays, work))[0]


def spread(piece, use=None):
    if use is None:
        use = lambda step, arrays: ()
    cut = piece.shape[0] // 32 * 16
    near, other, core = swap(piece, 2), swap(piece, 4), swap(piece, 1)
    near, other = after((near, other), use(0, [piece, core]))
    upper, lower = swap(near[:cut], 4), swap(other[cut:], 2)
    near1, other1 = swap(near, 1), swap(other, 1)
    upper, lower = after((upper, lower), use(1, [core, near, other, near1, other1]))
    upper1, lower1 = swap(upper, 1), swap(lower, 1)
    return [piece, core, near, near1, other, other1, upper, lower, upper1, lower1]


def plus(left, right):
    return (left.astype(f32) + right.astype(f32)).astype(bf16)


def pick(array, index, axis):
    return lax.dynamic_index_in_dim(array, index, axis, keepdims=False)


def fold_core(array, p):
    mine = lax.bitwise_and(p, 1)
    return plus(pick(array, mine, 0), swap(pick(array, 1 - mine, 0), 1))


def fold_plane(array, p):
    x, y = (lax.bitwise_and(lax.shift_right_logical(p, b), 1) for b in (1, 2))
    terms = []
    for bits in range(4):
        dx, dy = bits & 1, bits >> 1
        term = pick(pick(array, lax.bitwise_xor(x, dx), 0), lax.bitwise_xor(y, dy), 0)
        terms.append(swap(term, 2 * bits) if bits else term)
    return terms


def sum_low(terms):
    total = terms[0].astype(f32)
    for term in terms[1:]:
        total = total + term.astype(f32)
    return total.astype(bf16)


def body(
    outer, F,
    gene_ids, expr_bins, study_ids, lengths, prior_embed, cotangent,
    gene_table, expr_table, study_table, position_table,
    norm1_gain, norm1_shift, w_qkv, bias_query, bias_value, w_output, bias_output,
    norm2_gain, norm2_shift, w_up_proj, bias_up, w_down_proj, bias_down,
):
    n = gene_ids.shape[1]
    z, p = lax.axis_index("fsdp"), lax.axis_index("inner")
    gene_n = gene_table.shape[0] // INNER
    pos_n = position_table.shape[0] // INNER
    down_n = w_down_proj.shape[0] // INNER
    line_n = w_qkv.shape[0] // INNER
    prior, cot = prior_embed[0], cotangent[0]
    coord = jnp.stack([z.astype(i32), p.astype(i32), lengths[0], study_ids[0]])

    vectors = [
        v.reshape(1, -1)
        for v in (norm1_gain, norm1_shift, bias_query, bias_value,
                  bias_output, norm2_gain, norm2_shift, bias_down, bias_up)
    ]
    piece, small = prepare(
        coord, gene_ids, gene_table, position_table, w_qkv, w_up_proj, w_output, w_down_proj,
        expr_table, study_table, vectors,
    )
    got = [along(piece, k, F) for k in range(1, F)]
    gene_total = (F - 1) * gene_n

    def plan(j, first=0, count=gene_total):
        parts = []
        for k in range(F - 1):
            low, high = max(first, k * gene_n), min(first + count, (k + 1) * gene_n)
            if low < high:
                parts.append((k + 1, j, low - k * gene_n, high - low))
        return tuple(parts)

    def find(tables, plans):
        return lookup(coord, gene_ids, tables, tuple(plans), F, gene_n)

    found = [find([gene_table], [((0, None, 0, gene_table.shape[0]),)])]
    got = after(got, found[0])
    genes = piece[piece.shape[0] - 2 * n // gene_table.shape[1] :]
    stack = jnp.concatenate([g[gene_n:] for g in got] + [genes] + [g[:gene_n] for g in got])
    rest = stack.shape[0] - gene_total
    cut = stack.shape[0] // 32 * 16
    top, bottom = (0, cut - rest), (cut - rest, stack.shape[0] - cut)

    def look(step, arrays):
        if step == 0:
            found.append(find(arrays[:1], [plan(0)]))
        else:
            found.append(find(arrays[:3], [plan(1), plan(2), plan(4)]))
        return found[-1]

    pieces = spread(stack, look)
    inputs, query, keys, values, pos, cat, down, expr, study, vec, up_vec, ids = embed(
        coord, gene_ids, expr_bins, prior, found,
        [position_table, w_qkv, w_up_proj, w_output, w_down_proj, expr_table, study_table, small],
        [pieces[0], pieces[1], pieces[2], pieces[4], pieces[3], pieces[5], *pieces[6:]],
        (0, 1, 2, 4, 3, 5, 6, 8),
        (plan(3), plan(5), plan(6, *top), plan(6, *bottom), plan(7, *top), plan(7, *bottom)),
        F, gene_n, rest,
    )
    attended, wide, inverse, raised = attend(lengths, query, keys, values)
    hidden, mid, grad_attended, wg_feed, *grads = feed(
        coord, attended, inputs, cot, cat, down, vec, up_vec, F
    )
    wg_feed = fold_core(wg_feed, p)
    dqkv = attend_back(query, keys, values, wide, grad_attended, inverse, raised)
    wg_feed, dqkv = lax.optimization_barrier((wg_feed, dqkv))
    grad, norm = inputs_back(coord, *dqkv, inputs, mid, cat, vec)

    cut = n // 2

    def add_rows(cells, arrays, old=(), start=0, extra=None):
        return scatter(coord, tuple(cells), ids, arrays, old, extra, F, gene_n, pos_n, start)

    near, other = swap(grad, 2), swap(grad, 4)
    wg = weights_back(
        coord, expr_bins, *dqkv, inputs, grad, norm, vec, grads, w_qkv.shape[1], expr.shape[0], F
    )
    first = add_rows([(0, 0, n)], [grad])
    wg = fold_plane(jnp.concatenate([wg_feed, fold_core(wg, p)], axis=3), p)
    near, other, wg = after((near, other, wg), first)
    upper, lower = swap(near[:cut], 4), swap(other[cut:], 2)
    lines = sum_low(wg)
    second = add_rows([(2, 0, n), (4, 0, n)], [near, other])
    upper, lower = after((upper, lower), second)
    last = [(6, 0, cut), (6, cut, n - cut)]
    theirs = add_rows(last, [upper, lower], [first, second], 0)
    blocks = add_rows(last, [upper, lower], [first, second], F, lines)
    theirs = after(swap(theirs, 1), blocks)
    blocks = plus(blocks, jnp.pad(theirs, ((0, 0), (0, lines.shape[1]), (0, 0))))
    got = [along(blocks[k], k, F) for k in range(1, F)]
    own = count_rows(coord, after(ids, blocks), gene_table.shape[0])
    got = after(got, own)
    own = own.reshape(-1)
    if outer > 1:
        own = lax.psum(own, "outer")
    total = blocks[0].astype(f32)
    for g in got:
        total = total + g.astype(f32)
    if outer > 1:
        total = lax.psum(total, "outer")
    done = spread(total.astype(bf16))
    gene, pos, qkv, up, out, down, expr, study, *small = unpack(
        coord, done, F, gene_n, pos_n, line_n, down_n, w_up_proj.shape[1]
    )
    small = [s.reshape(-1) for s in small]
    return (
        hidden[None], gene, own, expr, study, pos, small[0], small[1], qkv, small[2], small[3],
        out, small[4], small[5], small[6], up, small[8], down, small[7],
    )


def solution(mesh):
    dp, F = mesh.devices.shape
    outer = dp // INNER
    mesh = Mesh(mesh.devices.reshape(outer, INNER, F), ("outer", "inner", "fsdp"))
    cells = ("outer", "inner", "fsdp")
    row, line = P("fsdp", None), P("fsdp")
    tables = (row,) * 4 + (line,) * 2 + (row, line, line, row, line, line, line, row, line, row, line)
    return jax.shard_map(
        functools.partial(body, outer, F),
        mesh=mesh,
        in_specs=(P(cells, None), P(cells, None), P(cells), P(cells), P(cells, None, None), P(cells, None, None))
        + tables,
        out_specs=(P(cells, None, None), row, line) + tables[1:],
        check_vma=False,
    )
```

```python
import functools

import jax
import jax.numpy as jnp
from jax import lax
from jax.experimental import pallas as pl
from jax.experimental.pallas import tpu as pltpu
from jax.sharding import Mesh
from jax.sharding import PartitionSpec as P

HEADS = 4
INNER = 8
GROUP = 2
GROUP_LAST = 2
MISC = 16
epsilon = 1e-05
LOG2E = 1.4426950408889634
bf16 = jnp.bfloat16
f32 = jnp.float32
i32 = jnp.int32


def params():
    return pltpu.CompilerParams(vmem_limit_bytes=56 << 20)


def cost(us):
    return pl.CostEstimate(flops=int(us * 5e7), bytes_accessed=0, transcendentals=0)


def dg(left, right, a, b):
    return lax.dot_general(left, right, (((a,), (b,)), ((), ())), preferred_element_type=f32)


def smem():
    return pl.BlockSpec(memory_space=pltpu.SMEM)


def whole(*shape):
    return pl.BlockSpec(shape, lambda *_: (0,) * len(shape))


def rows(size, width):
    return pl.BlockSpec((size, width), lambda i, *_: (i, 0))


def lanes(size):
    return pl.BlockSpec((1, size), lambda i, *_: (0, i))


def aligned(index, step):
    return pl.multiple_of(index, step)


def onehot(ids, base, count):
    number = lax.broadcasted_iota(i32, (count, ids.shape[1]), 0)
    return jnp.where(number == ids - base, 1.0, 0.0).astype(bf16)


def source(coord_ref, k, j, F):
    z = lax.rem(coord_ref[0] + F - k, F)
    return z * INNER + lax.bitwise_xor(coord_ref[1], j)


def lookup_kernel(plan, F, gene_n, coord_ref, ids_ref, *refs):
    total = find_rows(plan, F, gene_n, coord_ref, ids_ref[...], refs[:-1])
    refs[-1][...] = total.astype(bf16)


def lookup(coord, ids, tables, plan, F, gene_n, block=1024):
    n, width = ids.shape[1], tables[0].shape[1]
    used = sum(part[3] for parts in plan for part in parts)
    return pl.pallas_call(
        functools.partial(lookup_kernel, plan, F, gene_n),
        grid=(n // block,),
        in_specs=[smem(), lanes(block)] + [whole(*t.shape) for t in tables],
        out_specs=rows(block, width),
        out_shape=jax.ShapeDtypeStruct((n, width), bf16),
        compiler_params=params(),
        cost_estimate=cost(2.1 + n * used * 6.5e-7),
        name="lookup",
    )(coord, ids, *tables)


def count_kernel(size, coord_ref, ids_ref, out_ref):
    high_n = out_ref.shape[0]
    lines = -(-high_n // 16) * 16
    total = None
    for i in range(size):
        ids = ids_ref[i : i + 1, :]
        left = onehot(lax.shift_right_logical(ids, 7), coord_ref[0] * high_n, lines)
        right = onehot(lax.bitwise_and(ids, 127), 0, 128)
        term = dg(left, right, 1, 1)
        total = term if total is None else total + term
    add_to(out_ref, total[0:high_n, :].astype(i32))


def count_rows(coord, ids, own, size=8):
    cells, n = ids.shape
    return pl.pallas_call(
        functools.partial(count_kernel, size),
        grid=(cells // size,),
        in_specs=[smem(), rows(size, n)],
        out_specs=whole(own // 128, 128),
        out_shape=jax.ShapeDtypeStruct((own // 128, 128), i32),
        compiler_params=params(),
        cost_estimate=cost(1.15e-4 * cells * n),
        name="count_rows",
    )(coord, ids)


def add_to(ref, value):
    @pl.when(pl.program_id(0) == 0)
    def _():
        ref[...] = value

    @pl.when(pl.program_id(0) != 0)
    def _():
        ref[...] += value


def prepare_kernel(
    coord_ref, ids_ref, gene, pos, qkv, up, out, down, expr, study, *refs
):
    vectors, piece_ref, small_ref = refs[:9], refs[9], refs[10]
    p = coord_ref[1]
    width = gene.shape[1]
    sub = vectors[0].shape[1]
    per = width // sub
    lines = [
        jnp.concatenate([vectors[per * r + i][...] for i in range(per)], axis=1)
        for r in range(8 // per)
    ]
    last = vectors[8][...]
    lines.append(jnp.concatenate([last, jnp.zeros((1, width - last.shape[1]), bf16)], axis=1))
    small_ref[...] = jnp.concatenate(
        lines + [jnp.zeros((MISC - len(lines), width), bf16)], axis=0
    )
    at = 0
    for ref in (gene, pos):
        piece_ref[at : at + ref.shape[0], :] = ref[...]
        at += ref.shape[0]
    even = lax.bitwise_and(p, 1) == 0
    odd = [up[:, t * width : (t + 1) * width] for t in range(up.shape[1] // width)] + [out[...]]
    for t in range(qkv.shape[1] // width):
        piece_ref[at : at + qkv.shape[0], :] = jnp.where(
            even, qkv[:, t * width : (t + 1) * width], odd[t]
        )
        at += qkv.shape[0]
    piece_ref[at : at + down.shape[0], :] = down[...]
    at += down.shape[0]
    misc = jnp.where(p == 0, expr[...], jnp.where(p == 1, study[...], small_ref[...]))
    piece_ref[at : at + MISC, :] = jnp.where(p < 3, misc, jnp.zeros_like(misc))
    at += MISC
    n = ids_ref.shape[1]
    slot = lax.broadcasted_iota(i32, (1, n), 1)
    ids = jnp.where(slot < coord_ref[2], ids_ref[...], 255 * 128)
    for part in (lax.shift_right_logical(ids, 7), lax.bitwise_and(ids, 127)):
        part = part.astype(f32)
        lines = [part[:, t * width : (t + 1) * width] for t in range(n // width)]
        piece_ref[at : at + n // width, :] = jnp.concatenate(lines, axis=0).astype(bf16)
        at += n // width


def prepare(coord, ids, gene, pos, qkv, up, out, down, expr, study, vectors):
    width = gene.shape[1]
    eighth = [(a.shape[0] // INNER, a.shape[1]) for a in (gene, pos, down)]
    fourth = [(a.shape[0] // (INNER // 2), a.shape[1]) for a in (qkv, up, out)]
    mine = [pl.BlockSpec(s, lambda i, c: (c[1], 0)) for s in eighth]
    pair = [pl.BlockSpec(s, lambda i, c: (lax.shift_right_logical(c[1], 1), 0)) for s in fourth]
    total = sum(s[0] for s in eighth) + fourth[0][0] * fourth[0][1] // width + MISC
    total += 2 * ids.shape[1] // width
    return pl.pallas_call(
        prepare_kernel,
        grid_spec=pltpu.PrefetchScalarGridSpec(
            num_scalar_prefetch=1,
            grid=(1,),
            in_specs=[whole(*ids.shape)] + mine[0:2] + pair + mine[2:]
            + [whole(*a.shape) for a in (expr, study, *vectors)],
            out_specs=[whole(total, width), whole(MISC, width)],
        ),
        out_shape=[
            jax.ShapeDtypeStruct((total, width), bf16),
            jax.ShapeDtypeStruct((MISC, width), bf16),
        ],
        compiler_params=params(),
        cost_estimate=cost(2.5),
        name="prepare",
    )(coord, ids, gene, pos, qkv, up, out, down, expr, study, *vectors)


def assemble(F, n, coord_ref, local, pieces, outs, misc):
    pos_loc, qkv_loc, up_loc, out_loc, down_loc, *misc_loc = local
    pos, cat, down, expr, study, vec, up_vec, ids = outs
    z, p = coord_ref[0], coord_ref[1]
    width = pos.shape[1]
    pos_n, cat_n = pos_loc.shape[0] // INNER, qkv_loc.shape[0] // (INNER // 2)
    down_n = down_loc.shape[0] // INNER
    half = cat.shape[2]
    parts = half // width
    rows_z = cat_n * (INNER // 2)
    lines = n // width
    rest_n = pos_n + cat_n * parts + down_n + MISC + 2 * lines

    def genes(row, ref, at):
        high, low = ref[at : at + lines, :], ref[at + lines : at + 2 * lines, :]
        number = (high.astype(f32) * 128.0 + low.astype(f32)).astype(i32)
        for t in range(lines):
            ids[row : row + 1, t * width : (t + 1) * width] = number[t : t + 1, :]

    pos[pl.ds(aligned(z * pos_n * INNER, 16), pos_n * INNER), :] = pos_loc[...]
    down[pl.ds(aligned(z * down_n * INNER, 16), down_n * INNER), :] = down_loc[...]
    span = pl.ds(aligned(z * rows_z, 16), rows_z)
    cat[0, span, :] = qkv_loc[...]
    cat[1, span, 0 : half - width] = up_loc[...]
    cat[1, span, half - width :] = out_loc[...]
    for t in range(3):
        misc[z * INNER + t] = misc_loc[t][...]
    for j in range(INNER):
        pj = lax.bitwise_xor(p, j)
        ref = pieces[j]
        for k in range(1, F):
            zk = lax.rem(z + F - k, F)
            at = rest_n * (k - 1)
            pos[pl.ds(aligned((zk * INNER + pj) * pos_n, 16), pos_n), :] = ref[at : at + pos_n, :]
            at += pos_n
            row = aligned(zk * rows_z + lax.shift_right_logical(pj, 1) * cat_n, 16)
            side = lax.bitwise_and(pj, 1)
            for s in range(parts):
                cat[side, pl.ds(row, cat_n), s * width : (s + 1) * width] = ref[at : at + cat_n, :]
                at += cat_n
            down[pl.ds(aligned((zk * INNER + pj) * down_n, 16), down_n), :] = ref[at : at + down_n, :]
            at += down_n
            misc[zk * INNER + pj] = ref[at : at + MISC, :]
            genes(k * INNER + j, ref, at + MISC)
        genes(j, ref, rest_n * (F - 1))
    sub = width // F
    for zz in range(F):
        expr[MISC * zz : MISC * zz + MISC, :] = misc[zz * INNER]
        study[MISC * zz : MISC * zz + MISC, :] = misc[zz * INNER + 1]
    small = [misc[zz * INNER + 2].astype(f32) for zz in range(F)]
    for i in range(8):
        r, c = i // F, sub * (i % F)
        vec[i : i + 1, :] = jnp.concatenate([s[r : r + 1, c : c + sub] for s in small], axis=1)
    r = 8 // F
    up_vec[...] = jnp.concatenate(
        [s[r : r + 1, 0 : up_vec.shape[1] // F] for s in small], axis=1
    )


def standard(values):
    average = jnp.mean(values, axis=1, keepdims=True)
    centered = values - average
    scale = lax.rsqrt(jnp.mean(centered * centered, axis=1, keepdims=True) + epsilon)
    return centered * scale, scale


def slot_mask(len_ref, size):
    slot = pl.program_id(0) * size + lax.broadcasted_iota(i32, (size, 1), 0)
    return (slot < len_ref[2]).astype(f32)


def find_rows(plan, F, gene_n, coord_ref, ids, tables):
    total = None
    for table, parts in zip(tables, plan):
        hits = [
            onehot(ids, source(coord_ref, k, j, F) * gene_n + off, count)
            if j is not None
            else onehot(ids, coord_ref[0] * gene_n * INNER, count)
            for k, j, off, count in parts
        ]
        hits = hits[0] if len(hits) == 1 else jnp.concatenate(hits, axis=0)
        term = dg(hits, table[table.shape[0] - hits.shape[0] :, :], 0, 0)
        total = term if total is None else total + term
    return total


def embed_kernel(F, n, gene_n, plan, use, sizes, coord_ref, ids_ref, bins_ref, prior, *refs):
    size, found_n, local_n, piece_n = sizes
    found, refs = refs[:found_n], refs[found_n:]
    local, refs = refs[:local_n], refs[local_n:]
    pieces, refs = refs[:piece_n], refs[piece_n:]
    inputs_ref, q_ref, k_ref, v_ref = refs[0:4]
    pos, cat, down, expr, study, vec, up_vec, ids_all, misc = refs[4:]
    width = prior.shape[1]

    @pl.when(pl.program_id(0) == 0)
    def _():
        assemble(F, n, coord_ref, local, [pieces[t] for t in use], refs[4:-1], misc)

    total = find_rows(plan, F, gene_n, coord_ref, ids_ref[...], pieces[piece_n - len(plan) :])
    total = total + dg(onehot(bins_ref[...], 0, expr.shape[0]), expr[...], 0, 0)
    for ref in found:
        total = total + ref[...].astype(f32)
    here = (lax.broadcasted_iota(i32, (8, study.shape[0]), 1) == coord_ref[3]).astype(bf16)
    total = total + dg(here, study[...], 1, 0)[0:1, :]
    slots = pl.ds(aligned(pl.program_id(0) * size, size), size)
    total = total + pos[slots, :].astype(f32) + prior[...].astype(f32)
    total = total * slot_mask(coord_ref, size)
    inputs_ref[...] = total
    normed, _ = standard(total)
    normed = (normed * vec[0:1, :] + vec[1:2, :]).astype(bf16)
    mixed = dg(normed, cat[0], 1, 0)
    q_ref[...] = (mixed[:, 0:width] + vec[2:3, :]).astype(bf16)
    k_ref[...] = mixed[:, width : 2 * width].astype(bf16)
    v_ref[...] = (mixed[:, 2 * width :] + vec[3:4, :]).astype(bf16)


def embed(coord, ids, bins, prior, found, local, pieces, use, plan, F, gene_n, rest, size=1024):
    n, width = prior.shape
    pos, qkv, up, out, down, *_ = local
    block = rows(size, width)
    outs = [
        ((F * pos.shape[0], width), bf16),
        ((2, F * qkv.shape[0], qkv.shape[1]), bf16),
        ((F * down.shape[0], width), bf16),
        ((F * MISC, width), bf16),
        ((F * MISC, width), bf16),
        ((8, width), f32),
        ((1, up.shape[1]), f32),
        ((F * INNER, n), i32),
    ]
    short = len(pieces) - len(plan)
    kernel = functools.partial(
        embed_kernel, F, n, gene_n, plan, use, (size, len(found), len(local), len(pieces))
    )
    return pl.pallas_call(
        kernel,
        grid=(n // size,),
        in_specs=[smem(), lanes(size), lanes(size)]
        + [block] * (1 + len(found))
        + [whole(*a.shape) for a in local]
        + [whole(rest, width)] * short
        + [whole(*a.shape) for a in pieces[short:]],
        out_specs=[block] * 4 + [whole(*s) for s, _ in outs],
        out_shape=[jax.ShapeDtypeStruct((n, width), f32)]
        + [jax.ShapeDtypeStruct((n, width), bf16)] * 3
        + [jax.ShapeDtypeStruct(*s) for s in outs],
        scratch_shapes=[pltpu.VMEM((F * INNER, MISC, width), bf16)],
        compiler_params=params(),
        cost_estimate=cost(15.5),
        name="embed",
    )(coord, ids, bins, prior, *found, *local, *pieces)


def extend(pair, half, spare):
    size = pair.shape[1] // 2
    lane = lax.broadcasted_iota(i32, pair.shape, 1)
    base = size * (1 - half)
    out = jnp.where((lane >= size * half) & (lane < size * half + size), pair, jnp.zeros_like(pair))
    for t, value in enumerate(spare):
        out = jnp.where(lane == base + t, jnp.broadcast_to(value, pair.shape), out)
    return out


def one():
    return jnp.ones((1, 1), bf16)


def split3(value):
    high = value.astype(bf16)
    rest = value - high.astype(f32)
    middle = rest.astype(bf16)
    return high, middle, (rest - middle.astype(f32)).astype(bf16)


def attend_kernel(len_ref, q_ref, k_ref, v_ref, o_ref, wide_ref, inv_ref, e_ref, kx, vx):
    n, pair = k_ref.shape
    size = pair // 2
    factor = size ** (-0.5) * LOG2E

    @pl.when(pl.program_id(1) == 0)
    def _():
        slot = lax.broadcasted_iota(i32, (n, 1), 0)
        bias = jnp.where(slot < len_ref[0], 0.0, -1e9).astype(bf16)
        lane = lax.broadcasted_iota(i32, (n, pair), 1)
        for h in range(2):
            kx[h] = extend(k_ref[...], h, [bias])
            own = (lane >= size * h) & (lane < size * h + size)
            vx[h] = jnp.where(own, v_ref[...], jnp.ones_like(v_ref[...]))

    scores = [dg(extend(q_ref[...], h, [one()]), kx[h], 1, 1) for h in range(2)]
    peaks = [jnp.max(s, axis=1, keepdims=True) for s in scores]
    raised = [jnp.exp2((s - p) * factor).astype(bf16) for s, p in zip(scores, peaks)]
    outs, totals = [], []
    for h in range(2):
        e_ref[h] = raised[h]
        out = dg(raised[h], vx[h], 1, 0)
        outs.append(out)
        totals.append(jnp.concatenate([out[:, size:], out[:, :size]], axis=1))
    low = lax.broadcasted_iota(i32, outs[0].shape, 1) < size
    inverse = 1.0 / jnp.where(low, totals[0], totals[1])
    out = jnp.where(low, outs[0], outs[1]) * inverse
    inv_ref[...] = inverse
    wide_ref[...] = out
    o_ref[...] = out.astype(bf16)


def attend(length, q, k, v, size=512):
    n, width = q.shape
    two = 2 * width // HEADS
    block = pl.BlockSpec((size, two), lambda j, i: (i, j))
    full = pl.BlockSpec((n, two), lambda j, i: (0, j))
    return pl.pallas_call(
        attend_kernel,
        grid=(HEADS // 2, n // size),
        in_specs=[smem(), block, full, full],
        out_specs=[block] * 3 + [pl.BlockSpec((2, size, n), lambda j, i: (j, i, 0))],
        out_shape=[
            jax.ShapeDtypeStruct((n, width), bf16),
            jax.ShapeDtypeStruct((n, width), f32),
            jax.ShapeDtypeStruct((n, width), f32),
            jax.ShapeDtypeStruct((HEADS, n, n), bf16),
        ],
        scratch_shapes=[pltpu.VMEM((2, n, two), bf16)] * 2,
        compiler_params=params(),
        cost_estimate=cost(32),
        name="attend",
    )(length, q, k, v)


def attend_back_kernel(
    q_ref, k_ref, v_ref, o_ref, do_ref, inv_ref, e_ref, dq_ref, dk_ref, dv_ref, vx, dkt, dvt
):
    n, pair = k_ref.shape
    size = pair // 2
    scale = size ** (-0.5)

    @pl.when(pl.program_id(1) == 0)
    def _():
        for h in range(2):
            vx[h] = extend(v_ref[...], h, [one(), one(), one()])
        dkt[...] = jnp.zeros_like(dkt)
        dvt[...] = jnp.zeros_like(dvt)

    grad = (do_ref[...].astype(f32) * inv_ref[...]).astype(bf16)
    product = grad.astype(f32) * o_ref[...]
    qt = q_ref[...].T
    gt = grad.T
    grads = []
    for h in range(2):
        span = slice(size * h, size * h + size)
        inner = jnp.sum(product[:, span], axis=1, keepdims=True)
        raised = e_ref[h]
        back = dg(extend(grad, h, [*split3(-inner)]), vx[h], 1, 1)
        grad_scores = (raised.astype(f32) * back).astype(bf16)
        dvt[span, :] += dg(gt[span, :], raised, 1, 0)
        dkt[span, :] += dg(qt[span, :], grad_scores, 1, 0)
        grads.append(dg(grad_scores, k_ref[...], 1, 0))
    low = lax.broadcasted_iota(i32, grads[0].shape, 1) < size
    dq_ref[...] = (jnp.where(low, grads[0], grads[1]) * scale).astype(bf16)

    @pl.when(pl.program_id(1) == pl.num_programs(1) - 1)
    def _():
        dk_ref[...] = (dkt[...] * scale).T.astype(bf16)
        dv_ref[...] = dvt[...].T.astype(bf16)


def attend_back(q, k, v, o, do, inverse, raised, size=256):
    n, width = q.shape
    two = 2 * width // HEADS
    block = pl.BlockSpec((size, two), lambda j, i: (i, j))
    full = pl.BlockSpec((n, two), lambda j, i: (0, j))
    return pl.pallas_call(
        attend_back_kernel,
        grid=(HEADS // 2, n // size),
        in_specs=[block, full, full, block, block, block]
        + [pl.BlockSpec((2, size, n), lambda j, i: (j, i, 0))],
        out_specs=[block, full, full],
        out_shape=[jax.ShapeDtypeStruct((n, width), bf16)] * 3,
        scratch_shapes=[pltpu.VMEM((2, n, two), bf16)] + [pltpu.VMEM((two, n), f32)] * 2,
        compiler_params=params(),
        cost_estimate=cost(40),
        name="attend_back",
    )(q, k, v, o, do, inverse, raised)


def feed_kernel(
    size, len_ref, att_ref, in_ref, cot_ref, cat, down, vec, up_vec,
    hidden_ref, mid_ref, datt_ref, wg_ref, g_vec, g_up_vec, g_down, g_up, g_out,
):
    width = att_ref.shape[1]
    up_width = down.shape[0]
    w_up, w_out = cat[1, :, 0:up_width], cat[1, :, up_width:]
    mask = slot_mask(len_ref, size)
    att = att_ref[...]
    middle = in_ref[...] + dg(att, w_out, 1, 0) + vec[4:5, :]
    normed, scale = standard(middle)
    low = (normed * vec[5:6, :] + vec[6:7, :]).astype(bf16)
    upward = dg(low, w_up, 1, 0) + up_vec[...]
    share = 0.5 * (1.0 + lax.erf(upward * (0.5**0.5)))
    active = (upward * share).astype(bf16)
    result = middle + dg(active, down[...], 1, 0) + vec[7:8, :]
    hidden_ref[...] = (result * mask).astype(bf16)
    grad_low = (cot_ref[...].astype(f32) * mask).astype(bf16)
    grad = grad_low.astype(f32)
    bell = jnp.exp(upward * upward * -0.5) * 0.3989422804014327
    grad_up = ((share + upward * bell) * dg(grad_low, down[...], 1, 1)).astype(bf16)
    grad_norm = dg(grad_up, w_up, 1, 1)
    scaled = grad_norm * vec[5:6, :]
    back = scaled - jnp.mean(scaled, axis=1, keepdims=True)
    back = back - normed * jnp.mean(scaled * normed, axis=1, keepdims=True)
    grad_mid = grad + scale * back
    branch = grad_mid.astype(bf16)
    mid_ref[...] = grad_mid
    datt_ref[...] = dg(branch, w_out, 1, 1).astype(bf16)
    add_to(g_down, dg(active, grad_low, 0, 0))
    add_to(g_up, dg(low, grad_up, 0, 0))
    add_to(g_out, dg(att, branch, 0, 0))
    sums = [
        jnp.sum(t, axis=0, keepdims=True)
        for t in (branch.astype(f32), grad_norm * normed, grad_norm, grad)
    ]
    add_to(g_vec, jnp.concatenate(sums + sums, axis=0))
    add_to(g_up_vec, jnp.sum(grad_up.astype(f32), axis=0, keepdims=True))

    @pl.when(pl.program_id(0) == pl.num_programs(0) - 1)
    def _():
        F = wg_ref.shape[3]
        line_n, down_n = width // F // INNER, up_width // F // INNER
        for z in range(F):
            for p in range(INNER):
                at = line_n * (INNER * z + p)
                blocks = [
                    g_up[at : at + line_n, t * width : (t + 1) * width]
                    for t in range(up_width // width)
                ]
                blocks.append(g_out[at : at + line_n, :])
                at = down_n * (INNER * z + p)
                blocks.append(g_down[at : at + down_n, :])
                at = 0
                for b in blocks:
                    wg_ref[p % 2, p // 2 % 2, p // 4, z, at : at + b.shape[0], :] = b.astype(bf16)
                    at += b.shape[0]


def feed(coord, att, inputs, cot, cat, down, vec, up_vec, F, size=1024):
    n, width = att.shape
    up_width = down.shape[0]
    block = rows(size, width)
    w_rows = (width * (up_width + width) // width + up_width) // F // INNER
    shapes = [(2, 2, 2, F, w_rows, width), (8, width), (1, up_width)]
    return pl.pallas_call(
        functools.partial(feed_kernel, size),
        grid=(n // size,),
        in_specs=[smem(), block, block, block]
        + [whole(*a.shape) for a in (cat, down, vec, up_vec)],
        out_specs=[block] * 3 + [whole(*s) for s in shapes],
        out_shape=[
            jax.ShapeDtypeStruct((n, width), bf16),
            jax.ShapeDtypeStruct((n, width), f32),
            jax.ShapeDtypeStruct((n, width), bf16),
        ]
        + [jax.ShapeDtypeStruct(shapes[0], bf16)]
        + [jax.ShapeDtypeStruct(s, f32) for s in shapes[1:]],
        scratch_shapes=[
            pltpu.VMEM((up_width, width), f32),
            pltpu.VMEM((width, up_width), f32),
            pltpu.VMEM((width, width), f32),
        ],
        compiler_params=params(),
        cost_estimate=cost(20),
        name="feed",
    )(coord, att, inputs, cot, cat, down, vec, up_vec)


def inputs_back_kernel(size, coord_ref, dq_ref, dk_ref, dv_ref, in_ref, mid_ref, cat, vec, out_ref, norm_ref):
    width = dq_ref.shape[1]
    normed, scale = standard(in_ref[...])
    grad_norm = None
    for t, part in enumerate((dq_ref, dk_ref, dv_ref)):
        term = dg(part[...], cat[0, :, t * width : (t + 1) * width], 1, 1)
        grad_norm = term if grad_norm is None else grad_norm + term
    scaled = grad_norm * vec[0:1, :]
    back = scaled - jnp.mean(scaled, axis=1, keepdims=True)
    back = back - normed * jnp.mean(scaled * normed, axis=1, keepdims=True)
    out_ref[...] = ((mid_ref[...] + scale * back) * slot_mask(coord_ref, size)).astype(bf16)
    norm_ref[...] = grad_norm


def inputs_back(coord, dq, dk, dv, inputs, mid, cat, vec, size=1024):
    n, width = dq.shape
    block = rows(size, width)
    return pl.pallas_call(
        functools.partial(inputs_back_kernel, size),
        grid=(n // size,),
        in_specs=[smem()] + [block] * 5
        + [pl.BlockSpec((1, *cat.shape[1:]), lambda i: (0, 0, 0)), whole(*vec.shape)],
        out_specs=[block] * 2,
        out_shape=[jax.ShapeDtypeStruct((n, width), t) for t in (bf16, f32)],
        compiler_params=params(),
        cost_estimate=cost(6.4),
        name="inputs_back",
    )(coord, dq, dk, dv, inputs, mid, cat, vec)


def weights_back_kernel(
    size, F, scalar_ref, bins_ref, dq_ref, dk_ref, dv_ref, in_ref, grad_ref, norm_ref, vec,
    g_vec2, g_up_vec, wg_ref, g_qkv, g_vec, g_expr,
):
    width = dq_ref.shape[1]
    normed, _ = standard(in_ref[...])
    low = (normed * vec[0:1, :] + vec[1:2, :]).astype(bf16)
    for t, part in enumerate((dq_ref, dk_ref, dv_ref)):
        add_to(g_qkv.at[:, t * width : (t + 1) * width], dg(low, part[...], 0, 0))
    grad_norm, grad = norm_ref[...], grad_ref[...]
    sums = [
        jnp.sum(t, axis=0, keepdims=True)
        for t in (
            grad_norm * normed,
            grad_norm,
            dq_ref[...].astype(f32),
            dv_ref[...].astype(f32),
            grad.astype(f32),
        )
    ]
    add_to(g_vec, jnp.concatenate(sums + sums[0:3], axis=0))
    add_to(g_expr, dg(onehot(bins_ref[...], 0, g_expr.shape[0]), grad, 1, 0))

    @pl.when(pl.program_id(0) == pl.num_programs(0) - 1)
    def _():
        line_n = width // F // INNER
        sub = width // F
        up_sub = g_up_vec.shape[1] // F
        groups = g_expr.shape[0]
        here = lax.broadcasted_iota(i32, (groups, width), 0) == scalar_ref[3]
        g_study = jnp.where(here, jnp.broadcast_to(g_vec[4:5, :], (groups, width)), 0.0)
        vectors = [g_vec[i : i + 1, :] for i in range(4)] + [g_vec2[i : i + 1, :] for i in range(4)]
        for z in range(F):
            small = []
            for r in range(8 // F):
                small.append(
                    jnp.concatenate(
                        [vectors[r * F + i][:, z * sub : (z + 1) * sub] for i in range(F)], axis=1
                    )
                )
            up_row = g_up_vec[:, z * up_sub : (z + 1) * up_sub]
            small.append(jnp.concatenate([up_row, jnp.zeros((1, width - up_sub), f32)], axis=1))
            small.append(jnp.zeros((8 - len(small), width), f32))
            at = MISC * z
            misc = [
                g_expr[at : at + 8, :],
                g_expr[at + 8 : at + 16, :],
                g_study[at : at + 8, :],
                g_study[at + 8 : at + 16, :],
                jnp.concatenate(small, axis=0),
            ]
            for p in range(INNER):
                at = line_n * (INNER * z + p)
                blocks = [
                    g_qkv[at : at + line_n, t * width : (t + 1) * width] for t in range(3)
                ] + [misc[p] if p < 5 else jnp.zeros((8, width), f32)]
                wg_ref[p % 2, p // 2 % 2, p // 4, z] = jnp.concatenate(blocks, axis=0).astype(bf16)


def weights_back(coord, bins, dq, dk, dv, inputs, grad, norm, vec, grads, half, bins_total, F, size=1024):
    n, width = dq.shape
    block = rows(size, width)
    shape = (2, 2, 2, F, half // F // INNER + 8, width)
    return pl.pallas_call(
        functools.partial(weights_back_kernel, size, F),
        grid=(n // size,),
        in_specs=[smem(), lanes(size)] + [block] * 6 + [whole(*a.shape) for a in (vec, *grads)],
        out_specs=whole(*shape),
        out_shape=jax.ShapeDtypeStruct(shape, bf16),
        scratch_shapes=[
            pltpu.VMEM((width, half), f32),
            pltpu.VMEM((8, width), f32),
            pltpu.VMEM((bins_total, width), f32),
        ],
        compiler_params=params(),
        cost_estimate=cost(9),
        name="weights_back",
    )(coord, bins, dq, dk, dv, inputs, grad, norm, vec, *grads)


def scatter_kernel(cells, F, gene_n, pos_n, start_at, group, extra, coord_ref, *refs):
    ids, refs = refs[0], refs[1:]
    grads, refs = refs[: len(cells)], refs[len(cells) :]
    lines, old, out_ref = refs[:extra], refs[extra:-1], refs[-1]
    for g in range(group):
        number = pl.program_id(0) * group + start_at + g
        z = lax.rem(coord_ref[0] + number, F)
        other = (number < F).astype(i32)
        place = z * INNER + lax.bitwise_xor(coord_ref[1], other)
        total = None
        for (cell, start, size), ref in zip(cells, grads):
            hits = onehot(ids[cell : cell + 1, start : start + size], place * gene_n, gene_n)
            term = dg(hits, ref[...], 1, 0)
            total = term if total is None else total + term
        line = None
        for (cell, start, size), ref in zip(cells, grads):
            inside = (place * pos_n >= start) & (place * pos_n < start + size)
            at = aligned(jnp.where(inside, place * pos_n - start, 0), 16)
            term = jnp.where(inside, ref[pl.ds(at, pos_n), :].astype(f32), 0.0)
            line = term if line is None else line + term
        for ref in old:
            total = total + ref[g, 0:gene_n, :]
            line = line + ref[g, gene_n : gene_n + pos_n, :]
        out_ref[g, 0:gene_n, :] = total.astype(out_ref.dtype)
        out_ref[g, gene_n : gene_n + pos_n, :] = line.astype(out_ref.dtype)
        for ref in lines:
            out_ref[g, gene_n + pos_n :, :] = ref[z]


def scatter(coord, cells, ids, grads, old, extra, F, gene_n, pos_n, start):
    width = grads[0].shape[1]
    size = gene_n + pos_n
    count = F if old else 2 * F
    group = GROUP_LAST if old else GROUP
    more = [] if extra is None else [extra]
    full = size + sum(e.shape[1] for e in more)
    first = start // group
    return pl.pallas_call(
        functools.partial(scatter_kernel, cells, F, gene_n, pos_n, start, group, len(more)),
        grid=(count // group,),
        in_specs=[smem(), whole(INNER, ids.shape[1])]
        + [whole(*g.shape) for g in grads]
        + [whole(*e.shape) for e in more]
        + [pl.BlockSpec((group, size, width), lambda i: (i + first, 0, 0))] * len(old),
        out_specs=pl.BlockSpec((group, full, width), lambda i: (i, 0, 0)),
        out_shape=jax.ShapeDtypeStruct((count, full, width), bf16 if old else f32),
        compiler_params=params(),
        cost_estimate=cost(2.5 + count * sum(c[2] for c in cells) * 2.5e-4),
        name="scatter",
    )(coord, ids, *grads, *more, *old)


def unpack_kernel(F, gene_n, pos_n, line_n, down_n, coord_ref, *refs):
    pieces, refs = refs[: INNER + 2], refs[INNER + 2 :]
    gene, pos, qkv, up, out, down, expr, study = refs[:8]
    vectors, misc = refs[8:17], refs[17]
    p = coord_ref[1]
    width = gene.shape[1]
    for j in range(INNER):
        pj = lax.bitwise_xor(p, j)
        if j < 6:
            here = [(pieces[j], 0)]
        else:
            top, bottom = pieces[6 + 2 * (j - 6)], pieces[7 + 2 * (j - 6)]
            here = [(top, 0), (bottom, top.shape[0])]
        for ref, first in here:
            count = min(ref.shape[0], gene_n - first)
            gene[pl.ds(aligned(gene_n * pj + first, 16), count), :] = ref[0:count, :].astype(f32)
        ref, first = here[-1]
        at = gene_n - first
        tail = ref[at : at + pos_n, :].astype(f32)
        pos[pl.ds(aligned(pos_n * pj, 16), pos_n), :] = tail
        at += pos_n
        tail = ref[at:, :].astype(f32)
        row = pl.ds(aligned(line_n * pj, 8), line_n)
        at = 0
        for s in range(up.shape[1] // width):
            up[row, s * width : (s + 1) * width] = tail[at : at + line_n, :]
            at += line_n
        out[row, :] = tail[at : at + line_n, :]
        at += line_n
        down[pl.ds(aligned(pj * down_n, 16), down_n), :] = tail[at : at + down_n, :]
        at += down_n
        for s in range(3):
            qkv[row, s * width : (s + 1) * width] = tail[at : at + line_n, :]
            at += line_n
        misc[pj] = tail[at : at + 8, :]
    for t in range(2):
        expr[8 * t : 8 * t + 8, :] = misc[t]
        study[8 * t : 8 * t + 8, :] = misc[2 + t]
    small = misc[4]
    sub = width // F
    for i in range(8):
        vectors[i][...] = small[i // F : i // F + 1, sub * (i % F) : sub * (i % F + 1)]
    vectors[8][...] = small[8 // F : 8 // F + 1, 0 : vectors[8].shape[1]]


def unpack(coord, pieces, F, gene_n, pos_n, line_n, down_n, up_width):
    width = pieces[0].shape[1]
    vmem = pl.BlockSpec(memory_space=pltpu.VMEM)
    shapes = [
        (gene_n * INNER, width),
        (pos_n * INNER, width),
        (line_n * INNER, 3 * width),
        (line_n * INNER, up_width),
        (line_n * INNER, width),
        (down_n * INNER, width),
        (MISC, width),
        (MISC, width),
    ]
    shapes += [(1, width // F)] * 8 + [(1, up_width // F)]
    return pl.pallas_call(
        functools.partial(unpack_kernel, F, gene_n, pos_n, line_n, down_n),
        in_specs=[smem()] + [vmem] * len(pieces),
        out_shape=[jax.ShapeDtypeStruct(s, f32) for s in shapes],
        scratch_shapes=[pltpu.VMEM((INNER, 8, width), f32)],
        compiler_params=params(),
        cost_estimate=cost(3.7),
        name="unpack",
    )(coord, *pieces)


def swap(array, bit):
    return lax.ppermute(array, "inner", [(i, i ^ bit) for i in range(INNER)])


def along(array, step, F):
    return lax.ppermute(array, "fsdp", [(i, (i + step) % F) for i in range(F)])


def after(arrays, work):
    return lax.optimization_barrier((arrays, work))[0]


def spread(piece, use=None):
    if use is None:
        use = lambda step, arrays: ()
    cut = piece.shape[0] // 32 * 16
    near, other, core = swap(piece, 2), swap(piece, 4), swap(piece, 1)
    near, other = after((near, other), use(0, [piece, core]))
    upper, lower = swap(near[:cut], 4), swap(other[cut:], 2)
    near1, other1 = swap(near, 1), swap(other, 1)
    upper, lower = after((upper, lower), use(1, [core, near, other, near1, other1]))
    upper1, lower1 = swap(upper, 1), swap(lower, 1)
    return [piece, core, near, near1, other, other1, upper, lower, upper1, lower1]


def plus(left, right):
    return (left.astype(f32) + right.astype(f32)).astype(bf16)


def pick(array, index, axis):
    return lax.dynamic_index_in_dim(array, index, axis, keepdims=False)


def fold_core(array, p):
    mine = lax.bitwise_and(p, 1)
    return plus(pick(array, mine, 0), swap(pick(array, 1 - mine, 0), 1))


def fold_plane(array, p):
    x, y = (lax.bitwise_and(lax.shift_right_logical(p, b), 1) for b in (1, 2))
    terms = []
    for bits in range(4):
        dx, dy = bits & 1, bits >> 1
        term = pick(pick(array, lax.bitwise_xor(x, dx), 0), lax.bitwise_xor(y, dy), 0)
        terms.append(swap(term, 2 * bits) if bits else term)
    return terms


def sum_low(terms):
    total = terms[0].astype(f32)
    for term in terms[1:]:
        total = total + term.astype(f32)
    return total.astype(bf16)


def body(
    outer, F,
    gene_ids, expr_bins, study_ids, lengths, prior_embed, cotangent,
    gene_table, expr_table, study_table, position_table,
    norm1_gain, norm1_shift, w_qkv, bias_query, bias_value, w_output, bias_output,
    norm2_gain, norm2_shift, w_up_proj, bias_up, w_down_proj, bias_down,
):
    n = gene_ids.shape[1]
    z, p = lax.axis_index("fsdp"), lax.axis_index("inner")
    gene_n = gene_table.shape[0] // INNER
    pos_n = position_table.shape[0] // INNER
    down_n = w_down_proj.shape[0] // INNER
    line_n = w_qkv.shape[0] // INNER
    prior, cot = prior_embed[0], cotangent[0]
    coord = jnp.stack([z.astype(i32), p.astype(i32), lengths[0], study_ids[0]])

    vectors = [
        v.reshape(1, -1)
        for v in (norm1_gain, norm1_shift, bias_query, bias_value,
                  bias_output, norm2_gain, norm2_shift, bias_down, bias_up)
    ]
    piece, small = prepare(
        coord, gene_ids, gene_table, position_table, w_qkv, w_up_proj, w_output, w_down_proj,
        expr_table, study_table, vectors,
    )
    got = [along(piece, k, F) for k in range(1, F)]
    gene_total = (F - 1) * gene_n

    def plan(j, first=0, count=gene_total):
        parts = []
        for k in range(F - 1):
            low, high = max(first, k * gene_n), min(first + count, (k + 1) * gene_n)
            if low < high:
                parts.append((k + 1, j, low - k * gene_n, high - low))
        return tuple(parts)

    def find(tables, plans):
        return lookup(coord, gene_ids, tables, tuple(plans), F, gene_n)

    found = [find([gene_table], [((0, None, 0, gene_table.shape[0]),)])]
    got = after(got, found[0])
    genes = piece[piece.shape[0] - 2 * n // gene_table.shape[1] :]
    stack = jnp.concatenate([g[gene_n:] for g in got] + [genes] + [g[:gene_n] for g in got])
    rest = stack.shape[0] - gene_total
    cut = stack.shape[0] // 32 * 16
    top, bottom = (0, cut - rest), (cut - rest, stack.shape[0] - cut)

    def look(step, arrays):
        if step == 0:
            found.append(find(arrays[:1], [plan(0)]))
        else:
            found.append(find(arrays[:3], [plan(1), plan(2), plan(4)]))
        return found[-1]

    pieces = spread(stack, look)
    inputs, query, keys, values, pos, cat, down, expr, study, vec, up_vec, ids = embed(
        coord, gene_ids, expr_bins, prior, found,
        [position_table, w_qkv, w_up_proj, w_output, w_down_proj, expr_table, study_table, small],
        [pieces[0], pieces[1], pieces[2], pieces[4], pieces[3], pieces[5], *pieces[6:]],
        (0, 1, 2, 4, 3, 5, 6, 8),
        (plan(3), plan(5), plan(6, *top), plan(6, *bottom), plan(7, *top), plan(7, *bottom)),
        F, gene_n, rest,
    )
    attended, wide, inverse, raised = attend(lengths, query, keys, values)
    hidden, mid, grad_attended, wg_feed, *grads = feed(
        coord, attended, inputs, cot, cat, down, vec, up_vec, F
    )
    wg_feed = fold_core(wg_feed, p)
    dqkv = attend_back(query, keys, values, wide, grad_attended, inverse, raised)
    wg_feed, dqkv = lax.optimization_barrier((wg_feed, dqkv))
    grad, norm = inputs_back(coord, *dqkv, inputs, mid, cat, vec)

    cut = n // 2

    def add_rows(cells, arrays, old=(), start=0, extra=None):
        return scatter(coord, tuple(cells), ids, arrays, old, extra, F, gene_n, pos_n, start)

    near, other = swap(grad, 2), swap(grad, 4)
    wg = weights_back(
        coord, expr_bins, *dqkv, inputs, grad, norm, vec, grads, w_qkv.shape[1], expr.shape[0], F
    )
    first = add_rows([(0, 0, n)], [grad])
    wg = fold_plane(jnp.concatenate([wg_feed, fold_core(wg, p)], axis=3), p)
    near, other, wg = after((near, other, wg), first)
    upper, lower = swap(near[:cut], 4), swap(other[cut:], 2)
    lines = sum_low(wg)
    second = add_rows([(2, 0, n), (4, 0, n)], [near, other])
    upper, lower = after((upper, lower), second)
    last = [(6, 0, cut), (6, cut, n - cut)]
    theirs = add_rows(last, [upper, lower], [first, second], 0)
    blocks = add_rows(last, [upper, lower], [first, second], F, lines)
    theirs = after(swap(theirs, 1), blocks)
    blocks = plus(blocks, jnp.pad(theirs, ((0, 0), (0, lines.shape[1]), (0, 0))))
    got = [along(blocks[k], k, F) for k in range(1, F)]
    own = count_rows(coord, after(ids, blocks), gene_table.shape[0])
    got = after(got, own)
    own = own.reshape(-1)
    if outer > 1:
        own = lax.psum(own, "outer")
    total = blocks[0].astype(f32)
    for g in got:
        total = total + g.astype(f32)
    if outer > 1:
        total = lax.psum(total, "outer")
    done = spread(total.astype(bf16))
    gene, pos, qkv, up, out, down, expr, study, *small = unpack(
        coord, done, F, gene_n, pos_n, line_n, down_n, w_up_proj.shape[1]
    )
    small = [s.reshape(-1) for s in small]
    return (
        hidden[None], gene, own, expr, study, pos, small[0], small[1], qkv, small[2], small[3],
        out, small[4], small[5], small[6], up, small[8], down, small[7],
    )


def solution(mesh):
    dp, F = mesh.devices.shape
    outer = dp // INNER
    mesh = Mesh(mesh.devices.reshape(outer, INNER, F), ("outer", "inner", "fsdp"))
    cells = ("outer", "inner", "fsdp")
    row, line = P("fsdp", None), P("fsdp")
    tables = (row,) * 4 + (line,) * 2 + (row, line, line, row, line, line, line, row, line, row, line)
    return jax.shard_map(
        functools.partial(body, outer, F),
        mesh=mesh,
        in_specs=(P(cells, None), P(cells, None), P(cells), P(cells), P(cells, None, None), P(cells, None, None))
        + tables,
        out_specs=(P(cells, None, None), row, line) + tables[1:],
        check_vma=False,
    )
```

```python
import functools

import jax
import jax.numpy as jnp
from jax import lax
from jax.experimental import pallas as pl
from jax.experimental.pallas import tpu as pltpu
from jax.sharding import Mesh
from jax.sharding import PartitionSpec as P

HEADS = 4
INNER = 8
GROUP = 2
GROUP_LAST = 2
MISC = 16
epsilon = 1e-05
LOG2E = 1.4426950408889634
bf16 = jnp.bfloat16
f32 = jnp.float32
i32 = jnp.int32


def params():
    return pltpu.CompilerParams(vmem_limit_bytes=56 << 20)


def cost(us):
    return pl.CostEstimate(flops=int(us * 5e7), bytes_accessed=0, transcendentals=0)


def dg(left, right, a, b):
    return lax.dot_general(left, right, (((a,), (b,)), ((), ())), preferred_element_type=f32)


def smem():
    return pl.BlockSpec(memory_space=pltpu.SMEM)


def whole(*shape):
    return pl.BlockSpec(shape, lambda *_: (0,) * len(shape))


def rows(size, width):
    return pl.BlockSpec((size, width), lambda i, *_: (i, 0))


def lanes(size):
    return pl.BlockSpec((1, size), lambda i, *_: (0, i))


def aligned(index, step):
    return pl.multiple_of(index, step)


def onehot(ids, base, count):
    number = lax.broadcasted_iota(i32, (count, ids.shape[1]), 0)
    return jnp.where(number == ids - base, 1.0, 0.0).astype(bf16)


def source(coord_ref, k, j, F):
    z = lax.rem(coord_ref[0] + F - k, F)
    return z * INNER + lax.bitwise_xor(coord_ref[1], j)


def lookup_kernel(plan, F, gene_n, coord_ref, ids_ref, *refs):
    total = find_rows(plan, F, gene_n, coord_ref, ids_ref[...], refs[:-1])
    refs[-1][...] = total.astype(bf16)


def lookup(coord, ids, tables, plan, F, gene_n, block=1024):
    n, width = ids.shape[1], tables[0].shape[1]
    used = sum(part[3] for parts in plan for part in parts)
    return pl.pallas_call(
        functools.partial(lookup_kernel, plan, F, gene_n),
        grid=(n // block,),
        in_specs=[smem(), lanes(block)] + [whole(*t.shape) for t in tables],
        out_specs=rows(block, width),
        out_shape=jax.ShapeDtypeStruct((n, width), bf16),
        compiler_params=params(),
        cost_estimate=cost(2.1 + n * used * 6.5e-7),
        name="lookup",
    )(coord, ids, *tables)


def count_kernel(size, coord_ref, ids_ref, out_ref):
    high_n = out_ref.shape[0]
    lines = -(-high_n // 16) * 16
    total = None
    for i in range(size):
        ids = ids_ref[i : i + 1, :]
        left = onehot(lax.shift_right_logical(ids, 7), coord_ref[0] * high_n, lines)
        right = onehot(lax.bitwise_and(ids, 127), 0, 128)
        term = dg(left, right, 1, 1)
        total = term if total is None else total + term
    add_to(out_ref, total[0:high_n, :].astype(i32))


def count_rows(coord, ids, own, size=8):
    cells, n = ids.shape
    return pl.pallas_call(
        functools.partial(count_kernel, size),
        grid=(cells // size,),
        in_specs=[smem(), rows(size, n)],
        out_specs=whole(own // 128, 128),
        out_shape=jax.ShapeDtypeStruct((own // 128, 128), i32),
        compiler_params=params(),
        cost_estimate=cost(1.15e-4 * cells * n),
        name="count_rows",
    )(coord, ids)


def add_to(ref, value):
    @pl.when(pl.program_id(0) == 0)
    def _():
        ref[...] = value

    @pl.when(pl.program_id(0) != 0)
    def _():
        ref[...] += value


def prepare_kernel(
    coord_ref, ids_ref, gene, pos, qkv, up, out, down, expr, study, *refs
):
    vectors, piece_ref, small_ref = refs[:9], refs[9], refs[10]
    p = coord_ref[1]
    width = gene.shape[1]
    sub = vectors[0].shape[1]
    per = width // sub
    lines = [
        jnp.concatenate([vectors[per * r + i][...] for i in range(per)], axis=1)
        for r in range(8 // per)
    ]
    last = vectors[8][...]
    lines.append(jnp.concatenate([last, jnp.zeros((1, width - last.shape[1]), bf16)], axis=1))
    small_ref[...] = jnp.concatenate(
        lines + [jnp.zeros((MISC - len(lines), width), bf16)], axis=0
    )
    at = 0
    for ref in (gene, pos):
        piece_ref[at : at + ref.shape[0], :] = ref[...]
        at += ref.shape[0]
    even = lax.bitwise_and(p, 1) == 0
    odd = [up[:, t * width : (t + 1) * width] for t in range(up.shape[1] // width)] + [out[...]]
    for t in range(qkv.shape[1] // width):
        piece_ref[at : at + qkv.shape[0], :] = jnp.where(
            even, qkv[:, t * width : (t + 1) * width], odd[t]
        )
        at += qkv.shape[0]
    piece_ref[at : at + down.shape[0], :] = down[...]
    at += down.shape[0]
    misc = jnp.where(p == 0, expr[...], jnp.where(p == 1, study[...], small_ref[...]))
    piece_ref[at : at + MISC, :] = jnp.where(p < 3, misc, jnp.zeros_like(misc))
    at += MISC
    n = ids_ref.shape[1]
    slot = lax.broadcasted_iota(i32, (1, n), 1)
    ids = jnp.where(slot < coord_ref[2], ids_ref[...], 255 * 128)
    for part in (lax.shift_right_logical(ids, 7), lax.bitwise_and(ids, 127)):
        part = part.astype(f32)
        lines = [part[:, t * width : (t + 1) * width] for t in range(n // width)]
        piece_ref[at : at + n // width, :] = jnp.concatenate(lines, axis=0).astype(bf16)
        at += n // width


def prepare(coord, ids, gene, pos, qkv, up, out, down, expr, study, vectors):
    width = gene.shape[1]
    eighth = [(a.shape[0] // INNER, a.shape[1]) for a in (gene, pos, down)]
    fourth = [(a.shape[0] // (INNER // 2), a.shape[1]) for a in (qkv, up, out)]
    mine = [pl.BlockSpec(s, lambda i, c: (c[1], 0)) for s in eighth]
    pair = [pl.BlockSpec(s, lambda i, c: (lax.shift_right_logical(c[1], 1), 0)) for s in fourth]
    total = sum(s[0] for s in eighth) + fourth[0][0] * fourth[0][1] // width + MISC
    total += 2 * ids.shape[1] // width
    return pl.pallas_call(
        prepare_kernel,
        grid_spec=pltpu.PrefetchScalarGridSpec(
            num_scalar_prefetch=1,
            grid=(1,),
            in_specs=[whole(*ids.shape)] + mine[0:2] + pair + mine[2:]
            + [whole(*a.shape) for a in (expr, study, *vectors)],
            out_specs=[whole(total, width), whole(MISC, width)],
        ),
        out_shape=[
            jax.ShapeDtypeStruct((total, width), bf16),
            jax.ShapeDtypeStruct((MISC, width), bf16),
        ],
        compiler_params=params(),
        cost_estimate=cost(2.5),
        name="prepare",
    )(coord, ids, gene, pos, qkv, up, out, down, expr, study, *vectors)


def assemble(F, n, coord_ref, local, pieces, outs, misc):
    pos_loc, qkv_loc, up_loc, out_loc, down_loc, *misc_loc = local
    pos, cat, down, expr, study, vec, up_vec, ids = outs
    z, p = coord_ref[0], coord_ref[1]
    width = pos.shape[1]
    pos_n, cat_n = pos_loc.shape[0] // INNER, qkv_loc.shape[0] // (INNER // 2)
    down_n = down_loc.shape[0] // INNER
    half = cat.shape[2]
    parts = half // width
    rows_z = cat_n * (INNER // 2)
    lines = n // width
    rest_n = pos_n + cat_n * parts + down_n + MISC + 2 * lines

    def genes(row, ref, at):
        high, low = ref[at : at + lines, :], ref[at + lines : at + 2 * lines, :]
        number = (high.astype(f32) * 128.0 + low.astype(f32)).astype(i32)
        for t in range(lines):
            ids[row : row + 1, t * width : (t + 1) * width] = number[t : t + 1, :]

    pos[pl.ds(aligned(z * pos_n * INNER, 16), pos_n * INNER), :] = pos_loc[...]
    down[pl.ds(aligned(z * down_n * INNER, 16), down_n * INNER), :] = down_loc[...]
    span = pl.ds(aligned(z * rows_z, 16), rows_z)
    cat[0, span, :] = qkv_loc[...]
    cat[1, span, 0 : half - width] = up_loc[...]
    cat[1, span, half - width :] = out_loc[...]
    for t in range(3):
        misc[z * INNER + t] = misc_loc[t][...]
    for j in range(INNER):
        pj = lax.bitwise_xor(p, j)
        ref = pieces[j]
        for k in range(1, F):
            zk = lax.rem(z + F - k, F)
            at = rest_n * (k - 1)
            pos[pl.ds(aligned((zk * INNER + pj) * pos_n, 16), pos_n), :] = ref[at : at + pos_n, :]
            at += pos_n
            row = aligned(zk * rows_z + lax.shift_right_logical(pj, 1) * cat_n, 16)
            side = lax.bitwise_and(pj, 1)
            for s in range(parts):
                cat[side, pl.ds(row, cat_n), s * width : (s + 1) * width] = ref[at : at + cat_n, :]
                at += cat_n
            down[pl.ds(aligned((zk * INNER + pj) * down_n, 16), down_n), :] = ref[at : at + down_n, :]
            at += down_n
            misc[zk * INNER + pj] = ref[at : at + MISC, :]
            genes(k * INNER + j, ref, at + MISC)
        genes(j, ref, rest_n * (F - 1))
    sub = width // F
    for zz in range(F):
        expr[MISC * zz : MISC * zz + MISC, :] = misc[zz * INNER]
        study[MISC * zz : MISC * zz + MISC, :] = misc[zz * INNER + 1]
    small = [misc[zz * INNER + 2].astype(f32) for zz in range(F)]
    for i in range(8):
        r, c = i // F, sub * (i % F)
        vec[i : i + 1, :] = jnp.concatenate([s[r : r + 1, c : c + sub] for s in small], axis=1)
    r = 8 // F
    up_vec[...] = jnp.concatenate(
        [s[r : r + 1, 0 : up_vec.shape[1] // F] for s in small], axis=1
    )


def standard(values):
    average = jnp.mean(values, axis=1, keepdims=True)
    centered = values - average
    scale = lax.rsqrt(jnp.mean(centered * centered, axis=1, keepdims=True) + epsilon)
    return centered * scale, scale


def slot_mask(len_ref, size):
    slot = pl.program_id(0) * size + lax.broadcasted_iota(i32, (size, 1), 0)
    return (slot < len_ref[2]).astype(f32)


def find_rows(plan, F, gene_n, coord_ref, ids, tables):
    total = None
    for table, parts in zip(tables, plan):
        hits = [
            onehot(ids, source(coord_ref, k, j, F) * gene_n + off, count)
            if j is not None
            else onehot(ids, coord_ref[0] * gene_n * INNER, count)
            for k, j, off, count in parts
        ]
        hits = hits[0] if len(hits) == 1 else jnp.concatenate(hits, axis=0)
        term = dg(hits, table[table.shape[0] - hits.shape[0] :, :], 0, 0)
        total = term if total is None else total + term
    return total


def embed_kernel(F, n, gene_n, plan, use, sizes, coord_ref, ids_ref, bins_ref, prior, *refs):
    size, found_n, local_n, piece_n = sizes
    found, refs = refs[:found_n], refs[found_n:]
    local, refs = refs[:local_n], refs[local_n:]
    pieces, refs = refs[:piece_n], refs[piece_n:]
    inputs_ref, q_ref, k_ref, v_ref = refs[0:4]
    pos, cat, down, expr, study, vec, up_vec, ids_all, misc = refs[4:]
    width = prior.shape[1]

    @pl.when(pl.program_id(0) == 0)
    def _():
        assemble(F, n, coord_ref, local, [pieces[t] for t in use], refs[4:-1], misc)

    total = find_rows(plan, F, gene_n, coord_ref, ids_ref[...], pieces[piece_n - len(plan) :])
    total = total + dg(onehot(bins_ref[...], 0, expr.shape[0]), expr[...], 0, 0)
    for ref in found:
        total = total + ref[...].astype(f32)
    here = (lax.broadcasted_iota(i32, (8, study.shape[0]), 1) == coord_ref[3]).astype(bf16)
    total = total + dg(here, study[...], 1, 0)[0:1, :]
    slots = pl.ds(aligned(pl.program_id(0) * size, size), size)
    total = total + pos[slots, :].astype(f32) + prior[...].astype(f32)
    total = total * slot_mask(coord_ref, size)
    inputs_ref[...] = total
    normed, _ = standard(total)
    normed = (normed * vec[0:1, :] + vec[1:2, :]).astype(bf16)
    mixed = dg(normed, cat[0], 1, 0)
    q_ref[...] = (mixed[:, 0:width] + vec[2:3, :]).astype(bf16)
    k_ref[...] = mixed[:, width : 2 * width].astype(bf16)
    v_ref[...] = (mixed[:, 2 * width :] + vec[3:4, :]).astype(bf16)


def embed(coord, ids, bins, prior, found, local, pieces, use, plan, F, gene_n, rest, size=1024):
    n, width = prior.shape
    pos, qkv, up, out, down, *_ = local
    block = rows(size, width)
    outs = [
        ((F * pos.shape[0], width), bf16),
        ((2, F * qkv.shape[0], qkv.shape[1]), bf16),
        ((F * down.shape[0], width), bf16),
        ((F * MISC, width), bf16),
        ((F * MISC, width), bf16),
        ((8, width), f32),
        ((1, up.shape[1]), f32),
        ((F * INNER, n), i32),
    ]
    short = len(pieces) - len(plan)
    kernel = functools.partial(
        embed_kernel, F, n, gene_n, plan, use, (size, len(found), len(local), len(pieces))
    )
    return pl.pallas_call(
        kernel,
        grid=(n // size,),
        in_specs=[smem(), lanes(size), lanes(size)]
        + [block] * (1 + len(found))
        + [whole(*a.shape) for a in local]
        + [whole(rest, width)] * short
        + [whole(*a.shape) for a in pieces[short:]],
        out_specs=[block] * 4 + [whole(*s) for s, _ in outs],
        out_shape=[jax.ShapeDtypeStruct((n, width), f32)]
        + [jax.ShapeDtypeStruct((n, width), bf16)] * 3
        + [jax.ShapeDtypeStruct(*s) for s in outs],
        scratch_shapes=[pltpu.VMEM((F * INNER, MISC, width), bf16)],
        compiler_params=params(),
        cost_estimate=cost(15.5),
        name="embed",
    )(coord, ids, bins, prior, *found, *local, *pieces)


def extend(pair, half, spare):
    size = pair.shape[1] // 2
    lane = lax.broadcasted_iota(i32, pair.shape, 1)
    base = size * (1 - half)
    out = jnp.where((lane >= size * half) & (lane < size * half + size), pair, jnp.zeros_like(pair))
    for t, value in enumerate(spare):
        out = jnp.where(lane == base + t, jnp.broadcast_to(value, pair.shape), out)
    return out


def one():
    return jnp.ones((1, 1), bf16)


def split3(value):
    high = value.astype(bf16)
    rest = value - high.astype(f32)
    middle = rest.astype(bf16)
    return high, middle, (rest - middle.astype(f32)).astype(bf16)


def attend_kernel(len_ref, q_ref, k_ref, v_ref, o_ref, wide_ref, inv_ref, e_ref, kx, vx):
    n, pair = k_ref.shape
    size = pair // 2
    factor = size ** (-0.5) * LOG2E

    @pl.when(pl.program_id(1) == 0)
    def _():
        slot = lax.broadcasted_iota(i32, (n, 1), 0)
        bias = jnp.where(slot < len_ref[0], 0.0, -1e9).astype(bf16)
        lane = lax.broadcasted_iota(i32, (n, pair), 1)
        for h in range(2):
            kx[h] = extend(k_ref[...], h, [bias])
            own = (lane >= size * h) & (lane < size * h + size)
            vx[h] = jnp.where(own, v_ref[...], jnp.ones_like(v_ref[...]))

    scores = [dg(extend(q_ref[...], h, [one()]), kx[h], 1, 1) for h in range(2)]
    peaks = [jnp.max(s, axis=1, keepdims=True) for s in scores]
    raised = [jnp.exp2((s - p) * factor).astype(bf16) for s, p in zip(scores, peaks)]
    outs, totals = [], []
    for h in range(2):
        e_ref[h] = raised[h]
        out = dg(raised[h], vx[h], 1, 0)
        outs.append(out)
        totals.append(jnp.concatenate([out[:, size:], out[:, :size]], axis=1))
    low = lax.broadcasted_iota(i32, outs[0].shape, 1) < size
    inverse = 1.0 / jnp.where(low, totals[0], totals[1])
    out = jnp.where(low, outs[0], outs[1]) * inverse
    inv_ref[...] = inverse
    wide_ref[...] = out
    o_ref[...] = out.astype(bf16)


def attend(length, q, k, v, size=512):
    n, width = q.shape
    two = 2 * width // HEADS
    block = pl.BlockSpec((size, two), lambda j, i: (i, j))
    full = pl.BlockSpec((n, two), lambda j, i: (0, j))
    return pl.pallas_call(
        attend_kernel,
        grid=(HEADS // 2, n // size),
        in_specs=[smem(), block, full, full],
        out_specs=[block] * 3 + [pl.BlockSpec((2, size, n), lambda j, i: (j, i, 0))],
        out_shape=[
            jax.ShapeDtypeStruct((n, width), bf16),
            jax.ShapeDtypeStruct((n, width), f32),
            jax.ShapeDtypeStruct((n, width), f32),
            jax.ShapeDtypeStruct((HEADS, n, n), bf16),
        ],
        scratch_shapes=[pltpu.VMEM((2, n, two), bf16)] * 2,
        compiler_params=params(),
        cost_estimate=cost(32),
        name="attend",
    )(length, q, k, v)


def attend_back_kernel(
    q_ref, k_ref, v_ref, o_ref, do_ref, inv_ref, e_ref, dq_ref, dk_ref, dv_ref, vx, dkt, dvt
):
    n, pair = k_ref.shape
    size = pair // 2
    scale = size ** (-0.5)

    @pl.when(pl.program_id(1) == 0)
    def _():
        for h in range(2):
            vx[h] = extend(v_ref[...], h, [one(), one(), one()])
        dkt[...] = jnp.zeros_like(dkt)
        dvt[...] = jnp.zeros_like(dvt)

    grad = (do_ref[...].astype(f32) * inv_ref[...]).astype(bf16)
    product = grad.astype(f32) * o_ref[...]
    qt = q_ref[...].T
    gt = grad.T
    grads = []
    for h in range(2):
        span = slice(size * h, size * h + size)
        inner = jnp.sum(product[:, span], axis=1, keepdims=True)
        raised = e_ref[h]
        back = dg(extend(grad, h, [*split3(-inner)]), vx[h], 1, 1)
        grad_scores = (raised.astype(f32) * back).astype(bf16)
        dvt[span, :] += dg(gt[span, :], raised, 1, 0)
        dkt[span, :] += dg(qt[span, :], grad_scores, 1, 0)
        grads.append(dg(grad_scores, k_ref[...], 1, 0))
    low = lax.broadcasted_iota(i32, grads[0].shape, 1) < size
    dq_ref[...] = (jnp.where(low, grads[0], grads[1]) * scale).astype(bf16)

    @pl.when(pl.program_id(1) == pl.num_programs(1) - 1)
    def _():
        dk_ref[...] = (dkt[...] * scale).T.astype(bf16)
        dv_ref[...] = dvt[...].T.astype(bf16)


def attend_back(q, k, v, o, do, inverse, raised, size=256):
    n, width = q.shape
    two = 2 * width // HEADS
    block = pl.BlockSpec((size, two), lambda j, i: (i, j))
    full = pl.BlockSpec((n, two), lambda j, i: (0, j))
    return pl.pallas_call(
        attend_back_kernel,
        grid=(HEADS // 2, n // size),
        in_specs=[block, full, full, block, block, block]
        + [pl.BlockSpec((2, size, n), lambda j, i: (j, i, 0))],
        out_specs=[block, full, full],
        out_shape=[jax.ShapeDtypeStruct((n, width), bf16)] * 3,
        scratch_shapes=[pltpu.VMEM((2, n, two), bf16)] + [pltpu.VMEM((two, n), f32)] * 2,
        compiler_params=params(),
        cost_estimate=cost(40),
        name="attend_back",
    )(q, k, v, o, do, inverse, raised)


def feed_kernel(
    size, len_ref, att_ref, in_ref, cot_ref, cat, down, vec, up_vec,
    hidden_ref, mid_ref, datt_ref, wg_ref, g_vec, g_up_vec, g_down, g_up, g_out,
):
    width = att_ref.shape[1]
    up_width = down.shape[0]
    w_up, w_out = cat[1, :, 0:up_width], cat[1, :, up_width:]
    mask = slot_mask(len_ref, size)
    att = att_ref[...]
    middle = in_ref[...] + dg(att, w_out, 1, 0) + vec[4:5, :]
    normed, scale = standard(middle)
    low = (normed * vec[5:6, :] + vec[6:7, :]).astype(bf16)
    upward = dg(low, w_up, 1, 0) + up_vec[...]
    share = 0.5 * (1.0 + lax.erf(upward * (0.5**0.5)))
    active = (upward * share).astype(bf16)
    result = middle + dg(active, down[...], 1, 0) + vec[7:8, :]
    hidden_ref[...] = (result * mask).astype(bf16)
    grad_low = (cot_ref[...].astype(f32) * mask).astype(bf16)
    grad = grad_low.astype(f32)
    bell = jnp.exp(upward * upward * -0.5) * 0.3989422804014327
    grad_up = ((share + upward * bell) * dg(grad_low, down[...], 1, 1)).astype(bf16)
    grad_norm = dg(grad_up, w_up, 1, 1)
    scaled = grad_norm * vec[5:6, :]
    back = scaled - jnp.mean(scaled, axis=1, keepdims=True)
    back = back - normed * jnp.mean(scaled * normed, axis=1, keepdims=True)
    grad_mid = grad + scale * back
    branch = grad_mid.astype(bf16)
    mid_ref[...] = grad_mid
    datt_ref[...] = dg(branch, w_out, 1, 1).astype(bf16)
    add_to(g_down, dg(active, grad_low, 0, 0))
    add_to(g_up, dg(low, grad_up, 0, 0))
    add_to(g_out, dg(att, branch, 0, 0))
    sums = [
        jnp.sum(t, axis=0, keepdims=True)
        for t in (branch.astype(f32), grad_norm * normed, grad_norm, grad)
    ]
    add_to(g_vec, jnp.concatenate(sums + sums, axis=0))
    add_to(g_up_vec, jnp.sum(grad_up.astype(f32), axis=0, keepdims=True))

    @pl.when(pl.program_id(0) == pl.num_programs(0) - 1)
    def _():
        F = wg_ref.shape[3]
        line_n, down_n = width // F // INNER, up_width // F // INNER
        for z in range(F):
            for p in range(INNER):
                at = line_n * (INNER * z + p)
                blocks = [
                    g_up[at : at + line_n, t * width : (t + 1) * width]
                    for t in range(up_width // width)
                ]
                blocks.append(g_out[at : at + line_n, :])
                at = down_n * (INNER * z + p)
                blocks.append(g_down[at : at + down_n, :])
                at = 0
                for b in blocks:
                    wg_ref[p % 2, p // 2 % 2, p // 4, z, at : at + b.shape[0], :] = b.astype(bf16)
                    at += b.shape[0]


def feed(coord, att, inputs, cot, cat, down, vec, up_vec, F, size=1024):
    n, width = att.shape
    up_width = down.shape[0]
    block = rows(size, width)
    w_rows = (width * (up_width + width) // width + up_width) // F // INNER
    shapes = [(2, 2, 2, F, w_rows, width), (8, width), (1, up_width)]
    return pl.pallas_call(
        functools.partial(feed_kernel, size),
        grid=(n // size,),
        in_specs=[smem(), block, block, block]
        + [whole(*a.shape) for a in (cat, down, vec, up_vec)],
        out_specs=[block] * 3 + [whole(*s) for s in shapes],
        out_shape=[
            jax.ShapeDtypeStruct((n, width), bf16),
            jax.ShapeDtypeStruct((n, width), f32),
            jax.ShapeDtypeStruct((n, width), bf16),
        ]
        + [jax.ShapeDtypeStruct(shapes[0], bf16)]
        + [jax.ShapeDtypeStruct(s, f32) for s in shapes[1:]],
        scratch_shapes=[
            pltpu.VMEM((up_width, width), f32),
            pltpu.VMEM((width, up_width), f32),
            pltpu.VMEM((width, width), f32),
        ],
        compiler_params=params(),
        cost_estimate=cost(20),
        name="feed",
    )(coord, att, inputs, cot, cat, down, vec, up_vec)


def inputs_back_kernel(size, coord_ref, dq_ref, dk_ref, dv_ref, in_ref, mid_ref, cat, vec, out_ref, norm_ref):
    width = dq_ref.shape[1]
    normed, scale = standard(in_ref[...])
    grad_norm = None
    for t, part in enumerate((dq_ref, dk_ref, dv_ref)):
        term = dg(part[...], cat[0, :, t * width : (t + 1) * width], 1, 1)
        grad_norm = term if grad_norm is None else grad_norm + term
    scaled = grad_norm * vec[0:1, :]
    back = scaled - jnp.mean(scaled, axis=1, keepdims=True)
    back = back - normed * jnp.mean(scaled * normed, axis=1, keepdims=True)
    out_ref[...] = ((mid_ref[...] + scale * back) * slot_mask(coord_ref, size)).astype(bf16)
    norm_ref[...] = grad_norm


def inputs_back(coord, dq, dk, dv, inputs, mid, cat, vec, size=1024):
    n, width = dq.shape
    block = rows(size, width)
    return pl.pallas_call(
        functools.partial(inputs_back_kernel, size),
        grid=(n // size,),
        in_specs=[smem()] + [block] * 5
        + [pl.BlockSpec((1, *cat.shape[1:]), lambda i: (0, 0, 0)), whole(*vec.shape)],
        out_specs=[block] * 2,
        out_shape=[jax.ShapeDtypeStruct((n, width), t) for t in (bf16, f32)],
        compiler_params=params(),
        cost_estimate=cost(6.4),
        name="inputs_back",
    )(coord, dq, dk, dv, inputs, mid, cat, vec)


def weights_back_kernel(
    size, F, scalar_ref, bins_ref, dq_ref, dk_ref, dv_ref, in_ref, grad_ref, norm_ref, vec,
    g_vec2, g_up_vec, wg_ref, g_qkv, g_vec, g_expr,
):
    width = dq_ref.shape[1]
    normed, _ = standard(in_ref[...])
    low = (normed * vec[0:1, :] + vec[1:2, :]).astype(bf16)
    for t, part in enumerate((dq_ref, dk_ref, dv_ref)):
        add_to(g_qkv.at[:, t * width : (t + 1) * width], dg(low, part[...], 0, 0))
    grad_norm, grad = norm_ref[...], grad_ref[...]
    sums = [
        jnp.sum(t, axis=0, keepdims=True)
        for t in (
            grad_norm * normed,
            grad_norm,
            dq_ref[...].astype(f32),
            dv_ref[...].astype(f32),
            grad.astype(f32),
        )
    ]
    add_to(g_vec, jnp.concatenate(sums + sums[0:3], axis=0))
    add_to(g_expr, dg(onehot(bins_ref[...], 0, g_expr.shape[0]), grad, 1, 0))

    @pl.when(pl.program_id(0) == pl.num_programs(0) - 1)
    def _():
        line_n = width // F // INNER
        sub = width // F
        up_sub = g_up_vec.shape[1] // F
        groups = g_expr.shape[0]
        here = lax.broadcasted_iota(i32, (groups, width), 0) == scalar_ref[3]
        g_study = jnp.where(here, jnp.broadcast_to(g_vec[4:5, :], (groups, width)), 0.0)
        vectors = [g_vec[i : i + 1, :] for i in range(4)] + [g_vec2[i : i + 1, :] for i in range(4)]
        for z in range(F):
            small = []
            for r in range(8 // F):
                small.append(
                    jnp.concatenate(
                        [vectors[r * F + i][:, z * sub : (z + 1) * sub] for i in range(F)], axis=1
                    )
                )
            up_row = g_up_vec[:, z * up_sub : (z + 1) * up_sub]
            small.append(jnp.concatenate([up_row, jnp.zeros((1, width - up_sub), f32)], axis=1))
            small.append(jnp.zeros((8 - len(small), width), f32))
            at = MISC * z
            misc = [
                g_expr[at : at + 8, :],
                g_expr[at + 8 : at + 16, :],
                g_study[at : at + 8, :],
                g_study[at + 8 : at + 16, :],
                jnp.concatenate(small, axis=0),
            ]
            for p in range(INNER):
                at = line_n * (INNER * z + p)
                blocks = [
                    g_qkv[at : at + line_n, t * width : (t + 1) * width] for t in range(3)
                ] + [misc[p] if p < 5 else jnp.zeros((8, width), f32)]
                wg_ref[p % 2, p // 2 % 2, p // 4, z] = jnp.concatenate(blocks, axis=0).astype(bf16)


def weights_back(coord, bins, dq, dk, dv, inputs, grad, norm, vec, grads, half, bins_total, F, size=1024):
    n, width = dq.shape
    block = rows(size, width)
    shape = (2, 2, 2, F, half // F // INNER + 8, width)
    return pl.pallas_call(
        functools.partial(weights_back_kernel, size, F),
        grid=(n // size,),
        in_specs=[smem(), lanes(size)] + [block] * 6 + [whole(*a.shape) for a in (vec, *grads)],
        out_specs=whole(*shape),
        out_shape=jax.ShapeDtypeStruct(shape, bf16),
        scratch_shapes=[
            pltpu.VMEM((width, half), f32),
            pltpu.VMEM((8, width), f32),
            pltpu.VMEM((bins_total, width), f32),
        ],
        compiler_params=params(),
        cost_estimate=cost(9),
        name="weights_back",
    )(coord, bins, dq, dk, dv, inputs, grad, norm, vec, *grads)


def scatter_kernel(cells, F, gene_n, pos_n, start_at, group, extra, coord_ref, *refs):
    ids, refs = refs[0], refs[1:]
    grads, refs = refs[: len(cells)], refs[len(cells) :]
    lines, old, out_ref = refs[:extra], refs[extra:-1], refs[-1]
    for g in range(group):
        number = pl.program_id(0) * group + start_at + g
        z = lax.rem(coord_ref[0] + number, F)
        other = (number < F).astype(i32)
        place = z * INNER + lax.bitwise_xor(coord_ref[1], other)
        total = None
        for (cell, start, size), ref in zip(cells, grads):
            hits = onehot(ids[cell : cell + 1, start : start + size], place * gene_n, gene_n)
            term = dg(hits, ref[...], 1, 0)
            total = term if total is None else total + term
        line = None
        for (cell, start, size), ref in zip(cells, grads):
            inside = (place * pos_n >= start) & (place * pos_n < start + size)
            at = aligned(jnp.where(inside, place * pos_n - start, 0), 16)
            term = jnp.where(inside, ref[pl.ds(at, pos_n), :].astype(f32), 0.0)
            line = term if line is None else line + term
        for ref in old:
            total = total + ref[g, 0:gene_n, :]
            line = line + ref[g, gene_n : gene_n + pos_n, :]
        out_ref[g, 0:gene_n, :] = total.astype(out_ref.dtype)
        out_ref[g, gene_n : gene_n + pos_n, :] = line.astype(out_ref.dtype)
        for ref in lines:
            out_ref[g, gene_n + pos_n :, :] = ref[z]


def scatter(coord, cells, ids, grads, old, extra, F, gene_n, pos_n, start):
    width = grads[0].shape[1]
    size = gene_n + pos_n
    count = F if old else 2 * F
    group = GROUP_LAST if old else GROUP
    more = [] if extra is None else [extra]
    full = size + sum(e.shape[1] for e in more)
    first = start // group
    return pl.pallas_call(
        functools.partial(scatter_kernel, cells, F, gene_n, pos_n, start, group, len(more)),
        grid=(count // group,),
        in_specs=[smem(), whole(INNER, ids.shape[1])]
        + [whole(*g.shape) for g in grads]
        + [whole(*e.shape) for e in more]
        + [pl.BlockSpec((group, size, width), lambda i: (i + first, 0, 0))] * len(old),
        out_specs=pl.BlockSpec((group, full, width), lambda i: (i, 0, 0)),
        out_shape=jax.ShapeDtypeStruct((count, full, width), bf16 if old else f32),
        compiler_params=params(),
        cost_estimate=cost(2.5 + count * sum(c[2] for c in cells) * 2.5e-4),
        name="scatter",
    )(coord, ids, *grads, *more, *old)


def unpack_kernel(F, gene_n, pos_n, line_n, down_n, coord_ref, *refs):
    pieces, refs = refs[: INNER + 2], refs[INNER + 2 :]
    gene, pos, qkv, up, out, down, expr, study = refs[:8]
    vectors, misc = refs[8:17], refs[17]
    p = coord_ref[1]
    width = gene.shape[1]
    for j in range(INNER):
        pj = lax.bitwise_xor(p, j)
        if j < 6:
            here = [(pieces[j], 0)]
        else:
            top, bottom = pieces[6 + 2 * (j - 6)], pieces[7 + 2 * (j - 6)]
            here = [(top, 0), (bottom, top.shape[0])]
        for ref, first in here:
            count = min(ref.shape[0], gene_n - first)
            gene[pl.ds(aligned(gene_n * pj + first, 16), count), :] = ref[0:count, :].astype(f32)
        ref, first = here[-1]
        at = gene_n - first
        tail = ref[at : at + pos_n, :].astype(f32)
        pos[pl.ds(aligned(pos_n * pj, 16), pos_n), :] = tail
        at += pos_n
        tail = ref[at:, :].astype(f32)
        row = pl.ds(aligned(line_n * pj, 8), line_n)
        at = 0
        for s in range(up.shape[1] // width):
            up[row, s * width : (s + 1) * width] = tail[at : at + line_n, :]
            at += line_n
        out[row, :] = tail[at : at + line_n, :]
        at += line_n
        down[pl.ds(aligned(pj * down_n, 16), down_n), :] = tail[at : at + down_n, :]
        at += down_n
        for s in range(3):
            qkv[row, s * width : (s + 1) * width] = tail[at : at + line_n, :]
            at += line_n
        misc[pj] = tail[at : at + 8, :]
    for t in range(2):
        expr[8 * t : 8 * t + 8, :] = misc[t]
        study[8 * t : 8 * t + 8, :] = misc[2 + t]
    small = misc[4]
    sub = width // F
    for i in range(8):
        vectors[i][...] = small[i // F : i // F + 1, sub * (i % F) : sub * (i % F + 1)]
    vectors[8][...] = small[8 // F : 8 // F + 1, 0 : vectors[8].shape[1]]


def unpack(coord, pieces, F, gene_n, pos_n, line_n, down_n, up_width):
    width = pieces[0].shape[1]
    vmem = pl.BlockSpec(memory_space=pltpu.VMEM)
    shapes = [
        (gene_n * INNER, width),
        (pos_n * INNER, width),
        (line_n * INNER, 3 * width),
        (line_n * INNER, up_width),
        (line_n * INNER, width),
        (down_n * INNER, width),
        (MISC, width),
        (MISC, width),
    ]
    shapes += [(1, width // F)] * 8 + [(1, up_width // F)]
    return pl.pallas_call(
        functools.partial(unpack_kernel, F, gene_n, pos_n, line_n, down_n),
        in_specs=[smem()] + [vmem] * len(pieces),
        out_shape=[jax.ShapeDtypeStruct(s, f32) for s in shapes],
        scratch_shapes=[pltpu.VMEM((INNER, 8, width), f32)],
        compiler_params=params(),
        cost_estimate=cost(3.7),
        name="unpack",
    )(coord, *pieces)


def swap(array, bit):
    return lax.ppermute(array, "inner", [(i, i ^ bit) for i in range(INNER)])


def along(array, step, F):
    return lax.ppermute(array, "fsdp", [(i, (i + step) % F) for i in range(F)])


def share_along(array, F):
    if F != 4:
        return [along(array, k, F) for k in range(1, F)]
    z = lax.axis_index("fsdp")
    two = along(array, 2, F)
    up = lax.ppermute(array, "fsdp", [(0, 1), (1, 2), (2, 3)])
    down = lax.ppermute(array, "fsdp", [(1, 0), (2, 1), (3, 2)])
    far = lax.ppermute(two, "fsdp", [(2, 3), (1, 0)])
    return [jnp.where(z == 0, far, up), two, jnp.where(z == 3, far, down)]


def after(arrays, work):
    return lax.optimization_barrier((arrays, work))[0]


def spread(piece, use=None):
    if use is None:
        use = lambda step, arrays: ()
    cut = piece.shape[0] // 32 * 16
    near, other, core = swap(piece, 2), swap(piece, 4), swap(piece, 1)
    near, other = after((near, other), use(0, [piece, core]))
    upper, lower = swap(near[:cut], 4), swap(other[cut:], 2)
    near1, other1 = swap(near, 1), swap(other, 1)
    upper, lower = after((upper, lower), use(1, [core, near, other, near1, other1]))
    upper1, lower1 = swap(upper, 1), swap(lower, 1)
    return [piece, core, near, near1, other, other1, upper, lower, upper1, lower1]


def plus(left, right):
    return (left.astype(f32) + right.astype(f32)).astype(bf16)


def pick(array, index, axis):
    return lax.dynamic_index_in_dim(array, index, axis, keepdims=False)


def fold_core(array, p):
    mine = lax.bitwise_and(p, 1)
    return plus(pick(array, mine, 0), swap(pick(array, 1 - mine, 0), 1))


def fold_plane(array, p):
    x, y = (lax.bitwise_and(lax.shift_right_logical(p, b), 1) for b in (1, 2))
    terms = []
    for bits in range(4):
        dx, dy = bits & 1, bits >> 1
        term = pick(pick(array, lax.bitwise_xor(x, dx), 0), lax.bitwise_xor(y, dy), 0)
        terms.append(swap(term, 2 * bits) if bits else term)
    return terms


def sum_low(terms):
    total = terms[0].astype(f32)
    for term in terms[1:]:
        total = total + term.astype(f32)
    return total.astype(bf16)


def body(
    outer, F,
    gene_ids, expr_bins, study_ids, lengths, prior_embed, cotangent,
    gene_table, expr_table, study_table, position_table,
    norm1_gain, norm1_shift, w_qkv, bias_query, bias_value, w_output, bias_output,
    norm2_gain, norm2_shift, w_up_proj, bias_up, w_down_proj, bias_down,
):
    n = gene_ids.shape[1]
    z, p = lax.axis_index("fsdp"), lax.axis_index("inner")
    gene_n = gene_table.shape[0] // INNER
    pos_n = position_table.shape[0] // INNER
    down_n = w_down_proj.shape[0] // INNER
    line_n = w_qkv.shape[0] // INNER
    prior, cot = prior_embed[0], cotangent[0]
    coord = jnp.stack([z.astype(i32), p.astype(i32), lengths[0], study_ids[0]])

    vectors = [
        v.reshape(1, -1)
        for v in (norm1_gain, norm1_shift, bias_query, bias_value,
                  bias_output, norm2_gain, norm2_shift, bias_down, bias_up)
    ]
    piece, small = prepare(
        coord, gene_ids, gene_table, position_table, w_qkv, w_up_proj, w_output, w_down_proj,
        expr_table, study_table, vectors,
    )
    got = share_along(piece, F)
    gene_total = (F - 1) * gene_n

    def plan(j, first=0, count=gene_total):
        parts = []
        for k in range(F - 1):
            low, high = max(first, k * gene_n), min(first + count, (k + 1) * gene_n)
            if low < high:
                parts.append((k + 1, j, low - k * gene_n, high - low))
        return tuple(parts)

    def find(tables, plans):
        return lookup(coord, gene_ids, tables, tuple(plans), F, gene_n)

    found = [find([gene_table], [((0, None, 0, gene_table.shape[0]),)])]
    got = after(got, found[0])
    genes = piece[piece.shape[0] - 2 * n // gene_table.shape[1] :]
    stack = jnp.concatenate([g[gene_n:] for g in got] + [genes] + [g[:gene_n] for g in got])
    rest = stack.shape[0] - gene_total
    cut = stack.shape[0] // 32 * 16
    top, bottom = (0, cut - rest), (cut - rest, stack.shape[0] - cut)

    def look(step, arrays):
        if step == 0:
            found.append(find(arrays[:1], [plan(0)]))
        else:
            found.append(find(arrays[:3], [plan(1), plan(2), plan(4)]))
        return found[-1]

    pieces = spread(stack, look)
    inputs, query, keys, values, pos, cat, down, expr, study, vec, up_vec, ids = embed(
        coord, gene_ids, expr_bins, prior, found,
        [position_table, w_qkv, w_up_proj, w_output, w_down_proj, expr_table, study_table, small],
        [pieces[0], pieces[1], pieces[2], pieces[4], pieces[3], pieces[5], *pieces[6:]],
        (0, 1, 2, 4, 3, 5, 6, 8),
        (plan(3), plan(5), plan(6, *top), plan(6, *bottom), plan(7, *top), plan(7, *bottom)),
        F, gene_n, rest,
    )
    attended, wide, inverse, raised = attend(lengths, query, keys, values)
    hidden, mid, grad_attended, wg_feed, *grads = feed(
        coord, attended, inputs, cot, cat, down, vec, up_vec, F
    )
    wg_feed = fold_core(wg_feed, p)
    dqkv = attend_back(query, keys, values, wide, grad_attended, inverse, raised)
    wg_feed, dqkv = lax.optimization_barrier((wg_feed, dqkv))
    grad, norm = inputs_back(coord, *dqkv, inputs, mid, cat, vec)

    cut = n // 2

    def add_rows(cells, arrays, old=(), start=0, extra=None):
        return scatter(coord, tuple(cells), ids, arrays, old, extra, F, gene_n, pos_n, start)

    near, other = swap(grad, 2), swap(grad, 4)
    wg = weights_back(
        coord, expr_bins, *dqkv, inputs, grad, norm, vec, grads, w_qkv.shape[1], expr.shape[0], F
    )
    first = add_rows([(0, 0, n)], [grad])
    wg = fold_plane(jnp.concatenate([wg_feed, fold_core(wg, p)], axis=3), p)
    near, other, wg = after((near, other, wg), first)
    upper, lower = swap(near[:cut], 4), swap(other[cut:], 2)
    lines = sum_low(wg)
    second = add_rows([(2, 0, n), (4, 0, n)], [near, other])
    upper, lower = after((upper, lower), second)
    last = [(6, 0, cut), (6, cut, n - cut)]
    theirs = add_rows(last, [upper, lower], [first, second], 0)
    blocks = add_rows(last, [upper, lower], [first, second], F, lines)
    theirs = after(swap(theirs, 1), blocks)
    blocks = plus(blocks, jnp.pad(theirs, ((0, 0), (0, lines.shape[1]), (0, 0))))
    got = [along(blocks[k], k, F) for k in range(1, F)]
    own = count_rows(coord, after(ids, blocks), gene_table.shape[0])
    got = after(got, own)
    own = own.reshape(-1)
    if outer > 1:
        own = lax.psum(own, "outer")
    total = blocks[0].astype(f32)
    for g in got:
        total = total + g.astype(f32)
    if outer > 1:
        total = lax.psum(total, "outer")
    done = spread(total.astype(bf16))
    gene, pos, qkv, up, out, down, expr, study, *small = unpack(
        coord, done, F, gene_n, pos_n, line_n, down_n, w_up_proj.shape[1]
    )
    small = [s.reshape(-1) for s in small]
    return (
        hidden[None], gene, own, expr, study, pos, small[0], small[1], qkv, small[2], small[3],
        out, small[4], small[5], small[6], up, small[8], down, small[7],
    )


def solution(mesh):
    dp, F = mesh.devices.shape
    outer = dp // INNER
    mesh = Mesh(mesh.devices.reshape(outer, INNER, F), ("outer", "inner", "fsdp"))
    cells = ("outer", "inner", "fsdp")
    row, line = P("fsdp", None), P("fsdp")
    tables = (row,) * 4 + (line,) * 2 + (row, line, line, row, line, line, line, row, line, row, line)
    return jax.shard_map(
        functools.partial(body, outer, F),
        mesh=mesh,
        in_specs=(P(cells, None), P(cells, None), P(cells), P(cells), P(cells, None, None), P(cells, None, None))
        + tables,
        out_specs=(P(cells, None, None), row, line) + tables[1:],
        check_vma=False,
    )
```
